32 devices in a mesh: fsdp: 4 (over y, core), ctx: 2 (over x), tp: 4 (over z).
Axes of the slice: x: 2, y: 2, z: 4, core: 2. Of those that a mesh axis runs over, the one named last changes fastest.
Arguments:
- hidden_in: bfloat16 [4096, 2304], P(('fsdp', 'ctx')), may hold values from -36 to 36
- cotangent: bfloat16 [4096, 2304], P(('fsdp', 'ctx')), may hold values from -6 to 6
- segment_ids: int32 [4096], P('fsdp'), may hold values from -1 to 4, as said below
- pre_attention_gain: float32 [2304], replicated, may hold values from 0.25 to 1.75
- post_attention_gain: float32 [2304], replicated, may hold values from 0.25 to 1.75
- pre_feedforward_gain: float32 [2304], replicated, may hold values from 0.25 to 1.75
- post_feedforward_gain: float32 [2304], replicated, may hold values from 0.25 to 1.75
- query_weight: bfloat16 [2304, 2048], P(('fsdp', 'ctx'), 'tp'), may hold values from -0.3125 to 0.3125
- key_weight: bfloat16 [2304, 1024], P(('fsdp', 'ctx'), 'tp'), may hold values from -0.3125 to 0.3125
- value_weight: bfloat16 [2304, 1024], P(('fsdp', 'ctx'), 'tp'), may hold values from -0.125 to 0.125
- output_weight: bfloat16 [2304, 2048], P(('fsdp', 'ctx'), 'tp'), may hold values from -0.125 to 0.125
- gate_weight: bfloat16 [2304, 9216], P(('fsdp', 'ctx'), 'tp'), may hold values from -0.125 to 0.125
- up_weight: bfloat16 [2304, 9216], P(('fsdp', 'ctx'), 'tp'), may hold values from -0.125 to 0.125
- down_weight: bfloat16 [2304, 9216], P(('fsdp', 'ctx'), 'tp'), may hold values from -0.0625 to 0.0625
Outputs:
- hidden_out: bfloat16 [4096, 2304], P(('fsdp', 'ctx'))
- grad_hidden_in: bfloat16 [4096, 2304], P(('fsdp', 'ctx'))
- grad_pre_attention_gain: float32 [2304], P(('fsdp', 'ctx'))
- grad_post_attention_gain: float32 [2304], P(('fsdp', 'ctx'))
- grad_pre_feedforward_gain: float32 [2304], P(('fsdp', 'ctx'))
- grad_post_feedforward_gain: float32 [2304], P(('fsdp', 'ctx'))
- grad_query_weight: float32 [2304, 2048], P(('fsdp', 'ctx'), 'tp')
- grad_key_weight: float32 [2304, 1024], P(('fsdp', 'ctx'), 'tp')
- grad_value_weight: float32 [2304, 1024], P(('fsdp', 'ctx'), 'tp')
- grad_output_weight: float32 [2304, 2048], P(('fsdp', 'ctx'), 'tp')
- grad_gate_weight: float32 [2304, 9216], P(('fsdp', 'ctx'), 'tp')
- grad_up_weight: float32 [2304, 9216], P(('fsdp', 'ctx'), 'tp')
- grad_down_weight: float32 [2304, 9216], P(('fsdp', 'ctx'), 'tp')
The draws below stay inside these ranges and needn't reach their ends.
Inputs may be any that keep to these rules, and one draw needn't show every extreme that they name: `segment_ids`: within each group of 1024 tokens document ids increase in order, though some numbers (including 0) may be absent; each begins at a block's start, covers 1 to 4 blocks of 128 tokens with its padding (-1) only at the end of its last block, and never leaves its group; every group holds a document of 512 tokens and a block of padding only among its first 5 blocks.
All inputs are finite; a program needn't handle non-finite values.
Results may differ from the reference program's by a relative error of at most 0.022.
The reference program's roundings to bfloat16 on the way count: a program that leaves them out, or rounds other values in their place, can miss the bound.
Values may be sent and summed in bfloat16 or wider, within the bound.
No kernel may reach another device: no remote copies, remote signals or barrier semaphores. Data moves between devices by JAX's collectives and lax.ppermute only.
A program may use at most 256 MiB of HBM per device.

```python
import math
import jax
import jax.numpy as jnp
from jax import lax

D = 2304
FF = 9216
QH = 8
KVH = 4
HD = 256
BLOCK_TOKENS = 128
MAX_DOC_BLOCKS = 4
GROUP = 1024
TOKENS = 4096


def draw_hidden_in(key, part):
    key_rows, key_cols, key_base = jax.random.split(key, 3)
    row_scale = jnp.exp(jax.random.uniform(key_rows, (TOKENS, 1), jnp.float32, math.log(0.3), math.log(3.0)))
    col_scale = jnp.exp(jax.random.uniform(key_cols, (1, D), jnp.float32, math.log(0.5), math.log(2.0)))
    base = jnp.clip(jax.random.normal(key_base, (TOKENS, D), jnp.float32), -6.0, 6.0)
    return (base * row_scale * col_scale).astype(jnp.bfloat16)


def draw_segment_ids(key, part):
    group_list = TOKENS // GROUP
    block_list = GROUP // BLOCK_TOKENS
    key_count, key_fill, key_vacant, key_flip, key_group = jax.random.split(key, 5)
    count_values = jax.random.randint(key_count, (group_list, block_list), 1, MAX_DOC_BLOCKS + 1)
    fill_lengths = jax.random.randint(key_fill, (group_list, block_list), 1, BLOCK_TOKENS + 1)
    empty_blocks = jax.random.randint(key_vacant, (group_list, block_list), 0, 5) == 0
    reversed_rows = jax.random.randint(key_flip, (group_list, 1), 0, 2)
    chosen = jax.random.randint(key_group, (), 0, group_list)
    group_number = jnp.arange(group_list, dtype=jnp.int32)[:, None]
    number_value = jnp.arange(block_list, dtype=jnp.int32)[None, :]
    empty_blocks = empty_blocks & (number_value > 1) | (number_value == reversed_rows)
    longest_length = number_value == 1 - reversed_rows
    count_values = jnp.where(group_number == chosen, 1, count_values)
    count_values = jnp.where(longest_length, MAX_DOC_BLOCKS, jnp.where(empty_blocks, 1, count_values))
    fill_lengths = jnp.where(longest_length, BLOCK_TOKENS, jnp.where(empty_blocks, 0, fill_lengths))
    finish = jnp.cumsum(count_values, axis=1)
    starts = finish - count_values
    document = jnp.sum((starts[:, None, :] <= number_value[:, :, None]).astype(jnp.int32), axis=2) - 1
    last_end = jnp.take_along_axis(finish, document, axis=1)
    doc_fill = jnp.take_along_axis(fill_lengths, document, axis=1)
    block_fill = jnp.where(number_value == last_end - 1, doc_fill, BLOCK_TOKENS)
    offsets = jnp.arange(BLOCK_TOKENS, dtype=jnp.int32)[None, None, :]
    labels = jnp.where(offsets < block_fill[:, :, None], document[:, :, None], -1)
    return labels.reshape(TOKENS).astype(jnp.int32)


def spiked(values, stream_key, source, target, parts, factor):
    def block_of(axis_at):
        return (jnp.arange(values.shape[axis_at]) // (values.shape[axis_at] // parts)).reshape((-1,) + (1,) * (values.ndim - 1 - axis_at))

    near = jax.random.permutation(stream_key, parts)[block_of(target)]
    second = (block_of(target) + parts // 2) % parts
    return jnp.where((block_of(source) == near) | (block_of(source) == second), factor * values, values)


def block_scale(own_key, extent, cuts, smallest, top_value):
    factor_of, own = 1.0, jax.random.fold_in(own_key, 6)
    for dim, blocks in cuts:
        steps = jnp.exp(jax.random.uniform(jax.random.fold_in(own, dim), (blocks,), jnp.float32, smallest / len(cuts), top_value / len(cuts)))
        factor_of = factor_of * jnp.repeat(steps, extent[dim] // blocks).reshape([-1 if axis == dim else 1 for axis in range(len(extent))])
    return factor_of


def normal_values(own_key, dims, spread, limit, cuts=(), kind=jnp.bfloat16):
    factor_of = block_scale(own_key, dims, cuts, -0.22, 0.18) if cuts else 1.0
    entries = jax.random.normal(own_key, dims, jnp.float32) * spread * factor_of
    return jnp.minimum(jnp.maximum(entries, -limit), limit).astype(kind)


def noise_with(key, extent, deviation, reach, pieces, heavy, kind=jnp.bfloat16):
    array = deviation * jax.random.normal(key, extent, jnp.float32)
    if pieces:
        array = array * block_scale(key, extent, pieces, -0.22, 0.18)
    return jnp.clip(spiked(array, jax.random.fold_in(key, 3), *heavy), -reach, reach).astype(kind)


def setup_inputs(seed: int = 0) -> dict:
    arg_keys = jax.random.split(jax.random.key(seed), 15)
    return {
        "hidden_in": draw_hidden_in(jax.random.fold_in(arg_keys[14], 71), 0),
        "cotangent": noise_with(arg_keys[1], (TOKENS, D), 1.0, 6.0, ((0, 8),), (0, 1, 8, 2.0)),
        "segment_ids": draw_segment_ids(jax.random.fold_in(arg_keys[14], 71), 0),
        "pre_attention_gain": jnp.clip(1.0 + 0.15 * jax.random.normal(arg_keys[3], (D,), jnp.float32), 0.25, 1.75),
        "post_attention_gain": jnp.clip(1.0 + 0.15 * jax.random.normal(arg_keys[4], (D,), jnp.float32), 0.25, 1.75),
        "pre_feedforward_gain": jnp.clip(1.0 + 0.15 * jax.random.normal(arg_keys[5], (D,), jnp.float32), 0.25, 1.75),
        "post_feedforward_gain": jnp.clip(1.0 + 0.15 * jax.random.normal(arg_keys[6], (D,), jnp.float32), 0.25, 1.75),
        "query_weight": normal_values(arg_keys[7], (D, QH * HD), (D * 4 // 25) ** -0.5, 0.3125, ((0, 8), (1, 4))),
        "key_weight": normal_values(arg_keys[8], (D, KVH * HD), (D * 4 // 25) ** -0.5, 0.3125, ((0, 8), (1, 4))),
        "value_weight": normal_values(arg_keys[9], (D, KVH * HD), D ** -0.5, 0.125, ((0, 8), (1, 4))),
        "output_weight": normal_values(arg_keys[10], (D, QH * HD), (QH * HD) ** -0.5, 0.125, ((0, 8), (1, 4))),
        "gate_weight": normal_values(arg_keys[11], (D, FF), D ** -0.5, 0.125, ((0, 8), (1, 4))),
        "up_weight": normal_values(arg_keys[12], (D, FF), D ** -0.5, 0.125, ((0, 8), (1, 4))),
        "down_weight": normal_values(arg_keys[13], (D, FF), FF ** -0.5, 0.0625, ((0, 8), (1, 4))),
    }


CAP = 50.0
EPS = 1e-06
HIGH = lax.Precision.HIGHEST

@jax.custom_vjp
def low(v):
    return lax.optimization_barrier(v.astype(jnp.bfloat16)).astype(jnp.float32)

@jax.custom_vjp
def low_back(v):
    return v

def low_keep(v):
    return (low(v), None)

def low_pass(kept, grad):
    return (grad,)

def back_keep(v):
    return (v, None)

def back_low(kept, grad):
    return (low(grad),)
low.defvjp(low_keep, low_pass)
low_back.defvjp(back_keep, back_low)

def rms(value, gain):
    return value * lax.rsqrt(lax.optimization_barrier(jnp.mean(value * value, axis=-1, keepdims=True)) + EPS) * gain

def product(left, right):
    return jnp.dot(left, right, precision=HIGH)

def transposed_product(left, right):
    return lax.dot_general(left, right, (((1,), (1,)), ((), ())), precision=HIGH)

def attention(queries, keys, values, segments):
    count = queries.shape[0]
    heads_query = queries.reshape(count, KVH, QH // KVH, HD)
    heads_key = keys.reshape(count, KVH, HD)
    heads_value = values.reshape(count, KVH, HD)
    scores = low_back(jnp.einsum('qgrd,kgd->grqk', heads_query, heads_key, precision=HIGH) * HD ** (-0.5))
    capped = CAP * jnp.tanh(scores / CAP)
    places = jnp.arange(count, dtype=jnp.int32)
    allowed = (places[:, None] == places[None, :]) | (segments[:, None] == segments[None, :]) & (segments[:, None] >= 0) & (places[None, :] < places[:, None])
    powers = jnp.where(allowed, jnp.exp(capped), 0.0)
    probs = powers / lax.optimization_barrier(jnp.sum(powers, axis=-1, keepdims=True))
    attended = jnp.einsum('grqk,kgd->qgrd', low(probs), heads_value, precision=HIGH)
    return attended.reshape(count, QH * HD)

def layer(inputs, segments, gain_one, gain_two, gain_three, gain_four, query_matrix, key_matrix, value_matrix, output_matrix, gate_matrix, up_matrix, down_matrix):
    normed_one = low(rms(inputs, gain_one))
    queries = low(low_back(product(normed_one, query_matrix)))
    keys_all = low(low_back(product(normed_one, key_matrix)))
    values_all = low(low_back(product(normed_one, value_matrix)))
    attended = low(low_back(attention(queries, keys_all, values_all, segments)))
    branch_one = low_back(transposed_product(attended, output_matrix))
    middle = inputs + rms(branch_one, gain_two)
    normed_two = low(rms(middle, gain_three))
    gate_value = low_back(product(normed_two, gate_matrix))
    up_value = low_back(product(normed_two, up_matrix))
    hidden_units = low(jax.nn.gelu(gate_value, approximate=True) * up_value)
    branch_two = low_back(transposed_product(hidden_units, down_matrix))
    return middle + rms(branch_two, gain_four)

def reference(hidden_in, cotangent, segment_ids, pre_attention_gain, post_attention_gain, pre_feedforward_gain, post_feedforward_gain, query_weight, key_weight, value_weight, output_weight, gate_weight, up_weight, down_weight):
    params = (pre_attention_gain.astype(jnp.float32), post_attention_gain.astype(jnp.float32), pre_feedforward_gain.astype(jnp.float32), post_feedforward_gain.astype(jnp.float32), query_weight.astype(jnp.float32), key_weight.astype(jnp.float32), value_weight.astype(jnp.float32), output_weight.astype(jnp.float32), gate_weight.astype(jnp.float32), up_weight.astype(jnp.float32), down_weight.astype(jnp.float32))
    group_list = TOKENS // GROUP
    inputs = hidden_in.astype(jnp.float32).reshape(group_list, GROUP, D)
    upstream = cotangent.astype(jnp.float32).reshape(group_list, GROUP, D)
    segments = segment_ids.reshape(group_list, GROUP)

    def visit(running, record):
        piece_in, piece_up, piece_ids = record

        def forward(values_in, *weights):
            return layer(values_in, piece_ids, *weights)
        result, pullback = jax.vjp(jax.checkpoint(forward), piece_in, *params)
        gradients = pullback(piece_up)
        running = tuple((total + extra for total, extra in zip(running, gradients[1:])))
        return (running, (result.astype(jnp.bfloat16), gradients[0].astype(jnp.bfloat16)))
    initial = tuple((jnp.zeros(param.shape, jnp.float32) for param in params))
    totals, (outputs, grad_inputs) = lax.scan(visit, initial, (inputs, upstream, segments))
    return (outputs.reshape(TOKENS, D), grad_inputs.reshape(TOKENS, D), totals[0], totals[1], totals[2], totals[3], totals[4], totals[5], totals[6], totals[7], totals[8], totals[9], totals[10])
```

```python
import jax
import jax.numpy as jnp
from jax import lax
from jax.sharding import PartitionSpec as P

HD = 256
CAP = 50.0
EPS = 1e-06
ROWS = ("fsdp", "ctx")
LOW = jnp.bfloat16
F32 = jnp.float32


def passed_along(block, axis, distance):
    devices = range(lax.axis_size(axis))
    route = [(i - distance, i) for i in devices if i - distance in devices]
    return lax.ppermute(block, axis, route)


def shift(block, distance):
    size = lax.axis_size("tp")
    return lax.ppermute(block, "tp", [(i, (i + distance) % size) for i in range(size)])


def rms(value, gain):
    return value * lax.rsqrt(jnp.mean(value * value, axis=-1, keepdims=True) + EPS) * gain


def geglu(gate_value, up_value):
    return jax.nn.gelu(gate_value, approximate=True) * up_value


def product(left, right):
    return jnp.dot(left, right, preferred_element_type=F32)


def rows_product(left, right):
    return lax.dot_general(left, right, (((0,), (0,)), ((), ())), preferred_element_type=F32)


def transposed_product(left, right):
    return lax.dot_general(left, right, (((1,), (1,)), ((), ())), preferred_element_type=F32)


def distances(size):
    return sorted(range(1, size), key=lambda k: (abs(2 * k - size), k))


def scattered(partial):
    size = lax.axis_size("tp")
    rank = lax.axis_index("tp")
    blocks = partial.reshape(size, -1, partial.shape[-1])
    total = lax.dynamic_index_in_dim(blocks, rank, 0, False).astype(F32)
    for k in distances(size):
        block = lax.dynamic_index_in_dim(blocks, (rank + k) % size, 0, False)
        total = total + shift(block, k).astype(F32)
    return total


def gathered(block):
    size = lax.axis_size("tp")
    rank = lax.axis_index("tp")
    whole = jnp.zeros((size,) + block.shape, block.dtype)
    whole = lax.dynamic_update_index_in_dim(whole, block, rank, 0)
    for k in distances(size):
        whole = lax.dynamic_update_index_in_dim(whole, shift(block, k), (rank - k) % size, 0)
    return whole.reshape(-1, block.shape[-1])


def gathered_turned(block):
    size = lax.axis_size("tp")
    pieces = {k: shift(block, k) for k in distances(size)}
    return jnp.concatenate([block] + [pieces[k] for k in range(1, size)], axis=0)


def scattered_turned(partial):
    size = lax.axis_size("tp")
    blocks = partial.reshape(size, -1, partial.shape[-1])
    total = blocks[0].astype(F32)
    for k in distances(size):
        total = total + shift(blocks[k], -k).astype(F32)
    return total


def attention_scores(queries, keys_all, allowed, scaling):
    scores = (
        jnp.einsum("qgrd,kgd->grqk", queries, keys_all, preferred_element_type=F32) * scaling
    )
    capped = CAP * jnp.tanh(scores / CAP)
    powers = jnp.where(allowed[None, None], jnp.exp(capped), 0.0)
    return (scores, powers)


def gather_rows(weight):
    return lax.all_gather(weight, ROWS, axis=0, tiled=True)


def share_rows(grad):
    return lax.psum_scatter(grad.astype(LOW), ROWS, scatter_dimension=0, tiled=True)


def shards(
    hidden_in,
    cotangent,
    segment_ids,
    pre_attention_gain,
    post_attention_gain,
    pre_feedforward_gain,
    post_feedforward_gain,
    query_weight,
    key_weight,
    value_weight,
    output_weight,
    gate_weight,
    up_weight,
    down_weight,
):
    length = hidden_in.shape[0]
    heads_width = query_weight.shape[1]
    kv_width = key_weight.shape[1]
    kv_heads = kv_width // HD
    repeats = heads_width // kv_width
    units = gate_weight.shape[1]
    qkv_width = heads_width + 2 * kv_width
    scaling = HD ** (-0.5)
    tp_size = lax.axis_size("tp")
    tp_rank = lax.axis_index("tp")
    piece = length // tp_size

    attention_full = gather_rows(
        jnp.concatenate([query_weight, key_weight, value_weight, output_weight], axis=1)
    )
    gate_up_full = gather_rows(jnp.concatenate([gate_weight, up_weight], axis=1))
    down_full = gather_rows(down_weight)
    qkv_full = attention_full[:, :qkv_width]
    output_full = attention_full[:, qkv_width:]

    position = lax.axis_index("ctx")
    own_ids = lax.dynamic_slice_in_dim(segment_ids, position * length, length)
    prev_start = jnp.maximum(position - 1, 0) * length
    prev_ids = jnp.where(
        position > 0, lax.dynamic_slice_in_dim(segment_ids, prev_start, length), -2
    )
    key_ids = jnp.concatenate([prev_ids, own_ids])
    query_pos = jnp.arange(length, dtype=jnp.int32)
    key_pos = jnp.arange(2 * length, dtype=jnp.int32) - length
    allowed = (query_pos[:, None] == key_pos[None, :]) | (own_ids[:, None] == key_ids[None, :]) & (
        own_ids[:, None] >= 0
    ) & (key_pos[None, :] < query_pos[:, None])

    normed_one = rms(hidden_in.astype(F32), pre_attention_gain).astype(LOW)
    inputs = lax.dynamic_slice_in_dim(hidden_in, tp_rank * piece, piece).astype(F32)
    upstream = lax.dynamic_slice_in_dim(cotangent, tp_rank * piece, piece).astype(F32)

    qkv_low = product(normed_one, qkv_full).astype(LOW)
    queries = qkv_low[:, :heads_width].reshape(length, kv_heads, repeats, HD)
    kv_low = qkv_low[:, heads_width:]
    kv_all = jnp.concatenate([passed_along(kv_low, "ctx", 1), kv_low], axis=0)
    keys_all = kv_all[:, :kv_width].reshape(2 * length, kv_heads, HD)
    values_all = kv_all[:, kv_width:].reshape(2 * length, kv_heads, HD)
    scores, powers = attention_scores(queries, keys_all, allowed, scaling)
    totals = jnp.sum(powers, axis=-1, keepdims=True)
    probs_low = (powers / totals).astype(LOW)
    attended = jnp.einsum("grqk,kgd->qgrd", probs_low, values_all, preferred_element_type=F32)
    attended_low = attended.reshape(length, -1).astype(LOW)

    branch_one = scattered(transposed_product(attended_low, output_full).astype(LOW))
    middle = inputs + rms(branch_one, post_attention_gain)
    normed_two_own = rms(middle, pre_feedforward_gain).astype(LOW)
    normed_two = gathered_turned(normed_two_own)

    gate_up = product(normed_two, gate_up_full)
    gate_value = gate_up[:, :units]
    up_value = gate_up[:, units:]
    hidden_low = geglu(gate_value, up_value).astype(LOW)
    branch_two = scattered_turned(transposed_product(hidden_low, down_full).astype(LOW))
    result = middle + rms(branch_two, post_feedforward_gain)

    unused_four, pull_four = jax.vjp(rms, branch_two, post_feedforward_gain)
    grad_branch_two, grad_gain_four = pull_four(upstream)
    grad_two_low = gathered_turned(grad_branch_two.astype(LOW))

    grad_down_full = rows_product(grad_two_low, hidden_low)
    down_share = share_rows(grad_down_full)
    grad_hidden_units = product(grad_two_low, down_full)
    unused_glu, pull_glu = jax.vjp(geglu, gate_value, up_value)
    grad_gate, grad_up = pull_glu(grad_hidden_units)
    grad_gate_up = jnp.concatenate([grad_gate.astype(LOW), grad_up.astype(LOW)], axis=1)
    grad_normed_two = scattered_turned(transposed_product(grad_gate_up, gate_up_full).astype(LOW))
    gate_up_share = share_rows(rows_product(normed_two, grad_gate_up))

    unused_three, pull_three = jax.vjp(rms, middle, pre_feedforward_gain)
    grad_middle_norm, grad_gain_three = pull_three(grad_normed_two)
    grad_middle = upstream + grad_middle_norm
    unused_two, pull_two = jax.vjp(rms, branch_one, post_attention_gain)
    grad_branch_one, grad_gain_two = pull_two(grad_middle)
    grad_one_low = gathered(grad_branch_one.astype(LOW))

    grad_output_full = rows_product(grad_one_low, attended_low)
    grad_attended = (
        product(grad_one_low, output_full).astype(LOW).reshape(length, kv_heads, repeats, HD)
    )
    probs = powers / totals
    grad_probs = jnp.einsum(
        "qgrd,kgd->grqk", grad_attended, values_all, preferred_element_type=F32
    )
    inner = jnp.sum(probs * grad_probs, axis=-1, keepdims=True)
    grad_capped = probs * (grad_probs - inner)
    squashed = jnp.tanh(scores / CAP)
    grad_scores = (grad_capped * (1.0 - squashed * squashed)).astype(LOW)
    grad_query_low = (
        (
            jnp.einsum("grqk,kgd->qgrd", grad_scores, keys_all, preferred_element_type=F32)
            * scaling
        )
        .reshape(length, -1)
        .astype(LOW)
    )
    grad_keys_all = (
        jnp.einsum("grqk,qgrd->kgd", grad_scores, queries, preferred_element_type=F32) * scaling
    ).reshape(2 * length, -1)
    grad_values_all = jnp.einsum(
        "grqk,qgrd->kgd", probs_low, grad_attended, preferred_element_type=F32
    ).reshape(2 * length, -1)
    grad_kv_all = jnp.concatenate([grad_keys_all, grad_values_all], axis=1)
    grad_kv_back = passed_along(grad_kv_all[:length].astype(LOW), "ctx", -1).astype(F32)
    grad_kv_low = (grad_kv_all[length:] + grad_kv_back).astype(LOW)
    grad_qkv = jnp.concatenate([grad_query_low, grad_kv_low], axis=1)
    grad_normed_one = scattered(transposed_product(grad_qkv, qkv_full).astype(LOW))
    grad_qkv_full = rows_product(normed_one, grad_qkv)

    unused_one, pull_one = jax.vjp(rms, inputs, pre_attention_gain)
    grad_inputs_norm, grad_gain_one = pull_one(grad_normed_one)
    grad_inputs = gathered((grad_middle + grad_inputs_norm).astype(LOW))
    outputs = gathered(result.astype(LOW))

    gains = jnp.stack([grad_gain_one, grad_gain_two, grad_gain_three, grad_gain_four])
    gains_all = gains
    for k in range(1, tp_size):
        gains_all = gains_all + shift(gains, k)
    attention_share = share_rows(
        jnp.concatenate(
            [grad_qkv_full.astype(LOW), grad_output_full.astype(LOW), gains_all.T.astype(LOW)],
            axis=1,
        )
    ).astype(F32)

    edges = [0, heads_width, heads_width + kv_width, qkv_width, qkv_width + heads_width]
    attention_shares = [attention_share[:, a:b] for a, b in zip(edges[:-1], edges[1:])]
    gain_shares = [attention_share[:, edges[-1] + i] for i in range(4)]
    gate_up_share = gate_up_share.astype(F32)
    return (
        (outputs, grad_inputs)
        + tuple(gain_shares)
        + tuple(attention_shares)
        + (gate_up_share[:, :units], gate_up_share[:, units:], down_share.astype(F32))
    )


def solution(mesh):
    tokens = P(ROWS, None)
    weight = P(ROWS, "tp")
    return jax.shard_map(
        shards,
        mesh=mesh,
        in_specs=(tokens, tokens, P("fsdp")) + (P(),) * 4 + (weight,) * 7,
        out_specs=(tokens, tokens) + (P(ROWS),) * 4 + (weight,) * 7,
        check_vma=False,
    )
```

```python
import jax
import jax.numpy as jnp
from jax import lax
from jax.experimental.layout import Layout, with_layout_constraint
from jax.sharding import PartitionSpec as P


HD = 256
CAP = 50.0
EPS = 1e-06
ROWS = ("fsdp", "ctx")
LOW = jnp.bfloat16
F32 = jnp.float32


def passed_along(block, axis, distance):
    devices = range(lax.axis_size(axis))
    route = [(i - distance, i) for i in devices if i - distance in devices]
    return lax.ppermute(block, axis, route)


def shift(block, distance):
    size = lax.axis_size("tp")
    return lax.ppermute(block, "tp", [(i, (i + distance) % size) for i in range(size)])


def rms(value, gain):
    return value * lax.rsqrt(jnp.mean(value * value, axis=-1, keepdims=True) + EPS) * gain


def geglu(gate_value, up_value):
    return jax.nn.gelu(gate_value, approximate=True) * up_value


def product(left, right):
    return jnp.dot(left, right, preferred_element_type=F32)


def rows_product(left, right):
    return lax.dot_general(left, right, (((0,), (0,)), ((), ())), preferred_element_type=F32)


def transposed_product(left, right):
    return lax.dot_general(left, right, (((1,), (1,)), ((), ())), preferred_element_type=F32)


def distances(size):
    return sorted(range(1, size), key=lambda k: (abs(2 * k - size), k))


def scattered(partial):
    size = lax.axis_size("tp")
    rank = lax.axis_index("tp")
    blocks = partial.reshape(size, -1, partial.shape[-1])
    total = lax.dynamic_index_in_dim(blocks, rank, 0, False).astype(F32)
    for k in distances(size):
        block = lax.dynamic_index_in_dim(blocks, (rank + k) % size, 0, False)
        total = total + shift(block, k).astype(F32)
    return total


def gathered(block):
    size = lax.axis_size("tp")
    rank = lax.axis_index("tp")
    whole = jnp.zeros((size,) + block.shape, block.dtype)
    whole = lax.dynamic_update_index_in_dim(whole, block, rank, 0)
    for k in distances(size):
        whole = lax.dynamic_update_index_in_dim(whole, shift(block, k), (rank - k) % size, 0)
    return whole.reshape(-1, block.shape[-1])


def gathered_turned(block):
    size = lax.axis_size("tp")
    pieces = {k: shift(block, k) for k in distances(size)}
    return jnp.concatenate([block] + [pieces[k] for k in range(1, size)], axis=0)


def scattered_turned(partial):
    size = lax.axis_size("tp")
    blocks = partial.reshape(size, -1, partial.shape[-1])
    total = blocks[0].astype(F32)
    for k in distances(size):
        total = total + shift(blocks[k], -k).astype(F32)
    return total


def summed(value, axis):
    size = lax.axis_size(axis)
    bit = 1
    while bit < size:
        value = value + lax.ppermute(value, axis, [(i, i ^ bit) for i in range(size)])
        bit *= 2
    return value


def attention_scores(queries, keys_all, allowed, scaling):
    scores = (
        jnp.einsum("qgrd,kgd->grqk", queries, keys_all, preferred_element_type=F32) * scaling
    )
    capped = CAP * jnp.tanh(scores / CAP)
    powers = jnp.where(allowed[None, None], jnp.exp(capped), 0.0)
    return (scores, powers)


def by_rows(value):
    return with_layout_constraint(value, Layout(major_to_minor=(0, 1)))


def gather_rows(weight):
    return lax.all_gather(weight, ROWS, axis=0, tiled=True)


def share_rows(grad):
    return lax.psum_scatter(grad, ROWS, scatter_dimension=0, tiled=True)


def shards(
    hidden_in,
    cotangent,
    segment_ids,
    pre_attention_gain,
    post_attention_gain,
    pre_feedforward_gain,
    post_feedforward_gain,
    query_weight,
    key_weight,
    value_weight,
    output_weight,
    gate_weight,
    up_weight,
    down_weight,
):
    length = hidden_in.shape[0]
    heads_width = query_weight.shape[1]
    kv_width = key_weight.shape[1]
    kv_heads = kv_width // HD
    repeats = heads_width // kv_width
    units = gate_weight.shape[1]
    qkv_width = heads_width + 2 * kv_width
    scaling = HD ** (-0.5)
    tp_size = lax.axis_size("tp")
    tp_rank = lax.axis_index("tp")
    piece = length // tp_size

    attention_full = gather_rows(
        jnp.concatenate([query_weight, key_weight, value_weight, output_weight], axis=1)
    )
    gate_up_full = gather_rows(jnp.concatenate([gate_weight, up_weight], axis=1))
    down_full = gather_rows(down_weight)
    qkv_full = attention_full[:, :qkv_width]
    output_full = attention_full[:, qkv_width:]

    position = lax.axis_index("ctx")
    own_ids = lax.dynamic_slice_in_dim(segment_ids, position * length, length)
    prev_start = jnp.maximum(position - 1, 0) * length
    prev_ids = jnp.where(
        position > 0, lax.dynamic_slice_in_dim(segment_ids, prev_start, length), -2
    )
    key_ids = jnp.concatenate([prev_ids, own_ids])
    query_pos = jnp.arange(length, dtype=jnp.int32)
    key_pos = jnp.arange(2 * length, dtype=jnp.int32) - length
    allowed = (query_pos[:, None] == key_pos[None, :]) | (own_ids[:, None] == key_ids[None, :]) & (
        own_ids[:, None] >= 0
    ) & (key_pos[None, :] < query_pos[:, None])

    normed_one = rms(hidden_in.astype(F32), pre_attention_gain).astype(LOW)
    inputs = lax.dynamic_slice_in_dim(hidden_in, tp_rank * piece, piece).astype(F32)
    upstream = lax.dynamic_slice_in_dim(cotangent, tp_rank * piece, piece).astype(F32)

    qkv_low = product(normed_one, qkv_full).astype(LOW)
    queries = qkv_low[:, :heads_width].reshape(length, kv_heads, repeats, HD)
    kv_low = qkv_low[:, heads_width:]
    kv_all = jnp.concatenate([passed_along(kv_low, "ctx", 1), kv_low], axis=0)
    keys_all = kv_all[:, :kv_width].reshape(2 * length, kv_heads, HD)
    values_all = kv_all[:, kv_width:].reshape(2 * length, kv_heads, HD)
    scores, powers = attention_scores(queries, keys_all, allowed, scaling)
    totals = jnp.sum(powers, axis=-1, keepdims=True)
    probs_low = (powers / totals).astype(LOW)
    attended = jnp.einsum("grqk,kgd->qgrd", probs_low, values_all, preferred_element_type=F32)
    attended_low = attended.reshape(length, -1).astype(LOW)

    branch_one = scattered(transposed_product(attended_low, output_full).astype(LOW))
    middle = inputs + rms(branch_one, post_attention_gain)
    normed_two_own = rms(middle, pre_feedforward_gain).astype(LOW)
    normed_two = gathered_turned(normed_two_own)

    gate_up = product(normed_two, gate_up_full)
    gate_value = gate_up[:, :units]
    up_value = gate_up[:, units:]
    hidden_low = geglu(gate_value, up_value).astype(LOW)
    branch_two = scattered_turned(transposed_product(hidden_low, down_full).astype(LOW))
    result = middle + rms(branch_two, post_feedforward_gain)

    _, pull_four = jax.vjp(rms, branch_two, post_feedforward_gain)
    grad_branch_two, grad_gain_four = pull_four(upstream)
    grad_two_low = gathered_turned(grad_branch_two.astype(LOW))

    grad_down_low, grad_two_low = lax.optimization_barrier(
        (rows_product(grad_two_low, hidden_low).astype(LOW), grad_two_low)
    )
    down_share = share_rows(grad_down_low)
    grad_hidden_units = product(grad_two_low, down_full)
    _, pull_glu = jax.vjp(geglu, gate_value, up_value)
    grad_gate, grad_up = pull_glu(grad_hidden_units)
    grad_gate_up = jnp.concatenate([grad_gate.astype(LOW), grad_up.astype(LOW)], axis=1)
    grad_normed_two = scattered_turned(transposed_product(grad_gate_up, gate_up_full).astype(LOW))
    grad_gate_up_low = rows_product(normed_two, grad_gate_up).astype(LOW)

    _, pull_three = jax.vjp(rms, middle, pre_feedforward_gain)
    grad_middle_norm, grad_gain_three = pull_three(grad_normed_two)
    grad_middle = upstream + grad_middle_norm
    _, pull_two = jax.vjp(rms, branch_one, post_attention_gain)
    grad_branch_one, grad_gain_two = pull_two(grad_middle)
    grad_one_own, grad_gate_up_low = lax.optimization_barrier(
        (grad_branch_one.astype(LOW), grad_gate_up_low)
    )
    gate_up_share = share_rows(grad_gate_up_low)
    grad_one_low = gathered(grad_one_own)

    grad_output_full = rows_product(grad_one_low, attended_low)
    grad_attended = (
        product(grad_one_low, output_full).astype(LOW).reshape(length, kv_heads, repeats, HD)
    )
    probs = powers / totals
    grad_probs = jnp.einsum(
        "qgrd,kgd->grqk", grad_attended, values_all, preferred_element_type=F32
    )
    inner = jnp.sum(probs * grad_probs, axis=-1, keepdims=True)
    grad_capped = probs * (grad_probs - inner)
    squashed = jnp.tanh(scores / CAP)
    grad_scores = (grad_capped * (1.0 - squashed * squashed)).astype(LOW)
    grad_query_low = (
        (
            jnp.einsum("grqk,kgd->qgrd", grad_scores, keys_all, preferred_element_type=F32)
            * scaling
        )
        .reshape(length, -1)
        .astype(LOW)
    )
    grad_keys_all = (
        jnp.einsum("grqk,qgrd->kgd", grad_scores, queries, preferred_element_type=F32) * scaling
    ).reshape(2 * length, -1)
    grad_values_all = jnp.einsum(
        "grqk,qgrd->kgd", probs_low, grad_attended, preferred_element_type=F32
    ).reshape(2 * length, -1)
    grad_kv_all = jnp.concatenate([grad_keys_all, grad_values_all], axis=1)
    grad_kv_back = passed_along(grad_kv_all[:length].astype(LOW), "ctx", -1).astype(F32)
    grad_kv_low = (grad_kv_all[length:] + grad_kv_back).astype(LOW)
    grad_qkv = jnp.concatenate([grad_query_low, grad_kv_low], axis=1)
    grad_normed_one = scattered(transposed_product(grad_qkv, qkv_full).astype(LOW))
    grad_qkv_full = rows_product(normed_one, grad_qkv)

    _, pull_one = jax.vjp(rms, inputs, pre_attention_gain)
    grad_inputs_norm, grad_gain_one = pull_one(grad_normed_one)
    grad_inputs = gathered((grad_middle + grad_inputs_norm).astype(LOW))
    outputs = gathered(result.astype(LOW))

    gains = jnp.stack([grad_gain_one, grad_gain_two, grad_gain_three, grad_gain_four])
    for axis in ("tp",) + ROWS:
        gains = summed(gains, axis)
    share = attention_full.shape[0] // (lax.axis_size("fsdp") * lax.axis_size("ctx"))
    row_rank = lax.axis_index("fsdp") * lax.axis_size("ctx") + lax.axis_index("ctx")
    gain_shares = lax.dynamic_slice_in_dim(gains, row_rank * share, share, axis=1)
    attention_share = share_rows(
        by_rows(jnp.concatenate([grad_qkv_full.astype(LOW), grad_output_full.astype(LOW)], axis=1))
    ).astype(F32)

    edges = [0, heads_width, heads_width + kv_width, qkv_width, qkv_width + heads_width]
    attention_shares = [attention_share[:, a:b] for a, b in zip(edges[:-1], edges[1:])]
    gate_up_share = gate_up_share.astype(F32)
    return (
        (outputs, grad_inputs)
        + tuple(gain_shares[i] for i in range(4))
        + tuple(attention_shares)
        + (gate_up_share[:, :units], gate_up_share[:, units:], down_share.astype(F32))
    )


def solution(mesh):
    tokens = P(ROWS, None)
    weight = P(ROWS, "tp")
    return jax.shard_map(
        shards,
        mesh=mesh,
        in_specs=(tokens, tokens, P("fsdp")) + (P(),) * 4 + (weight,) * 7,
        out_specs=(tokens, tokens) + (P(ROWS),) * 4 + (weight,) * 7,
        check_vma=False,
    )
```

```python
import jax
import jax.numpy as jnp
from jax import lax
from jax.experimental.layout import Layout, with_layout_constraint
from jax.sharding import PartitionSpec as P


HD = 256
CAP = 50.0
EPS = 1e-06
ROWS = ("fsdp", "ctx")
LOW = jnp.bfloat16
F32 = jnp.float32


def passed_along(block, axis, distance):
    devices = range(lax.axis_size(axis))
    route = [(i - distance, i) for i in devices if i - distance in devices]
    return lax.ppermute(block, axis, route)


def rms(value, gain):
    return value * lax.rsqrt(jnp.mean(value * value, axis=-1, keepdims=True) + EPS) * gain


def geglu(gate_value, up_value):
    return jax.nn.gelu(gate_value, approximate=True) * up_value


def product(left, right):
    return jnp.dot(left, right, preferred_element_type=F32)


def rows_product(left, right):
    return lax.dot_general(left, right, (((0,), (0,)), ((), ())), preferred_element_type=F32)


def transposed_product(left, right):
    return lax.dot_general(left, right, (((1,), (1,)), ((), ())), preferred_element_type=F32)


def onward(block, distance, senders):
    return lax.ppermute(block, "tp", [(i, i + distance) for i in senders])


def scattered(blocks):
    size = lax.axis_size("tp")
    rising, falling = None, None
    for step in range(1, size):
        rise, fall = blocks[step], blocks[size - step]
        if rising is not None:
            rise = (rise.astype(F32) + rising.astype(F32)).astype(LOW)
            fall = (fall.astype(F32) + falling.astype(F32)).astype(LOW)
        rise, fall = lax.optimization_barrier((rise, fall))
        rising = onward(rise, 1, range(step))
        falling = onward(fall, -1, range(size - step, size))
    return blocks[0].astype(F32) + (rising.astype(F32) + falling.astype(F32))


def gathered(block):
    size = lax.axis_size("tp")
    rank = lax.axis_index("tp")
    rising, falling = [block], [block]
    for step in range(1, size):
        rise = onward(rising[-1], 1, range(step - 1, size - 1))
        fall = onward(falling[-1], -1, range(1, size - step + 1))
        rise, fall = lax.optimization_barrier((rise, fall))
        rising.append(rise)
        falling.append(fall)
    return [block] + [
        jnp.where(rank >= k, rising[k], falling[size - k]) for k in range(1, size)
    ]


def turned_blocks(partial):
    size = lax.axis_size("tp")
    blocks = partial.reshape(size, -1, partial.shape[-1])
    return [blocks[k] for k in range(size)]


def ordered_blocks(partial):
    size = lax.axis_size("tp")
    rank = lax.axis_index("tp")
    blocks = partial.reshape(size, -1, partial.shape[-1])
    return [
        lax.dynamic_index_in_dim(blocks, (rank - k) % size, 0, False) for k in range(size)
    ]


def in_order(pieces):
    size = lax.axis_size("tp")
    rank = lax.axis_index("tp")
    whole = jnp.zeros((size,) + pieces[0].shape, pieces[0].dtype)
    for k in range(size):
        whole = lax.dynamic_update_index_in_dim(whole, pieces[k], (rank - k) % size, 0)
    return whole.reshape(-1, pieces[0].shape[-1])


def summed(value, axis):
    size = lax.axis_size(axis)
    bit = 1
    while bit < size:
        value = value + lax.ppermute(value, axis, [(i, i ^ bit) for i in range(size)])
        bit *= 2
    return value


def attention_scores(queries, keys_all, allowed, scaling):
    scores = (
        jnp.einsum("qgrd,kgd->grqk", queries, keys_all, preferred_element_type=F32) * scaling
    )
    capped = CAP * jnp.tanh(scores / CAP)
    powers = jnp.where(allowed[None, None], jnp.exp(capped), 0.0)
    return (scores, powers)


def by_rows(value):
    return with_layout_constraint(value, Layout(major_to_minor=(0, 1)))


def gather_rows(weight):
    return lax.all_gather(weight, ROWS, axis=0, tiled=True)


def share_rows(grad):
    return lax.psum_scatter(grad, ROWS, scatter_dimension=0, tiled=True)


def shards(
    hidden_in,
    cotangent,
    segment_ids,
    pre_attention_gain,
    post_attention_gain,
    pre_feedforward_gain,
    post_feedforward_gain,
    query_weight,
    key_weight,
    value_weight,
    output_weight,
    gate_weight,
    up_weight,
    down_weight,
):
    length = hidden_in.shape[0]
    heads_width = query_weight.shape[1]
    kv_width = key_weight.shape[1]
    kv_heads = kv_width // HD
    repeats = heads_width // kv_width
    units = gate_weight.shape[1]
    qkv_width = heads_width + 2 * kv_width
    scaling = HD ** (-0.5)
    tp_size = lax.axis_size("tp")
    tp_rank = lax.axis_index("tp")
    piece = length // tp_size

    attention_full = gather_rows(
        jnp.concatenate([query_weight, key_weight, value_weight, output_weight], axis=1)
    )
    gate_up_full = gather_rows(jnp.concatenate([gate_weight, up_weight], axis=1))
    down_full = gather_rows(down_weight)
    qkv_full = attention_full[:, :qkv_width]
    output_full = attention_full[:, qkv_width:]

    position = lax.axis_index("ctx")
    own_ids = lax.dynamic_slice_in_dim(segment_ids, position * length, length)
    prev_start = jnp.maximum(position - 1, 0) * length
    prev_ids = jnp.where(
        position > 0, lax.dynamic_slice_in_dim(segment_ids, prev_start, length), -2
    )
    key_ids = jnp.concatenate([prev_ids, own_ids])
    query_pos = jnp.arange(length, dtype=jnp.int32)
    key_pos = jnp.arange(2 * length, dtype=jnp.int32) - length
    allowed = (query_pos[:, None] == key_pos[None, :]) | (own_ids[:, None] == key_ids[None, :]) & (
        own_ids[:, None] >= 0
    ) & (key_pos[None, :] < query_pos[:, None])

    normed_one = rms(hidden_in.astype(F32), pre_attention_gain).astype(LOW)
    inputs = lax.dynamic_slice_in_dim(hidden_in, tp_rank * piece, piece).astype(F32)
    upstream = lax.dynamic_slice_in_dim(cotangent, tp_rank * piece, piece).astype(F32)

    qkv_low = product(normed_one, qkv_full).astype(LOW)
    queries = qkv_low[:, :heads_width].reshape(length, kv_heads, repeats, HD)
    kv_low = qkv_low[:, heads_width:]
    kv_all = jnp.concatenate([passed_along(kv_low, "ctx", 1), kv_low], axis=0)
    keys_all = kv_all[:, :kv_width].reshape(2 * length, kv_heads, HD)
    values_all = kv_all[:, kv_width:].reshape(2 * length, kv_heads, HD)
    scores, powers = attention_scores(queries, keys_all, allowed, scaling)
    totals = jnp.sum(powers, axis=-1, keepdims=True)
    probs_low = (powers / totals).astype(LOW)
    attended = jnp.einsum("grqk,kgd->qgrd", probs_low, values_all, preferred_element_type=F32)
    attended_low = attended.reshape(length, -1).astype(LOW)

    branch_one = scattered(
        ordered_blocks(transposed_product(attended_low, output_full).astype(LOW))
    )
    middle = inputs + rms(branch_one, post_attention_gain)
    normed_two_own = rms(middle, pre_feedforward_gain).astype(LOW)
    normed_two = jnp.concatenate(gathered(normed_two_own), axis=0)

    gate_up = product(normed_two, gate_up_full)
    gate_value = gate_up[:, :units]
    up_value = gate_up[:, units:]
    hidden_low = geglu(gate_value, up_value).astype(LOW)
    branch_two = scattered(
        turned_blocks(transposed_product(hidden_low, down_full).astype(LOW))
    )
    result = middle + rms(branch_two, post_feedforward_gain)

    _, pull_four = jax.vjp(rms, branch_two, post_feedforward_gain)
    grad_branch_two, grad_gain_four = pull_four(upstream)
    grad_two_low = jnp.concatenate(gathered(grad_branch_two.astype(LOW)), axis=0)

    grad_down_low, grad_two_low = lax.optimization_barrier(
        (rows_product(grad_two_low, hidden_low).astype(LOW), grad_two_low)
    )
    down_share = share_rows(grad_down_low)
    _, pull_glu = jax.vjp(geglu, gate_value, up_value)
    grad_gate, grad_up = pull_glu(product(grad_two_low, down_full))
    grad_gate_up = jnp.concatenate([grad_gate.astype(LOW), grad_up.astype(LOW)], axis=1)
    grad_normed_two = scattered(
        turned_blocks(transposed_product(grad_gate_up, gate_up_full).astype(LOW))
    )
    grad_gate_up_low = rows_product(normed_two, grad_gate_up).astype(LOW)

    _, pull_three = jax.vjp(rms, middle, pre_feedforward_gain)
    grad_middle_norm, grad_gain_three = pull_three(grad_normed_two)
    grad_middle = upstream + grad_middle_norm
    _, pull_two = jax.vjp(rms, branch_one, post_attention_gain)
    grad_branch_one, grad_gain_two = pull_two(grad_middle)
    grad_one_own, grad_gate_up_low = lax.optimization_barrier(
        (grad_branch_one.astype(LOW), grad_gate_up_low)
    )
    gate_up_share = share_rows(grad_gate_up_low)
    grad_one_low = in_order(gathered(grad_one_own))
    result_low, grad_one_low = lax.optimization_barrier((result.astype(LOW), grad_one_low))
    outputs = in_order(gathered(result_low))

    grad_output_full = rows_product(grad_one_low, attended_low)
    grad_attended = (
        product(grad_one_low, output_full).astype(LOW).reshape(length, kv_heads, repeats, HD)
    )
    probs = powers / totals
    grad_probs = jnp.einsum(
        "qgrd,kgd->grqk", grad_attended, values_all, preferred_element_type=F32
    )
    inner = jnp.sum(probs * grad_probs, axis=-1, keepdims=True)
    grad_capped = probs * (grad_probs - inner)
    squashed = jnp.tanh(scores / CAP)
    grad_scores = (grad_capped * (1.0 - squashed * squashed)).astype(LOW)
    grad_query_low = (
        (
            jnp.einsum("grqk,kgd->qgrd", grad_scores, keys_all, preferred_element_type=F32)
            * scaling
        )
        .reshape(length, -1)
        .astype(LOW)
    )
    grad_keys_all = (
        jnp.einsum("grqk,qgrd->kgd", grad_scores, queries, preferred_element_type=F32) * scaling
    ).reshape(2 * length, -1)
    grad_values_all = jnp.einsum(
        "grqk,qgrd->kgd", probs_low, grad_attended, preferred_element_type=F32
    ).reshape(2 * length, -1)
    grad_kv_all = jnp.concatenate([grad_keys_all, grad_values_all], axis=1)
    grad_kv_back = passed_along(grad_kv_all[:length].astype(LOW), "ctx", -1).astype(F32)
    grad_kv_low = (grad_kv_all[length:] + grad_kv_back).astype(LOW)
    grad_qkv = jnp.concatenate([grad_query_low, grad_kv_low], axis=1)
    grad_normed_one = scattered(
        ordered_blocks(transposed_product(grad_qkv, qkv_full).astype(LOW))
    )
    grad_qkv_full = rows_product(normed_one, grad_qkv)

    _, pull_one = jax.vjp(rms, inputs, pre_attention_gain)
    grad_inputs_norm, grad_gain_one = pull_one(grad_normed_one)
    grad_inputs = in_order(gathered((grad_middle + grad_inputs_norm).astype(LOW)))

    gains = jnp.stack([grad_gain_one, grad_gain_two, grad_gain_three, grad_gain_four])
    for axis in ("tp",) + ROWS:
        gains = summed(gains, axis)
    share = attention_full.shape[0] // (lax.axis_size("fsdp") * lax.axis_size("ctx"))
    row_rank = lax.axis_index("fsdp") * lax.axis_size("ctx") + lax.axis_index("ctx")
    gain_shares = lax.dynamic_slice_in_dim(gains, row_rank * share, share, axis=1)
    attention_share = share_rows(
        by_rows(jnp.concatenate([grad_qkv_full.astype(LOW), grad_output_full.astype(LOW)], axis=1))
    ).astype(F32)

    edges = [0, heads_width, heads_width + kv_width, qkv_width, qkv_width + heads_width]
    attention_shares = [attention_share[:, a:b] for a, b in zip(edges[:-1], edges[1:])]
    gate_up_share = gate_up_share.astype(F32)
    return (
        (outputs, grad_inputs)
        + tuple(gain_shares[i] for i in range(4))
        + tuple(attention_shares)
        + (gate_up_share[:, :units], gate_up_share[:, units:], down_share.astype(F32))
    )


def solution(mesh):
    tokens = P(ROWS, None)
    weight = P(ROWS, "tp")
    return jax.shard_map(
        shards,
        mesh=mesh,
        in_specs=(tokens, tokens, P("fsdp")) + (P(),) * 4 + (weight,) * 7,
        out_specs=(tokens, tokens) + (P(ROWS),) * 4 + (weight,) * 7,
        check_vma=False,
    )
```

```python
import jax
import jax.numpy as jnp
from jax import lax
from jax.experimental.layout import Layout, with_layout_constraint
from jax.sharding import PartitionSpec as P


HD = 256
CAP = 50.0
EPS = 1e-06
ROWS = ("fsdp", "ctx")
LOW = jnp.bfloat16
F32 = jnp.float32


def passed_along(block, axis, distance):
    devices = range(lax.axis_size(axis))
    route = [(i - distance, i) for i in devices if i - distance in devices]
    return lax.ppermute(block, axis, route)


def rms(value, gain):
    return value * lax.rsqrt(jnp.mean(value * value, axis=-1, keepdims=True) + EPS) * gain


def geglu(gate_value, up_value):
    return jax.nn.gelu(gate_value, approximate=True) * up_value


def product(left, right):
    return jnp.dot(left, right, preferred_element_type=F32)


def rows_product(left, right):
    return lax.dot_general(left, right, (((0,), (0,)), ((), ())), preferred_element_type=F32)


def transposed_product(left, right):
    return lax.dot_general(left, right, (((1,), (1,)), ((), ())), preferred_element_type=F32)


def onward(block, distance, senders):
    return lax.ppermute(block, "tp", [(i, i + distance) for i in senders])


def scattered(blocks):
    size = lax.axis_size("tp")
    rising, falling = None, None
    for step in range(1, size):
        rise, fall = blocks[step], blocks[size - step]
        if rising is not None:
            rise = (rise.astype(F32) + rising.astype(F32)).astype(LOW)
            fall = (fall.astype(F32) + falling.astype(F32)).astype(LOW)
        rise, fall = lax.optimization_barrier((rise, fall))
        rising = onward(rise, 1, range(step))
        falling = onward(fall, -1, range(size - step, size))
    return blocks[0].astype(F32) + (rising.astype(F32) + falling.astype(F32))


def gathered(block):
    size = lax.axis_size("tp")
    rank = lax.axis_index("tp")
    rising, falling = [block], [block]
    for step in range(1, size):
        rise = onward(rising[-1], 1, range(step - 1, size - 1))
        fall = onward(falling[-1], -1, range(1, size - step + 1))
        rise, fall = lax.optimization_barrier((rise, fall))
        rising.append(rise)
        falling.append(fall)
    return [block] + [
        jnp.where(rank >= k, rising[k], falling[size - k]) for k in range(1, size)
    ]


def turned_blocks(partial):
    size = lax.axis_size("tp")
    blocks = partial.reshape(size, -1, partial.shape[-1])
    return [blocks[k] for k in range(size)]


def ordered_blocks(partial):
    size = lax.axis_size("tp")
    rank = lax.axis_index("tp")
    blocks = partial.reshape(size, -1, partial.shape[-1])
    return [
        lax.dynamic_index_in_dim(blocks, (rank - k) % size, 0, False) for k in range(size)
    ]


def in_order(pieces):
    size = lax.axis_size("tp")
    rank = lax.axis_index("tp")
    whole = jnp.zeros((size,) + pieces[0].shape, pieces[0].dtype)
    for k in range(size):
        whole = lax.dynamic_update_index_in_dim(whole, pieces[k], (rank - k) % size, 0)
    return whole.reshape(-1, pieces[0].shape[-1])


def summed(value, axis):
    size = lax.axis_size(axis)
    bit = 1
    while bit < size:
        value = value + lax.ppermute(value, axis, [(i, i ^ bit) for i in range(size)])
        bit *= 2
    return value


def attention_scores(queries, keys_all, allowed, scaling):
    scores = (
        jnp.einsum("qgrd,kgd->grqk", queries, keys_all, preferred_element_type=F32) * scaling
    )
    capped = CAP * jnp.tanh(scores / CAP)
    powers = jnp.where(allowed[None, None], jnp.exp(capped), 0.0)
    return (scores, powers)


def by_rows(value):
    return with_layout_constraint(value, Layout(major_to_minor=(0, 1)))


def gather_rows(weight):
    return lax.all_gather(weight, ROWS, axis=0, tiled=True)


def rows_of_core(left, core):
    pairs = lax.axis_size("fsdp") // 2
    split = left.reshape(left.shape[0], pairs, 2, -1)
    return lax.dynamic_index_in_dim(split, core, 2, False).reshape(left.shape[0], -1)


def sent_to_core(left, right):
    other = 1 - lax.axis_index("fsdp") % 2
    return rows_product(rows_of_core(left, other), right).astype(LOW)


def over_cores(block):
    return lax.ppermute(block, "fsdp", [(i, i ^ 1) for i in range(lax.axis_size("fsdp"))])


def chip_rows(left, right, arrived):
    own = rows_product(rows_of_core(left, lax.axis_index("fsdp") % 2), right)
    return (own + arrived.astype(F32)).astype(LOW)


def share_rows(grad):
    width = lax.axis_size("ctx")
    ranks = range(lax.axis_size("fsdp") * width)
    groups = [[r for r in ranks if r // width % 2 == core] for core in range(2)]
    return lax.psum_scatter(
        grad, ROWS, scatter_dimension=0, tiled=True, axis_index_groups=groups
    )


def shards(
    hidden_in,
    cotangent,
    segment_ids,
    pre_attention_gain,
    post_attention_gain,
    pre_feedforward_gain,
    post_feedforward_gain,
    query_weight,
    key_weight,
    value_weight,
    output_weight,
    gate_weight,
    up_weight,
    down_weight,
):
    length = hidden_in.shape[0]
    heads_width = query_weight.shape[1]
    kv_width = key_weight.shape[1]
    kv_heads = kv_width // HD
    repeats = heads_width // kv_width
    units = gate_weight.shape[1]
    qkv_width = heads_width + 2 * kv_width
    scaling = HD ** (-0.5)
    tp_size = lax.axis_size("tp")
    tp_rank = lax.axis_index("tp")
    piece = length // tp_size

    attention_full = gather_rows(
        jnp.concatenate([query_weight, key_weight, value_weight, output_weight], axis=1)
    )
    gate_up_full = gather_rows(jnp.concatenate([gate_weight, up_weight], axis=1))
    down_full = gather_rows(down_weight)
    qkv_full = attention_full[:, :qkv_width]
    output_full = attention_full[:, qkv_width:]

    position = lax.axis_index("ctx")
    own_ids = lax.dynamic_slice_in_dim(segment_ids, position * length, length)
    prev_start = jnp.maximum(position - 1, 0) * length
    prev_ids = jnp.where(
        position > 0, lax.dynamic_slice_in_dim(segment_ids, prev_start, length), -2
    )
    key_ids = jnp.concatenate([prev_ids, own_ids])
    query_pos = jnp.arange(length, dtype=jnp.int32)
    key_pos = jnp.arange(2 * length, dtype=jnp.int32) - length
    allowed = (query_pos[:, None] == key_pos[None, :]) | (own_ids[:, None] == key_ids[None, :]) & (
        own_ids[:, None] >= 0
    ) & (key_pos[None, :] < query_pos[:, None])

    normed_one = rms(hidden_in.astype(F32), pre_attention_gain).astype(LOW)
    inputs = lax.dynamic_slice_in_dim(hidden_in, tp_rank * piece, piece).astype(F32)
    upstream = lax.dynamic_slice_in_dim(cotangent, tp_rank * piece, piece).astype(F32)

    qkv_low = product(normed_one, qkv_full).astype(LOW)
    queries = qkv_low[:, :heads_width].reshape(length, kv_heads, repeats, HD)
    kv_low = qkv_low[:, heads_width:]
    kv_all = jnp.concatenate([passed_along(kv_low, "ctx", 1), kv_low], axis=0)
    keys_all = kv_all[:, :kv_width].reshape(2 * length, kv_heads, HD)
    values_all = kv_all[:, kv_width:].reshape(2 * length, kv_heads, HD)
    scores, powers = attention_scores(queries, keys_all, allowed, scaling)
    totals = jnp.sum(powers, axis=-1, keepdims=True)
    probs_low = (powers / totals).astype(LOW)
    attended = jnp.einsum("grqk,kgd->qgrd", probs_low, values_all, preferred_element_type=F32)
    attended_low = attended.reshape(length, -1).astype(LOW)

    branch_one = scattered(
        ordered_blocks(transposed_product(attended_low, output_full).astype(LOW))
    )
    middle = inputs + rms(branch_one, post_attention_gain)
    normed_two_own = rms(middle, pre_feedforward_gain).astype(LOW)
    normed_two = jnp.concatenate(gathered(normed_two_own), axis=0)

    gate_up = product(normed_two, gate_up_full)
    gate_value = gate_up[:, :units]
    up_value = gate_up[:, units:]
    hidden_low = geglu(gate_value, up_value).astype(LOW)
    branch_two = scattered(
        turned_blocks(transposed_product(hidden_low, down_full).astype(LOW))
    )
    result = middle + rms(branch_two, post_feedforward_gain)

    _, pull_four = jax.vjp(rms, branch_two, post_feedforward_gain)
    grad_branch_two, grad_gain_four = pull_four(upstream)
    grad_two_low = jnp.concatenate(gathered(grad_branch_two.astype(LOW)), axis=0)

    down_sent, grad_two_low = lax.optimization_barrier(
        (sent_to_core(grad_two_low, hidden_low), grad_two_low)
    )
    down_arrived = over_cores(down_sent)
    _, pull_glu = jax.vjp(geglu, gate_value, up_value)
    grad_gate, grad_up = pull_glu(product(grad_two_low, down_full))
    grad_gate_up = jnp.concatenate([grad_gate.astype(LOW), grad_up.astype(LOW)], axis=1)
    grad_down_low, grad_gate_up = lax.optimization_barrier(
        (chip_rows(grad_two_low, hidden_low, down_arrived), grad_gate_up)
    )
    down_share = share_rows(grad_down_low)
    grad_normed_two = transposed_product(grad_gate_up, gate_up_full).astype(LOW)
    grad_normed_two = scattered(turned_blocks(grad_normed_two))
    gate_up_arrived = over_cores(sent_to_core(normed_two, grad_gate_up))
    grad_gate_up_low = chip_rows(normed_two, grad_gate_up, gate_up_arrived)

    _, pull_three = jax.vjp(rms, middle, pre_feedforward_gain)
    grad_middle_norm, grad_gain_three = pull_three(grad_normed_two)
    grad_middle = upstream + grad_middle_norm
    _, pull_two = jax.vjp(rms, branch_one, post_attention_gain)
    grad_branch_one, grad_gain_two = pull_two(grad_middle)
    grad_one_own, grad_gate_up_low = lax.optimization_barrier(
        (grad_branch_one.astype(LOW), grad_gate_up_low)
    )
    gate_up_share = share_rows(grad_gate_up_low)
    grad_one_low = in_order(gathered(grad_one_own))
    result_low, grad_one_low = lax.optimization_barrier((result.astype(LOW), grad_one_low))
    outputs = in_order(gathered(result_low))

    output_arrived = over_cores(sent_to_core(grad_one_low, attended_low))
    output_share = share_rows(chip_rows(grad_one_low, attended_low, output_arrived))
    grad_attended = (
        product(grad_one_low, output_full).astype(LOW).reshape(length, kv_heads, repeats, HD)
    )
    probs = powers / totals
    grad_probs = jnp.einsum(
        "qgrd,kgd->grqk", grad_attended, values_all, preferred_element_type=F32
    )
    inner = jnp.sum(probs * grad_probs, axis=-1, keepdims=True)
    grad_capped = probs * (grad_probs - inner)
    squashed = jnp.tanh(scores / CAP)
    grad_scores = (grad_capped * (1.0 - squashed * squashed)).astype(LOW)
    grad_query_low = (
        (
            jnp.einsum("grqk,kgd->qgrd", grad_scores, keys_all, preferred_element_type=F32)
            * scaling
        )
        .reshape(length, -1)
        .astype(LOW)
    )
    grad_keys_all = (
        jnp.einsum("grqk,qgrd->kgd", grad_scores, queries, preferred_element_type=F32) * scaling
    ).reshape(2 * length, -1)
    grad_values_all = jnp.einsum(
        "grqk,qgrd->kgd", probs_low, grad_attended, preferred_element_type=F32
    ).reshape(2 * length, -1)
    grad_kv_all = jnp.concatenate([grad_keys_all, grad_values_all], axis=1)
    grad_kv_back = passed_along(grad_kv_all[:length].astype(LOW), "ctx", -1).astype(F32)
    grad_kv_low = (grad_kv_all[length:] + grad_kv_back).astype(LOW)
    grad_qkv = jnp.concatenate([grad_query_low, grad_kv_low], axis=1)
    grad_normed_one = scattered(
        ordered_blocks(transposed_product(grad_qkv, qkv_full).astype(LOW))
    )
    qkv_arrived = over_cores(sent_to_core(normed_one, grad_qkv))
    qkv_share = share_rows(by_rows(chip_rows(normed_one, grad_qkv, qkv_arrived))).astype(F32)

    _, pull_one = jax.vjp(rms, inputs, pre_attention_gain)
    grad_inputs_norm, grad_gain_one = pull_one(grad_normed_one)
    grad_inputs = in_order(gathered((grad_middle + grad_inputs_norm).astype(LOW)))

    gains = jnp.stack([grad_gain_one, grad_gain_two, grad_gain_three, grad_gain_four])
    for axis in ("tp",) + ROWS:
        gains = summed(gains, axis)
    share = attention_full.shape[0] // (lax.axis_size("fsdp") * lax.axis_size("ctx"))
    row_rank = lax.axis_index("fsdp") * lax.axis_size("ctx") + lax.axis_index("ctx")
    gain_shares = lax.dynamic_slice_in_dim(gains, row_rank * share, share, axis=1)
    edges = [0, heads_width, heads_width + kv_width, qkv_width]
    qkv_shares = [qkv_share[:, a:b] for a, b in zip(edges[:-1], edges[1:])]
    gate_up_share = gate_up_share.astype(F32)
    return (
        (outputs, grad_inputs)
        + tuple(gain_shares[i] for i in range(4))
        + tuple(qkv_shares)
        + (output_share.astype(F32), gate_up_share[:, :units], gate_up_share[:, units:], down_share.astype(F32))
    )


def solution(mesh):
    tokens = P(ROWS, None)
    weight = P(ROWS, "tp")
    return jax.shard_map(
        shards,
        mesh=mesh,
        in_specs=(tokens, tokens, P("fsdp")) + (P(),) * 4 + (weight,) * 7,
        out_specs=(tokens, tokens) + (P(ROWS),) * 4 + (weight,) * 7,
        check_vma=False,
    )
```

```python
import jax
import jax.numpy as jnp
from jax import lax
from jax.experimental.layout import Layout, with_layout_constraint
from jax.sharding import PartitionSpec as P


HD = 256
CAP = 50.0
EPS = 1e-06
ROWS = ("fsdp", "ctx")
LOW = jnp.bfloat16
F32 = jnp.float32


def passed_along(block, axis, distance):
    devices = range(lax.axis_size(axis))
    route = [(i - distance, i) for i in devices if i - distance in devices]
    return lax.ppermute(block, axis, route)


def rms(value, gain):
    return value * lax.rsqrt(jnp.mean(value * value, axis=-1, keepdims=True) + EPS) * gain


def geglu(gate_value, up_value):
    return jax.nn.gelu(gate_value, approximate=True) * up_value


def product(left, right):
    return jnp.dot(left, right, preferred_element_type=F32)


def rows_product(left, right):
    return lax.dot_general(left, right, (((0,), (0,)), ((), ())), preferred_element_type=F32)


def transposed_product(left, right):
    return lax.dot_general(left, right, (((1,), (1,)), ((), ())), preferred_element_type=F32)


def onward(block, distance, senders):
    return lax.ppermute(block, "tp", [(i, i + distance) for i in senders])


def shift(block, distance):
    size = lax.axis_size("tp")
    return lax.ppermute(block, "tp", [(i, (i + distance) % size) for i in range(size)])


def distances(size):
    return sorted(range(1, size), key=lambda k: (abs(2 * k - size), k))


def sent_scattered(blocks):
    blocks = lax.optimization_barrier(tuple(blocks))
    arrived = [shift(blocks[k], -k) for k in distances(len(blocks))]
    total = blocks[0].astype(F32)
    for block in arrived:
        total = total + block.astype(F32)
    return total


def sent_gathered(block):
    size = lax.axis_size("tp")
    pieces = {k: shift(block, k) for k in distances(size)}
    return [block] + [pieces[k] for k in range(1, size)]


def scattered(blocks):
    size = lax.axis_size("tp")
    rising, falling = None, None
    for step in range(1, size):
        rise, fall = blocks[step], blocks[size - step]
        if rising is not None:
            rise = (rise.astype(F32) + rising.astype(F32)).astype(LOW)
            fall = (fall.astype(F32) + falling.astype(F32)).astype(LOW)
        rise, fall = lax.optimization_barrier((rise, fall))
        rising = onward(rise, 1, range(step))
        falling = onward(fall, -1, range(size - step, size))
    return blocks[0].astype(F32) + (rising.astype(F32) + falling.astype(F32))


def gathered(block):
    size = lax.axis_size("tp")
    rank = lax.axis_index("tp")
    rising, falling = [block], [block]
    for step in range(1, size):
        rise = onward(rising[-1], 1, range(step - 1, size - 1))
        fall = onward(falling[-1], -1, range(1, size - step + 1))
        rise, fall = lax.optimization_barrier((rise, fall))
        rising.append(rise)
        falling.append(fall)
    return [block] + [
        jnp.where(rank >= k, rising[k], falling[size - k]) for k in range(1, size)
    ]


def turned_blocks(partial):
    size = lax.axis_size("tp")
    blocks = partial.reshape(size, -1, partial.shape[-1])
    return [blocks[k] for k in range(size)]


def ordered_blocks(partial):
    size = lax.axis_size("tp")
    rank = lax.axis_index("tp")
    blocks = partial.reshape(size, -1, partial.shape[-1])
    return [
        lax.dynamic_index_in_dim(blocks, (rank - k) % size, 0, False) for k in range(size)
    ]


def in_order(pieces):
    size = lax.axis_size("tp")
    rank = lax.axis_index("tp")
    whole = jnp.zeros((size,) + pieces[0].shape, pieces[0].dtype)
    for k in range(size):
        whole = lax.dynamic_update_index_in_dim(whole, pieces[k], (rank - k) % size, 0)
    return whole.reshape(-1, pieces[0].shape[-1])


def summed(value, axis):
    size = lax.axis_size(axis)
    bit = 1
    while bit < size:
        value = value + lax.ppermute(value, axis, [(i, i ^ bit) for i in range(size)])
        bit *= 2
    return value


def attention_scores(queries, keys_all, allowed, scaling):
    scores = (
        jnp.einsum("qgrd,kgd->grqk", queries, keys_all, preferred_element_type=F32) * scaling
    )
    capped = CAP * jnp.tanh(scores / CAP)
    powers = jnp.where(allowed[None, None], jnp.exp(capped), 0.0)
    return (scores, powers)


def by_rows(value):
    return with_layout_constraint(value, Layout(major_to_minor=(0, 1)))


def row_groups():
    width = lax.axis_size("ctx")
    ranks = range(lax.axis_size("fsdp") * width)
    return [[r for r in ranks if r // width % 2 == core] for core in range(2)]


def swapped(value, first, second):
    part = value.shape[-1] // (first * second)
    order = [i * second + j for j in range(second) for i in range(first)]
    return jnp.concatenate([value[..., k * part : (k + 1) * part] for k in order], axis=-1)


def by_core(value):
    return swapped(value, lax.axis_size("fsdp") // 2, 2)


def by_chip(value):
    return swapped(value, 2, lax.axis_size("fsdp") // 2)


def gather_rows(weight):
    first, second = row_groups()
    return lax.all_gather(
        weight, ROWS, axis=0, tiled=True, axis_index_groups=[first + second]
    )


def rows_of_core(left, core):
    half = left.shape[-1] // 2
    return lax.dynamic_slice_in_dim(left, core * half, half, axis=left.ndim - 1)


def sent_to_core(left, right):
    other = 1 - lax.axis_index("fsdp") % 2
    return rows_product(rows_of_core(left, other), right).astype(LOW)


def over_cores(block):
    return lax.ppermute(block, "fsdp", [(i, i ^ 1) for i in range(lax.axis_size("fsdp"))])


def chip_rows(left, right, arrived):
    own = rows_product(rows_of_core(left, lax.axis_index("fsdp") % 2), right)
    return (own + arrived.astype(F32)).astype(LOW)


def share_rows(grad):
    return lax.psum_scatter(
        grad, ROWS, scatter_dimension=0, tiled=True, axis_index_groups=row_groups()
    )


def shards(
    hidden_in,
    cotangent,
    segment_ids,
    pre_attention_gain,
    post_attention_gain,
    pre_feedforward_gain,
    post_feedforward_gain,
    query_weight,
    key_weight,
    value_weight,
    output_weight,
    gate_weight,
    up_weight,
    down_weight,
):
    length = hidden_in.shape[0]
    heads_width = query_weight.shape[1]
    kv_width = key_weight.shape[1]
    kv_heads = kv_width // HD
    repeats = heads_width // kv_width
    units = gate_weight.shape[1]
    qkv_width = heads_width + 2 * kv_width
    scaling = HD ** (-0.5)
    tp_size = lax.axis_size("tp")
    tp_rank = lax.axis_index("tp")
    piece = length // tp_size

    attention_full = gather_rows(
        jnp.concatenate([query_weight, key_weight, value_weight, output_weight], axis=1)
    )
    gate_up_full = gather_rows(jnp.concatenate([gate_weight, up_weight], axis=1))
    down_full = gather_rows(down_weight)
    qkv_full = attention_full[:, :qkv_width]
    output_full = attention_full[:, qkv_width:]

    position = lax.axis_index("ctx")
    own_ids = lax.dynamic_slice_in_dim(segment_ids, position * length, length)
    prev_start = jnp.maximum(position - 1, 0) * length
    prev_ids = jnp.where(
        position > 0, lax.dynamic_slice_in_dim(segment_ids, prev_start, length), -2
    )
    key_ids = jnp.concatenate([prev_ids, own_ids])
    query_pos = jnp.arange(length, dtype=jnp.int32)
    key_pos = jnp.arange(2 * length, dtype=jnp.int32) - length
    allowed = (query_pos[:, None] == key_pos[None, :]) | (own_ids[:, None] == key_ids[None, :]) & (
        own_ids[:, None] >= 0
    ) & (key_pos[None, :] < query_pos[:, None])

    pre_attention_gain, post_attention_gain, pre_feedforward_gain, post_feedforward_gain = (
        by_core(gain)
        for gain in (
            pre_attention_gain,
            post_attention_gain,
            pre_feedforward_gain,
            post_feedforward_gain,
        )
    )
    hidden_in = by_core(hidden_in)
    normed_one = rms(hidden_in.astype(F32), pre_attention_gain).astype(LOW)
    inputs = lax.dynamic_slice_in_dim(hidden_in, tp_rank * piece, piece).astype(F32)
    upstream = by_core(
        lax.dynamic_slice_in_dim(cotangent, tp_rank * piece, piece)
    ).astype(F32)

    qkv_low = product(normed_one, qkv_full).astype(LOW)
    queries = qkv_low[:, :heads_width].reshape(length, kv_heads, repeats, HD)
    kv_low = qkv_low[:, heads_width:]
    kv_all = jnp.concatenate([passed_along(kv_low, "ctx", 1), kv_low], axis=0)
    keys_all = kv_all[:, :kv_width].reshape(2 * length, kv_heads, HD)
    values_all = kv_all[:, kv_width:].reshape(2 * length, kv_heads, HD)
    scores, powers = attention_scores(queries, keys_all, allowed, scaling)
    totals = jnp.sum(powers, axis=-1, keepdims=True)
    probs_low = (powers / totals).astype(LOW)
    attended = jnp.einsum("grqk,kgd->qgrd", probs_low, values_all, preferred_element_type=F32)
    attended_low = attended.reshape(length, -1).astype(LOW)

    branch_one = scattered(
        ordered_blocks(transposed_product(attended_low, output_full).astype(LOW))
    )
    middle = inputs + rms(branch_one, post_attention_gain)
    normed_two_own = rms(middle, pre_feedforward_gain).astype(LOW)
    normed_two = jnp.concatenate(gathered(normed_two_own), axis=0)

    gate_up = product(normed_two, gate_up_full)
    gate_value = gate_up[:, :units]
    up_value = gate_up[:, units:]
    hidden_low = geglu(gate_value, up_value).astype(LOW)
    branch_two = scattered(
        turned_blocks(transposed_product(hidden_low, down_full).astype(LOW))
    )
    result = middle + rms(branch_two, post_feedforward_gain)

    _, pull_four = jax.vjp(rms, branch_two, post_feedforward_gain)
    grad_branch_two, grad_gain_four = pull_four(upstream)
    grad_two_low = jnp.concatenate(gathered(grad_branch_two.astype(LOW)), axis=0)

    result_low, grad_two_low = lax.optimization_barrier(
        (by_chip(result.astype(LOW)), grad_two_low)
    )
    down_sent, grad_two_low = lax.optimization_barrier(
        (sent_to_core(grad_two_low, hidden_low), grad_two_low)
    )
    down_arrived = over_cores(down_sent)
    outputs = in_order(sent_gathered(result_low))
    _, pull_glu = jax.vjp(geglu, gate_value, up_value)
    grad_gate, grad_up = pull_glu(product(grad_two_low, down_full))
    grad_gate_up = jnp.concatenate([grad_gate.astype(LOW), grad_up.astype(LOW)], axis=1)
    grad_down_low, grad_gate_up = lax.optimization_barrier(
        (chip_rows(grad_two_low, hidden_low, down_arrived), grad_gate_up)
    )
    down_share = share_rows(grad_down_low)
    grad_normed_two = transposed_product(grad_gate_up, gate_up_full).astype(LOW)
    grad_normed_two = sent_scattered(turned_blocks(grad_normed_two))
    gate_up_sent = sent_to_core(normed_two, grad_gate_up)
    gate_up_arrived = over_cores(gate_up_sent)
    grad_gate_up_low = chip_rows(normed_two, grad_gate_up, gate_up_arrived)

    gate_up_share = share_rows(grad_gate_up_low)

    _, pull_three = jax.vjp(rms, middle, pre_feedforward_gain)
    grad_middle_norm, grad_gain_three = pull_three(grad_normed_two)
    grad_middle = upstream + grad_middle_norm
    _, pull_two = jax.vjp(rms, branch_one, post_attention_gain)
    grad_branch_one, grad_gain_two = pull_two(grad_middle)
    grad_one_low = in_order(sent_gathered(grad_branch_one.astype(LOW)))

    output_sent = sent_to_core(grad_one_low, attended_low)
    output_arrived = over_cores(output_sent)
    output_share = share_rows(chip_rows(grad_one_low, attended_low, output_arrived))
    grad_attended = (
        product(grad_one_low, output_full).astype(LOW).reshape(length, kv_heads, repeats, HD)
    )
    probs = powers / totals
    grad_probs = jnp.einsum(
        "qgrd,kgd->grqk", grad_attended, values_all, preferred_element_type=F32
    )
    inner = jnp.sum(probs * grad_probs, axis=-1, keepdims=True)
    grad_capped = probs * (grad_probs - inner)
    squashed = jnp.tanh(scores / CAP)
    grad_scores = (grad_capped * (1.0 - squashed * squashed)).astype(LOW)
    grad_query_low = (
        (
            jnp.einsum("grqk,kgd->qgrd", grad_scores, keys_all, preferred_element_type=F32)
            * scaling
        )
        .reshape(length, -1)
        .astype(LOW)
    )
    grad_keys_all = (
        jnp.einsum("grqk,qgrd->kgd", grad_scores, queries, preferred_element_type=F32) * scaling
    ).reshape(2 * length, -1)
    grad_values_all = jnp.einsum(
        "grqk,qgrd->kgd", probs_low, grad_attended, preferred_element_type=F32
    ).reshape(2 * length, -1)
    grad_kv_all = jnp.concatenate([grad_keys_all, grad_values_all], axis=1)
    grad_kv_back = passed_along(grad_kv_all[:length].astype(LOW), "ctx", -1).astype(F32)
    grad_kv_low = (grad_kv_all[length:] + grad_kv_back).astype(LOW)
    grad_qkv = jnp.concatenate([grad_query_low, grad_kv_low], axis=1)
    grad_normed_one = transposed_product(grad_qkv, qkv_full).astype(LOW)
    grad_normed_one = sent_scattered(ordered_blocks(grad_normed_one))
    qkv_sent = sent_to_core(normed_one, grad_qkv)
    qkv_arrived = over_cores(qkv_sent)
    grad_qkv_low = by_rows(chip_rows(normed_one, grad_qkv, qkv_arrived))
    qkv_share = share_rows(grad_qkv_low).astype(F32)

    _, pull_one = jax.vjp(rms, inputs, pre_attention_gain)
    grad_inputs_norm, grad_gain_one = pull_one(grad_normed_one)
    grad_inputs_own, grad_qkv_low = lax.optimization_barrier(
        (by_chip((grad_middle + grad_inputs_norm).astype(LOW)), grad_qkv_low)
    )
    grad_inputs = in_order(sent_gathered(grad_inputs_own))

    gains = by_chip(jnp.stack([grad_gain_one, grad_gain_two, grad_gain_three, grad_gain_four]))
    for axis in ("tp",) + ROWS:
        gains = summed(gains, axis)
    share = attention_full.shape[0] // (lax.axis_size("fsdp") * lax.axis_size("ctx"))
    row_rank = lax.axis_index("fsdp") * lax.axis_size("ctx") + lax.axis_index("ctx")
    gain_shares = lax.dynamic_slice_in_dim(gains, row_rank * share, share, axis=1)
    edges = [0, heads_width, heads_width + kv_width, qkv_width]
    qkv_shares = [qkv_share[:, a:b] for a, b in zip(edges[:-1], edges[1:])]
    gate_up_share = gate_up_share.astype(F32)
    return (
        (outputs, grad_inputs)
        + tuple(gain_shares[i] for i in range(4))
        + tuple(qkv_shares)
        + (output_share.astype(F32), gate_up_share[:, :units], gate_up_share[:, units:], down_share.astype(F32))
    )


def solution(mesh):
    tokens = P(ROWS, None)
    weight = P(ROWS, "tp")
    return jax.shard_map(
        shards,
        mesh=mesh,
        in_specs=(tokens, tokens, P("fsdp")) + (P(),) * 4 + (weight,) * 7,
        out_specs=(tokens, tokens) + (P(ROWS),) * 4 + (weight,) * 7,
        check_vma=False,
    )
```

```python
import jax
import jax.numpy as jnp
from jax import lax
from jax.experimental.layout import Layout, with_layout_constraint
from jax.sharding import PartitionSpec as P


HD = 256
BLOCK_TOKENS = 128
MAX_DOC_BLOCKS = 4
CAP = 50.0
EPS = 1e-06
ROWS = ("fsdp", "ctx")
LOW = jnp.bfloat16
F32 = jnp.float32


def passed_along(block, axis, distance):
    devices = range(lax.axis_size(axis))
    route = [(i - distance, i) for i in devices if i - distance in devices]
    return lax.ppermute(block, axis, route)


def rms(value, gain):
    return value * lax.rsqrt(jnp.mean(value * value, axis=-1, keepdims=True) + EPS) * gain


def geglu(gate_value, up_value):
    return jax.nn.gelu(gate_value, approximate=True) * up_value


def product(left, right):
    return jnp.dot(left, right, preferred_element_type=F32)


def rows_product(left, right):
    return lax.dot_general(left, right, (((0,), (0,)), ((), ())), preferred_element_type=F32)


def transposed_product(left, right):
    return lax.dot_general(left, right, (((1,), (1,)), ((), ())), preferred_element_type=F32)


def onward(block, distance, senders):
    return lax.ppermute(block, "tp", [(i, i + distance) for i in senders])


def shift(block, distance):
    size = lax.axis_size("tp")
    return lax.ppermute(block, "tp", [(i, (i + distance) % size) for i in range(size)])


def distances(size):
    return sorted(range(1, size), key=lambda k: (abs(2 * k - size), k))


def sent_scattered(blocks):
    blocks = lax.optimization_barrier(tuple(blocks))
    arrived = [shift(blocks[k], -k) for k in distances(len(blocks))]
    total = blocks[0].astype(F32)
    for block in arrived:
        total = total + block.astype(F32)
    return total


def sent_gathered(block):
    size = lax.axis_size("tp")
    pieces = {k: shift(block, k) for k in distances(size)}
    return [block] + [pieces[k] for k in range(1, size)]


def scattered(blocks):
    size = lax.axis_size("tp")
    rising, falling = None, None
    for step in range(1, size):
        rise, fall = blocks[step], blocks[size - step]
        if rising is not None:
            rise = (rise.astype(F32) + rising.astype(F32)).astype(LOW)
            fall = (fall.astype(F32) + falling.astype(F32)).astype(LOW)
        rise, fall = lax.optimization_barrier((rise, fall))
        rising = onward(rise, 1, range(step))
        falling = onward(fall, -1, range(size - step, size))
    return blocks[0].astype(F32) + (rising.astype(F32) + falling.astype(F32))


def gathered(block):
    size = lax.axis_size("tp")
    rank = lax.axis_index("tp")
    rising, falling = [block], [block]
    for step in range(1, size):
        rise = onward(rising[-1], 1, range(step - 1, size - 1))
        fall = onward(falling[-1], -1, range(1, size - step + 1))
        rise, fall = lax.optimization_barrier((rise, fall))
        rising.append(rise)
        falling.append(fall)
    return [block] + [
        jnp.where(rank >= k, rising[k], falling[size - k]) for k in range(1, size)
    ]


def turned_blocks(partial):
    size = lax.axis_size("tp")
    blocks = partial.reshape(size, -1, partial.shape[-1])
    return [blocks[k] for k in range(size)]


def ordered_blocks(partial):
    size = lax.axis_size("tp")
    rank = lax.axis_index("tp")
    blocks = partial.reshape(size, -1, partial.shape[-1])
    return [
        lax.dynamic_index_in_dim(blocks, (rank - k) % size, 0, False) for k in range(size)
    ]


def in_order(pieces):
    size = lax.axis_size("tp")
    rank = lax.axis_index("tp")
    whole = jnp.zeros((size,) + pieces[0].shape, pieces[0].dtype)
    for k in range(size):
        whole = lax.dynamic_update_index_in_dim(whole, pieces[k], (rank - k) % size, 0)
    return whole.reshape(-1, pieces[0].shape[-1])


def summed(value, axis):
    size = lax.axis_size(axis)
    bit = 1
    while bit < size:
        value = value + lax.ppermute(value, axis, [(i, i ^ bit) for i in range(size)])
        bit *= 2
    return value


def attention_scores(queries, keys_all, allowed, scaling):
    scores = (
        jnp.einsum("qgrd,kgd->grqk", queries, keys_all, preferred_element_type=F32) * scaling
    )
    capped = CAP * jnp.tanh(scores / CAP)
    powers = jnp.where(allowed[None, None], jnp.exp(capped), 0.0)
    return (scores, powers)


def by_rows(value):
    return with_layout_constraint(value, Layout(major_to_minor=(0, 1)))


def row_groups():
    width = lax.axis_size("ctx")
    ranks = range(lax.axis_size("fsdp") * width)
    return [[r for r in ranks if r // width % 2 == core] for core in range(2)]


def swapped(value, first, second):
    part = value.shape[-1] // (first * second)
    order = [i * second + j for j in range(second) for i in range(first)]
    return jnp.concatenate([value[..., k * part : (k + 1) * part] for k in order], axis=-1)


def by_core(value):
    return swapped(value, lax.axis_size("fsdp") // 2, 2)


def by_chip(value):
    return swapped(value, 2, lax.axis_size("fsdp") // 2)


def gather_rows(weight):
    first, second = row_groups()
    return lax.all_gather(
        weight, ROWS, axis=0, tiled=True, axis_index_groups=[first + second]
    )


def sent_rows(weight, after=()):
    ranks = lax.axis_size("fsdp") * lax.axis_size("ctx")
    if (lax.axis_size("fsdp"), lax.axis_size("ctx")) != (4, 2):
        return gather_rows(weight), ()
    core, pair, width = 2, 4, 1

    def sent(block, bits):
        return lax.ppermute(block, ROWS, [(r, r ^ bits) for r in range(ranks)])

    weight, after = lax.optimization_barrier((weight, after))
    held = {0: weight}
    for bits in (pair | width, width, pair):
        held[bits] = sent(weight, bits)
    for bits in (0, width, pair, pair | width):
        held[bits | core] = sent(held[bits], core)
    place = {0: 0, width: 1, pair: 2, core: 4}
    rank = lax.axis_index("fsdp") * 2 + lax.axis_index("ctx")
    own = (rank // core) % 2 * 4 + rank // pair * 2 + rank % 2
    whole = jnp.zeros((ranks,) + weight.shape, weight.dtype)
    for bits in held:
        at = own ^ (place[bits & width] | place[bits & pair] | place[bits & core])
        whole = lax.dynamic_update_index_in_dim(whole, held[bits], at, 0)
    return whole.reshape(-1, weight.shape[1]), (held[pair | width],)


def rows_of_core(left, core):
    half = left.shape[-1] // 2
    return lax.dynamic_slice_in_dim(left, core * half, half, axis=left.ndim - 1)


def sent_to_core(left, right):
    other = 1 - lax.axis_index("fsdp") % 2
    return rows_product(rows_of_core(left, other), right).astype(LOW)


def over_cores(block):
    return lax.ppermute(block, "fsdp", [(i, i ^ 1) for i in range(lax.axis_size("fsdp"))])


def chip_rows(left, right, arrived):
    own = rows_product(rows_of_core(left, lax.axis_index("fsdp") % 2), right)
    return (own + arrived.astype(F32)).astype(LOW)


def share_rows(grad):
    return lax.psum_scatter(
        grad, ROWS, scatter_dimension=0, tiled=True, axis_index_groups=row_groups()
    )


def shards(
    hidden_in,
    cotangent,
    segment_ids,
    pre_attention_gain,
    post_attention_gain,
    pre_feedforward_gain,
    post_feedforward_gain,
    query_weight,
    key_weight,
    value_weight,
    output_weight,
    gate_weight,
    up_weight,
    down_weight,
):
    length = hidden_in.shape[0]
    heads_width = query_weight.shape[1]
    kv_width = key_weight.shape[1]
    kv_heads = kv_width // HD
    repeats = heads_width // kv_width
    units = gate_weight.shape[1]
    qkv_width = heads_width + 2 * kv_width
    scaling = HD ** (-0.5)
    tp_size = lax.axis_size("tp")
    tp_rank = lax.axis_index("tp")
    piece = length // tp_size

    qkv_full, first_sent = sent_rows(
        jnp.concatenate([query_weight, key_weight, value_weight], axis=1)
    )
    output_full, _ = sent_rows(output_weight, first_sent)
    gate_up_full = gather_rows(jnp.concatenate([gate_weight, up_weight], axis=1))
    down_full = gather_rows(down_weight)

    position = lax.axis_index("ctx")
    own_ids = lax.dynamic_slice_in_dim(segment_ids, position * length, length)
    before = min(length, (MAX_DOC_BLOCKS - 1) * BLOCK_TOKENS)
    prev_start = jnp.maximum(position * length - before, 0)
    prev_ids = jnp.where(
        position > 0, lax.dynamic_slice_in_dim(segment_ids, prev_start, before), -2
    )
    key_ids = jnp.concatenate([prev_ids, own_ids])
    query_pos = jnp.arange(length, dtype=jnp.int32)
    key_pos = jnp.arange(before + length, dtype=jnp.int32) - before
    allowed = (query_pos[:, None] == key_pos[None, :]) | (own_ids[:, None] == key_ids[None, :]) & (
        own_ids[:, None] >= 0
    ) & (key_pos[None, :] < query_pos[:, None])

    pre_attention_gain, post_attention_gain, pre_feedforward_gain, post_feedforward_gain = (
        by_core(gain)
        for gain in (
            pre_attention_gain,
            post_attention_gain,
            pre_feedforward_gain,
            post_feedforward_gain,
        )
    )
    hidden_in = by_core(hidden_in)
    normed_one = rms(hidden_in.astype(F32), pre_attention_gain).astype(LOW)
    inputs = lax.dynamic_slice_in_dim(hidden_in, tp_rank * piece, piece).astype(F32)
    upstream = by_core(
        lax.dynamic_slice_in_dim(cotangent, tp_rank * piece, piece)
    ).astype(F32)

    qkv_low = product(normed_one, qkv_full).astype(LOW)
    queries = qkv_low[:, :heads_width].reshape(length, kv_heads, repeats, HD)
    kv_low = qkv_low[:, heads_width:]
    kv_all = jnp.concatenate([passed_along(kv_low[-before:], "ctx", 1), kv_low], axis=0)
    keys_all = kv_all[:, :kv_width].reshape(before + length, kv_heads, HD)
    values_all = kv_all[:, kv_width:].reshape(before + length, kv_heads, HD)
    scores, powers = attention_scores(queries, keys_all, allowed, scaling)
    totals = jnp.sum(powers, axis=-1, keepdims=True)
    probs_low = (powers / totals).astype(LOW)
    attended = jnp.einsum("grqk,kgd->qgrd", probs_low, values_all, preferred_element_type=F32)
    attended_low = attended.reshape(length, -1).astype(LOW)

    branch_one = scattered(
        ordered_blocks(transposed_product(attended_low, output_full).astype(LOW))
    )
    middle = inputs + rms(branch_one, post_attention_gain)
    normed_two_own = rms(middle, pre_feedforward_gain).astype(LOW)
    normed_two = jnp.concatenate(gathered(normed_two_own), axis=0)

    gate_up = product(normed_two, gate_up_full)
    gate_value = gate_up[:, :units]
    up_value = gate_up[:, units:]
    hidden_low = geglu(gate_value, up_value).astype(LOW)
    branch_two = scattered(
        turned_blocks(transposed_product(hidden_low, down_full).astype(LOW))
    )
    result = middle + rms(branch_two, post_feedforward_gain)

    _, pull_four = jax.vjp(rms, branch_two, post_feedforward_gain)
    grad_branch_two, grad_gain_four = pull_four(upstream)
    grad_two_low = jnp.concatenate(gathered(grad_branch_two.astype(LOW)), axis=0)

    down_sent, grad_two_low = lax.optimization_barrier(
        (sent_to_core(grad_two_low, hidden_low), grad_two_low)
    )
    down_arrived = over_cores(down_sent)
    _, pull_glu = jax.vjp(geglu, gate_value, up_value)
    grad_gate, grad_up = pull_glu(product(grad_two_low, down_full))
    grad_gate_up = jnp.concatenate([grad_gate.astype(LOW), grad_up.astype(LOW)], axis=1)
    grad_normed_two = transposed_product(grad_gate_up, gate_up_full).astype(LOW)
    grad_normed_two = sent_scattered(turned_blocks(grad_normed_two))
    grad_down_low = chip_rows(grad_two_low, hidden_low, down_arrived)
    down_share = share_rows(grad_down_low)
    gate_up_sent = sent_to_core(normed_two, grad_gate_up)
    gate_up_arrived = over_cores(gate_up_sent)
    grad_gate_up_low = chip_rows(normed_two, grad_gate_up, gate_up_arrived)
    gate_up_share = share_rows(grad_gate_up_low)

    _, pull_three = jax.vjp(rms, middle, pre_feedforward_gain)
    grad_middle_norm, grad_gain_three = pull_three(grad_normed_two)
    grad_middle = upstream + grad_middle_norm
    _, pull_two = jax.vjp(rms, branch_one, post_attention_gain)
    grad_branch_one, grad_gain_two = pull_two(grad_middle)
    grad_one_low = in_order(sent_gathered(grad_branch_one.astype(LOW)))
    result_low, grad_one_low = lax.optimization_barrier(
        (by_chip(result.astype(LOW)), grad_one_low)
    )
    outputs = in_order(sent_gathered(result_low))

    output_sent = sent_to_core(grad_one_low, attended_low)
    output_arrived = over_cores(output_sent)
    output_share = share_rows(chip_rows(grad_one_low, attended_low, output_arrived))
    grad_attended = product(grad_one_low, output_full).astype(LOW)
    grad_attended = grad_attended.reshape(length, kv_heads, repeats, HD)
    probs = powers / totals
    grad_probs = jnp.einsum(
        "qgrd,kgd->grqk", grad_attended, values_all, preferred_element_type=F32
    )
    inner = jnp.sum(probs * grad_probs, axis=-1, keepdims=True)
    grad_capped = probs * (grad_probs - inner)
    squashed = jnp.tanh(scores / CAP)
    grad_scores = (grad_capped * (1.0 - squashed * squashed)).astype(LOW)
    grad_query_low = (
        (
            jnp.einsum("grqk,kgd->qgrd", grad_scores, keys_all, preferred_element_type=F32)
            * scaling
        )
        .reshape(length, -1)
        .astype(LOW)
    )
    grad_keys_all = (
        jnp.einsum("grqk,qgrd->kgd", grad_scores, queries, preferred_element_type=F32) * scaling
    ).reshape(before + length, -1)
    grad_values_all = jnp.einsum(
        "grqk,qgrd->kgd", probs_low, grad_attended, preferred_element_type=F32
    ).reshape(before + length, -1)
    grad_kv_all = jnp.concatenate([grad_keys_all, grad_values_all], axis=1)
    grad_kv_back = passed_along(grad_kv_all[:before].astype(LOW), "ctx", -1)
    grad_kv_back = jnp.pad(grad_kv_back, ((length - before, 0), (0, 0))).astype(F32)
    grad_kv_low = (grad_kv_all[before:] + grad_kv_back).astype(LOW)
    grad_qkv = jnp.concatenate([grad_query_low, grad_kv_low], axis=1)
    grad_normed_one = transposed_product(grad_qkv, qkv_full).astype(LOW)
    grad_normed_one = sent_scattered(ordered_blocks(grad_normed_one))
    qkv_sent = sent_to_core(normed_one, grad_qkv)
    qkv_arrived = over_cores(qkv_sent)
    grad_qkv_low = by_rows(chip_rows(normed_one, grad_qkv, qkv_arrived))
    qkv_share = share_rows(grad_qkv_low).astype(F32)

    _, pull_one = jax.vjp(rms, inputs, pre_attention_gain)
    grad_inputs_norm, grad_gain_one = pull_one(grad_normed_one)
    grad_inputs_low = by_chip((grad_middle + grad_inputs_norm).astype(LOW))
    grad_inputs = in_order(sent_gathered(grad_inputs_low))

    gains = by_chip(jnp.stack([grad_gain_one, grad_gain_two, grad_gain_three, grad_gain_four]))
    for axis in ("tp",) + ROWS:
        gains = summed(gains, axis)
    share = qkv_full.shape[0] // (lax.axis_size("fsdp") * lax.axis_size("ctx"))
    row_rank = lax.axis_index("fsdp") * lax.axis_size("ctx") + lax.axis_index("ctx")
    gain_shares = lax.dynamic_slice_in_dim(gains, row_rank * share, share, axis=1)
    edges = [0, heads_width, heads_width + kv_width, qkv_width]
    qkv_shares = [qkv_share[:, a:b] for a, b in zip(edges[:-1], edges[1:])]
    gate_up_share = gate_up_share.astype(F32)
    return (
        (outputs, grad_inputs)
        + tuple(gain_shares[i] for i in range(4))
        + tuple(qkv_shares)
        + (output_share.astype(F32), gate_up_share[:, :units], gate_up_share[:, units:], down_share.astype(F32))
    )


def solution(mesh):
    tokens = P(ROWS, None)
    weight = P(ROWS, "tp")
    return jax.shard_map(
        shards,
        mesh=mesh,
        in_specs=(tokens, tokens, P("fsdp")) + (P(),) * 4 + (weight,) * 7,
        out_specs=(tokens, tokens) + (P(ROWS),) * 4 + (weight,) * 7,
        check_vma=False,
    )
```

```python
import jax
import jax.numpy as jnp
from jax import lax
from jax.experimental.layout import Layout, with_layout_constraint
from jax.sharding import PartitionSpec as P


HD = 256
BLOCK_TOKENS = 128
MAX_DOC_BLOCKS = 4
CAP = 50.0
EPS = 1e-06
ROWS = ("fsdp", "ctx")
LOW = jnp.bfloat16
F32 = jnp.float32


def passed_along(block, axis, distance):
    devices = range(lax.axis_size(axis))
    route = [(i - distance, i) for i in devices if i - distance in devices]
    return lax.ppermute(block, axis, route)


def rms(value, gain):
    return value * lax.rsqrt(jnp.mean(value * value, axis=-1, keepdims=True) + EPS) * gain


def geglu(gate_value, up_value):
    return jax.nn.gelu(gate_value, approximate=True) * up_value


def product(left, right):
    return jnp.dot(left, right, preferred_element_type=F32)


def rows_product(left, right):
    return lax.dot_general(left, right, (((0,), (0,)), ((), ())), preferred_element_type=F32)


def transposed_product(left, right):
    return lax.dot_general(left, right, (((1,), (1,)), ((), ())), preferred_element_type=F32)


def onward(block, distance, senders):
    return lax.ppermute(block, "tp", [(i, i + distance) for i in senders])


def shift(block, distance):
    size = lax.axis_size("tp")
    return lax.ppermute(block, "tp", [(i, (i + distance) % size) for i in range(size)])


def distances(size):
    return sorted(range(1, size), key=lambda k: (abs(2 * k - size), k))


def sent_scattered(blocks):
    blocks = lax.optimization_barrier(tuple(blocks))
    arrived = [shift(blocks[k], -k) for k in distances(len(blocks))]
    total = blocks[0].astype(F32)
    for block in arrived:
        total = total + block.astype(F32)
    return total


def sent_gathered(block):
    size = lax.axis_size("tp")
    pieces = {k: shift(block, k) for k in distances(size)}
    return [block] + [pieces[k] for k in range(1, size)]


def scattered(blocks):
    size = lax.axis_size("tp")
    rising, falling = None, None
    for step in range(1, size):
        rise, fall = blocks[step], blocks[size - step]
        if rising is not None:
            rise = (rise.astype(F32) + rising.astype(F32)).astype(LOW)
            fall = (fall.astype(F32) + falling.astype(F32)).astype(LOW)
        rise, fall = lax.optimization_barrier((rise, fall))
        rising = onward(rise, 1, range(step))
        falling = onward(fall, -1, range(size - step, size))
    return blocks[0].astype(F32) + (rising.astype(F32) + falling.astype(F32))


def gathered(block):
    size = lax.axis_size("tp")
    rank = lax.axis_index("tp")
    rising, falling = [block], [block]
    for step in range(1, size):
        rise = onward(rising[-1], 1, range(step - 1, size - 1))
        fall = onward(falling[-1], -1, range(1, size - step + 1))
        rise, fall = lax.optimization_barrier((rise, fall))
        rising.append(rise)
        falling.append(fall)
    return [block] + [
        jnp.where(rank >= k, rising[k], falling[size - k]) for k in range(1, size)
    ]


def turned_blocks(partial):
    size = lax.axis_size("tp")
    blocks = partial.reshape(size, -1, partial.shape[-1])
    return [blocks[k] for k in range(size)]


def ordered_blocks(partial):
    size = lax.axis_size("tp")
    rank = lax.axis_index("tp")
    blocks = partial.reshape(size, -1, partial.shape[-1])
    return [
        lax.dynamic_index_in_dim(blocks, (rank - k) % size, 0, False) for k in range(size)
    ]


def in_order(pieces):
    size = lax.axis_size("tp")
    rank = lax.axis_index("tp")
    whole = jnp.zeros((size,) + pieces[0].shape, pieces[0].dtype)
    for k in range(size):
        whole = lax.dynamic_update_index_in_dim(whole, pieces[k], (rank - k) % size, 0)
    return whole.reshape(-1, pieces[0].shape[-1])


def exchanged(value):
    size = lax.axis_size("tp")
    rank = lax.axis_index("tp")
    width = value.shape[1] // size
    pieces = [value[:, k * width : (k + 1) * width] for k in range(size)]
    pieces = lax.optimization_barrier(tuple(pieces))
    whole = jnp.zeros((size,) + pieces[0].shape, value.dtype)
    whole = lax.dynamic_update_index_in_dim(whole, pieces[0], rank, 0)
    for k in distances(size):
        arrived = shift(pieces[k], -k)
        whole = lax.dynamic_update_index_in_dim(whole, arrived, (rank + k) % size, 0)
    return whole.reshape(-1, width)


def summed(value, axis):
    size = lax.axis_size(axis)
    bit = 1
    while bit < size:
        value = value + lax.ppermute(value, axis, [(i, i ^ bit) for i in range(size)])
        bit *= 2
    return value


def attention_scores(queries, keys_all, allowed, scaling):
    scores = (
        jnp.einsum("qgrd,kgd->grqk", queries, keys_all, preferred_element_type=F32) * scaling
    )
    capped = CAP * jnp.tanh(scores / CAP)
    powers = jnp.where(allowed[None, None], jnp.exp(capped), 0.0)
    return (scores, powers)


def by_rows(value):
    return with_layout_constraint(value, Layout(major_to_minor=(0, 1)))


def row_groups():
    width = lax.axis_size("ctx")
    ranks = range(lax.axis_size("fsdp") * width)
    return [[r for r in ranks if r // width % 2 == core] for core in range(2)]


def swapped(value, first, second):
    part = value.shape[-1] // (first * second)
    order = [i * second + j for j in range(second) for i in range(first)]
    return jnp.concatenate([value[..., k * part : (k + 1) * part] for k in order], axis=-1)


def by_core(value):
    return swapped(value, lax.axis_size("fsdp") // 2, 2)


def by_chip(value):
    return swapped(value, 2, lax.axis_size("fsdp") // 2)


def gather_rows(weight):
    first, second = row_groups()
    return lax.all_gather(
        weight, ROWS, axis=0, tiled=True, axis_index_groups=[first + second]
    )


def rows_of_core(left, core):
    half = left.shape[-1] // 2
    return lax.dynamic_slice_in_dim(left, core * half, half, axis=left.ndim - 1)


def sent_to_core(left, right):
    other = 1 - lax.axis_index("fsdp") % 2
    return rows_product(rows_of_core(left, other), right).astype(LOW)


def over_cores(block):
    return lax.ppermute(block, "fsdp", [(i, i ^ 1) for i in range(lax.axis_size("fsdp"))])


def chip_rows(left, right, arrived):
    own = rows_product(rows_of_core(left, lax.axis_index("fsdp") % 2), right)
    return (own + arrived.astype(F32)).astype(LOW)


def share_rows(grad):
    return lax.psum_scatter(
        grad, ROWS, scatter_dimension=0, tiled=True, axis_index_groups=row_groups()
    )


def shards(
    hidden_in,
    cotangent,
    segment_ids,
    pre_attention_gain,
    post_attention_gain,
    pre_feedforward_gain,
    post_feedforward_gain,
    query_weight,
    key_weight,
    value_weight,
    output_weight,
    gate_weight,
    up_weight,
    down_weight,
):
    length = hidden_in.shape[0]
    heads_width = query_weight.shape[1]
    kv_width = key_weight.shape[1]
    kv_heads = kv_width // HD
    repeats = heads_width // kv_width
    units = gate_weight.shape[1]
    qkv_width = heads_width + 2 * kv_width
    scaling = HD ** (-0.5)
    tp_size = lax.axis_size("tp")
    tp_rank = lax.axis_index("tp")
    piece = length // tp_size

    attention_full = gather_rows(
        jnp.concatenate([query_weight, key_weight, value_weight, output_weight], axis=1)
    )
    qkv_full = attention_full[:, :qkv_width]
    output_full = attention_full[:, qkv_width:]
    units_full = gather_rows(jnp.concatenate([gate_weight, up_weight, down_weight], axis=1))
    gate_up_full = units_full[:, : 2 * units]
    down_full = units_full[:, 2 * units :]
    output_pieces = jnp.concatenate(sent_gathered(output_weight), axis=1)
    output_all = gather_rows(output_pieces)

    position = lax.axis_index("ctx")
    own_ids = lax.dynamic_slice_in_dim(segment_ids, position * length, length)
    before = min(length, (MAX_DOC_BLOCKS - 1) * BLOCK_TOKENS)
    prev_start = jnp.maximum(position * length - before, 0)
    prev_ids = jnp.where(
        position > 0, lax.dynamic_slice_in_dim(segment_ids, prev_start, before), -2
    )
    key_ids = jnp.concatenate([prev_ids, own_ids])
    query_pos = jnp.arange(length, dtype=jnp.int32)
    key_pos = jnp.arange(before + length, dtype=jnp.int32) - before
    allowed = (query_pos[:, None] == key_pos[None, :]) | (own_ids[:, None] == key_ids[None, :]) & (
        own_ids[:, None] >= 0
    ) & (key_pos[None, :] < query_pos[:, None])

    pre_attention_gain, post_attention_gain, pre_feedforward_gain, post_feedforward_gain = (
        by_core(gain)
        for gain in (
            pre_attention_gain,
            post_attention_gain,
            pre_feedforward_gain,
            post_feedforward_gain,
        )
    )
    hidden_in = by_core(hidden_in)
    normed_one = rms(hidden_in.astype(F32), pre_attention_gain).astype(LOW)
    inputs = lax.dynamic_slice_in_dim(hidden_in, tp_rank * piece, piece).astype(F32)
    upstream = by_core(
        lax.dynamic_slice_in_dim(cotangent, tp_rank * piece, piece)
    ).astype(F32)

    qkv_low = product(normed_one, qkv_full).astype(LOW)
    queries = qkv_low[:, :heads_width].reshape(length, kv_heads, repeats, HD)
    kv_low = qkv_low[:, heads_width:]
    kv_all = jnp.concatenate([passed_along(kv_low[-before:], "ctx", 1), kv_low], axis=0)
    keys_all = kv_all[:, :kv_width].reshape(before + length, kv_heads, HD)
    values_all = kv_all[:, kv_width:].reshape(before + length, kv_heads, HD)
    scores, powers = attention_scores(queries, keys_all, allowed, scaling)
    totals = jnp.sum(powers, axis=-1, keepdims=True)
    probs_low = (powers / totals).astype(LOW)
    attended = jnp.einsum("grqk,kgd->qgrd", probs_low, values_all, preferred_element_type=F32)
    attended_low = attended.reshape(length, -1).astype(LOW)

    branch_one = scattered(
        ordered_blocks(transposed_product(attended_low, output_full).astype(LOW))
    )
    middle = inputs + rms(branch_one, post_attention_gain)
    normed_two_own = rms(middle, pre_feedforward_gain).astype(LOW)
    normed_two = jnp.concatenate(gathered(normed_two_own), axis=0)

    gate_up = product(normed_two, gate_up_full)
    gate_value = gate_up[:, :units]
    up_value = gate_up[:, units:]
    hidden_low = geglu(gate_value, up_value).astype(LOW)
    branch_two = scattered(
        turned_blocks(transposed_product(hidden_low, down_full).astype(LOW))
    )
    result = middle + rms(branch_two, post_feedforward_gain)

    _, pull_four = jax.vjp(rms, branch_two, post_feedforward_gain)
    grad_branch_two, grad_gain_four = pull_four(upstream)
    grad_two_low = jnp.concatenate(gathered(grad_branch_two.astype(LOW)), axis=0)

    result_low, grad_two_low = lax.optimization_barrier(
        (by_chip(result.astype(LOW)), grad_two_low)
    )
    outputs = lax.all_gather(result_low, "tp", axis=0, tiled=True)
    down_sent, grad_two_low = lax.optimization_barrier(
        (sent_to_core(grad_two_low, hidden_low), grad_two_low)
    )
    down_arrived = over_cores(down_sent)
    _, pull_glu = jax.vjp(geglu, gate_value, up_value)
    grad_gate, grad_up = pull_glu(product(grad_two_low, down_full))
    grad_gate_up = jnp.concatenate([grad_gate.astype(LOW), grad_up.astype(LOW)], axis=1)
    grad_normed_two = transposed_product(grad_gate_up, gate_up_full).astype(LOW)
    grad_normed_two = sent_scattered(turned_blocks(grad_normed_two))
    grad_down_low = chip_rows(grad_two_low, hidden_low, down_arrived)
    down_share = share_rows(grad_down_low)
    gate_up_sent = sent_to_core(normed_two, grad_gate_up)
    gate_up_arrived = over_cores(gate_up_sent)
    grad_gate_up_low = chip_rows(normed_two, grad_gate_up, gate_up_arrived)
    gate_up_share = share_rows(grad_gate_up_low)

    _, pull_three = jax.vjp(rms, middle, pre_feedforward_gain)
    grad_middle_norm, grad_gain_three = pull_three(grad_normed_two)
    grad_middle = upstream + grad_middle_norm
    _, pull_two = jax.vjp(rms, branch_one, post_attention_gain)
    grad_branch_one, grad_gain_two = pull_two(grad_middle)
    grad_one_own = grad_branch_one.astype(LOW)
    grad_attended = product(grad_one_own, output_all).astype(LOW)
    grad_attended, grad_one_own = lax.optimization_barrier(
        (exchanged(grad_attended), grad_one_own)
    )
    grad_attended = grad_attended.reshape(length, kv_heads, repeats, HD)
    grad_one_low = in_order(sent_gathered(grad_one_own))
    output_sent = sent_to_core(grad_one_low, attended_low)
    output_arrived = over_cores(output_sent)
    output_share = share_rows(chip_rows(grad_one_low, attended_low, output_arrived))
    probs = powers / totals
    grad_probs = jnp.einsum(
        "qgrd,kgd->grqk", grad_attended, values_all, preferred_element_type=F32
    )
    inner = jnp.sum(probs * grad_probs, axis=-1, keepdims=True)
    grad_capped = probs * (grad_probs - inner)
    squashed = jnp.tanh(scores / CAP)
    grad_scores = (grad_capped * (1.0 - squashed * squashed)).astype(LOW)
    grad_query_low = (
        (
            jnp.einsum("grqk,kgd->qgrd", grad_scores, keys_all, preferred_element_type=F32)
            * scaling
        )
        .reshape(length, -1)
        .astype(LOW)
    )
    grad_keys_all = (
        jnp.einsum("grqk,qgrd->kgd", grad_scores, queries, preferred_element_type=F32) * scaling
    ).reshape(before + length, -1)
    grad_values_all = jnp.einsum(
        "grqk,qgrd->kgd", probs_low, grad_attended, preferred_element_type=F32
    ).reshape(before + length, -1)
    grad_kv_all = jnp.concatenate([grad_keys_all, grad_values_all], axis=1)
    grad_kv_back = passed_along(grad_kv_all[:before].astype(LOW), "ctx", -1)
    grad_kv_back = jnp.pad(grad_kv_back, ((length - before, 0), (0, 0))).astype(F32)
    grad_kv_low = (grad_kv_all[before:] + grad_kv_back).astype(LOW)
    grad_qkv = jnp.concatenate([grad_query_low, grad_kv_low], axis=1)
    grad_normed_one = transposed_product(grad_qkv, qkv_full).astype(LOW)
    grad_normed_one = sent_scattered(ordered_blocks(grad_normed_one))
    qkv_sent = sent_to_core(normed_one, grad_qkv)
    qkv_arrived = over_cores(qkv_sent)
    grad_qkv_low = by_rows(chip_rows(normed_one, grad_qkv, qkv_arrived))
    qkv_share = share_rows(grad_qkv_low).astype(F32)

    _, pull_one = jax.vjp(rms, inputs, pre_attention_gain)
    grad_inputs_norm, grad_gain_one = pull_one(grad_normed_one)
    grad_inputs_low = by_chip((grad_middle + grad_inputs_norm).astype(LOW))
    grad_inputs = in_order(sent_gathered(grad_inputs_low))

    gains = by_chip(jnp.stack([grad_gain_one, grad_gain_two, grad_gain_three, grad_gain_four]))
    for axis in ("tp",) + ROWS:
        gains = summed(gains, axis)
    share = hidden_in.shape[1] // (lax.axis_size("fsdp") * lax.axis_size("ctx"))
    row_rank = lax.axis_index("fsdp") * lax.axis_size("ctx") + lax.axis_index("ctx")
    gain_shares = lax.dynamic_slice_in_dim(gains, row_rank * share, share, axis=1)
    edges = [0, heads_width, heads_width + kv_width, qkv_width]
    qkv_shares = [qkv_share[:, a:b] for a, b in zip(edges[:-1], edges[1:])]
    gate_up_share = gate_up_share.astype(F32)
    return (
        (outputs, grad_inputs)
        + tuple(gain_shares[i] for i in range(4))
        + tuple(qkv_shares)
        + (output_share.astype(F32), gate_up_share[:, :units], gate_up_share[:, units:], down_share.astype(F32))
    )


def solution(mesh):
    tokens = P(ROWS, None)
    weight = P(ROWS, "tp")
    return jax.shard_map(
        shards,
        mesh=mesh,
        in_specs=(tokens, tokens, P("fsdp")) + (P(),) * 4 + (weight,) * 7,
        out_specs=(tokens, tokens) + (P(ROWS),) * 4 + (weight,) * 7,
        check_vma=False,
    )
```

```python
import jax
import jax.numpy as jnp
from jax import lax
from jax.experimental.layout import Layout, with_layout_constraint
from jax.sharding import PartitionSpec as P


HD = 256
BLOCK_TOKENS = 128
MAX_DOC_BLOCKS = 4
CAP = 50.0
EPS = 1e-06
ROWS = ("fsdp", "ctx")
LOW = jnp.bfloat16
F32 = jnp.float32


def passed_along(block, axis, distance):
    devices = range(lax.axis_size(axis))
    route = [(i - distance, i) for i in devices if i - distance in devices]
    return lax.ppermute(block, axis, route)


def rms(value, gain):
    return value * lax.rsqrt(jnp.mean(value * value, axis=-1, keepdims=True) + EPS) * gain


def geglu(gate_value, up_value):
    return jax.nn.gelu(gate_value, approximate=True) * up_value


def product(left, right):
    return jnp.dot(left, right, preferred_element_type=F32)


def rows_product(left, right):
    return lax.dot_general(left, right, (((0,), (0,)), ((), ())), preferred_element_type=F32)


def transposed_product(left, right):
    return lax.dot_general(left, right, (((1,), (1,)), ((), ())), preferred_element_type=F32)


def onward(block, distance, senders):
    return lax.ppermute(block, "tp", [(i, i + distance) for i in senders])


def shift(block, distance):
    size = lax.axis_size("tp")
    return lax.ppermute(block, "tp", [(i, (i + distance) % size) for i in range(size)])


def distances(size):
    return sorted(range(1, size), key=lambda k: (abs(2 * k - size), k))


def sent_scattered(blocks):
    blocks = lax.optimization_barrier(tuple(blocks))
    arrived = [shift(blocks[k], -k) for k in distances(len(blocks))]
    total = blocks[0].astype(F32)
    for block in arrived:
        total = total + block.astype(F32)
    return total


def sent_gathered(block):
    size = lax.axis_size("tp")
    pieces = {k: shift(block, k) for k in distances(size)}
    return [block] + [pieces[k] for k in range(1, size)]


def scattered(blocks):
    size = lax.axis_size("tp")
    rising, falling = None, None
    for step in range(1, size):
        rise, fall = blocks[step], blocks[size - step]
        if rising is not None:
            rise = (rise.astype(F32) + rising.astype(F32)).astype(LOW)
            fall = (fall.astype(F32) + falling.astype(F32)).astype(LOW)
        rise, fall = lax.optimization_barrier((rise, fall))
        rising = onward(rise, 1, range(step))
        falling = onward(fall, -1, range(size - step, size))
    return blocks[0].astype(F32) + (rising.astype(F32) + falling.astype(F32))


def gathered(block):
    size = lax.axis_size("tp")
    rank = lax.axis_index("tp")
    rising, falling = [block], [block]
    for step in range(1, size):
        rise = onward(rising[-1], 1, range(step - 1, size - 1))
        fall = onward(falling[-1], -1, range(1, size - step + 1))
        rise, fall = lax.optimization_barrier((rise, fall))
        rising.append(rise)
        falling.append(fall)
    return [block] + [
        jnp.where(rank >= k, rising[k], falling[size - k]) for k in range(1, size)
    ]


def turned_blocks(partial):
    size = lax.axis_size("tp")
    blocks = partial.reshape(size, -1, partial.shape[-1])
    return [blocks[k] for k in range(size)]


def ordered_blocks(partial):
    size = lax.axis_size("tp")
    rank = lax.axis_index("tp")
    blocks = partial.reshape(size, -1, partial.shape[-1])
    return [
        lax.dynamic_index_in_dim(blocks, (rank - k) % size, 0, False) for k in range(size)
    ]


def in_order(pieces):
    size = lax.axis_size("tp")
    rank = lax.axis_index("tp")
    whole = jnp.zeros((size,) + pieces[0].shape, pieces[0].dtype)
    for k in range(size):
        whole = lax.dynamic_update_index_in_dim(whole, pieces[k], (rank - k) % size, 0)
    return whole.reshape(-1, pieces[0].shape[-1])


def exchanged(value):
    size = lax.axis_size("tp")
    rank = lax.axis_index("tp")
    width = value.shape[1] // size
    pieces = [value[:, k * width : (k + 1) * width] for k in range(size)]
    pieces = lax.optimization_barrier(tuple(pieces))
    whole = jnp.zeros((size,) + pieces[0].shape, value.dtype)
    whole = lax.dynamic_update_index_in_dim(whole, pieces[0], rank, 0)
    for k in distances(size):
        arrived = shift(pieces[k], -k)
        whole = lax.dynamic_update_index_in_dim(whole, arrived, (rank + k) % size, 0)
    return whole.reshape(-1, width)


def summed(value, axis):
    size = lax.axis_size(axis)
    bit = 1
    while bit < size:
        value = value + lax.ppermute(value, axis, [(i, i ^ bit) for i in range(size)])
        bit *= 2
    return value


def attention_scores(queries, keys_all, allowed, scaling):
    scores = (
        jnp.einsum("qgrd,kgd->grqk", queries, keys_all, preferred_element_type=F32) * scaling
    )
    capped = CAP * jnp.tanh(scores / CAP)
    powers = jnp.where(allowed[None, None], jnp.exp(capped), 0.0)
    return (scores, powers)


def by_rows(value):
    return with_layout_constraint(value, Layout(major_to_minor=(0, 1)))


def row_groups():
    width = lax.axis_size("ctx")
    ranks = range(lax.axis_size("fsdp") * width)
    return [[r for r in ranks if r // width % 2 == core] for core in range(2)]


def swapped(value, first, second):
    part = value.shape[-1] // (first * second)
    order = [i * second + j for j in range(second) for i in range(first)]
    return jnp.concatenate([value[..., k * part : (k + 1) * part] for k in order], axis=-1)


def by_core(value):
    return swapped(value, lax.axis_size("fsdp") // 2, 2)


def by_chip(value):
    return swapped(value, 2, lax.axis_size("fsdp") // 2)


def gather_rows(weight):
    first, second = row_groups()
    return lax.all_gather(
        weight, ROWS, axis=0, tiled=True, axis_index_groups=[first + second]
    )


def rows_of_core(left, core):
    half = left.shape[-1] // 2
    return lax.dynamic_slice_in_dim(left, core * half, half, axis=left.ndim - 1)


def sent_to_core(left, right):
    other = 1 - lax.axis_index("fsdp") % 2
    return rows_product(rows_of_core(left, other), right).astype(LOW)


def over_cores(block):
    return lax.ppermute(block, "fsdp", [(i, i ^ 1) for i in range(lax.axis_size("fsdp"))])


def chip_rows(left, right, arrived):
    own = rows_product(rows_of_core(left, lax.axis_index("fsdp") % 2), right)
    return (own + arrived.astype(F32)).astype(LOW)


def share_rows(grad):
    return lax.psum_scatter(
        grad, ROWS, scatter_dimension=0, tiled=True, axis_index_groups=row_groups()
    )


def shards(
    hidden_in,
    cotangent,
    segment_ids,
    pre_attention_gain,
    post_attention_gain,
    pre_feedforward_gain,
    post_feedforward_gain,
    query_weight,
    key_weight,
    value_weight,
    output_weight,
    gate_weight,
    up_weight,
    down_weight,
):
    length = hidden_in.shape[0]
    heads_width = query_weight.shape[1]
    kv_width = key_weight.shape[1]
    kv_heads = kv_width // HD
    repeats = heads_width // kv_width
    units = gate_weight.shape[1]
    qkv_width = heads_width + 2 * kv_width
    scaling = HD ** (-0.5)
    tp_size = lax.axis_size("tp")
    piece = length // tp_size

    attention_full = gather_rows(
        jnp.concatenate([query_weight, key_weight, value_weight, output_weight], axis=1)
    )
    qkv_full = attention_full[:, :qkv_width]
    output_full = attention_full[:, qkv_width:]
    units_full = gather_rows(jnp.concatenate([gate_weight, up_weight, down_weight], axis=1))
    gate_up_full = units_full[:, : 2 * units]
    down_full = units_full[:, 2 * units :]
    output_pieces = jnp.concatenate(sent_gathered(output_weight), axis=1)
    output_all = gather_rows(output_pieces)

    position = lax.axis_index("ctx")
    own_ids = lax.dynamic_slice_in_dim(segment_ids, position * length, length)
    before = min(length, (MAX_DOC_BLOCKS - 1) * BLOCK_TOKENS)
    prev_start = jnp.maximum(position * length - before, 0)
    prev_ids = jnp.where(
        position > 0, lax.dynamic_slice_in_dim(segment_ids, prev_start, before), -2
    )
    key_ids = jnp.concatenate([prev_ids, own_ids])
    query_pos = jnp.arange(length, dtype=jnp.int32)
    key_pos = jnp.arange(before + length, dtype=jnp.int32) - before
    allowed = (query_pos[:, None] == key_pos[None, :]) | (own_ids[:, None] == key_ids[None, :]) & (
        own_ids[:, None] >= 0
    ) & (key_pos[None, :] < query_pos[:, None])

    pre_attention_gain, post_attention_gain, pre_feedforward_gain, post_feedforward_gain = (
        by_core(gain)
        for gain in (
            pre_attention_gain,
            post_attention_gain,
            pre_feedforward_gain,
            post_feedforward_gain,
        )
    )
    hidden_in = by_core(hidden_in)
    normed_one = rms(hidden_in.astype(F32), pre_attention_gain).astype(LOW)
    inputs_turned = jnp.concatenate(ordered_blocks(hidden_in), axis=0)
    upstream_turned = by_core(jnp.concatenate(ordered_blocks(cotangent), axis=0))
    inputs = inputs_turned[:piece].astype(F32)
    upstream = upstream_turned[:piece].astype(F32)

    qkv_low = product(normed_one, qkv_full).astype(LOW)
    queries = qkv_low[:, :heads_width].reshape(length, kv_heads, repeats, HD)
    kv_low = qkv_low[:, heads_width:]
    kv_all = jnp.concatenate([passed_along(kv_low[-before:], "ctx", 1), kv_low], axis=0)
    keys_all = kv_all[:, :kv_width].reshape(before + length, kv_heads, HD)
    values_all = kv_all[:, kv_width:].reshape(before + length, kv_heads, HD)
    scores, powers = attention_scores(queries, keys_all, allowed, scaling)
    totals = jnp.sum(powers, axis=-1, keepdims=True)
    probs_low = (powers / totals).astype(LOW)
    attended = jnp.einsum("grqk,kgd->qgrd", probs_low, values_all, preferred_element_type=F32)
    attended_low = attended.reshape(length, -1).astype(LOW)

    branch_one = scattered(
        ordered_blocks(transposed_product(attended_low, output_full).astype(LOW))
    )
    branch_one_low = jnp.concatenate(gathered(branch_one.astype(LOW)), axis=0).astype(F32)
    middle_turned = inputs_turned.astype(F32) + rms(branch_one_low, post_attention_gain)
    middle = middle_turned[:piece]
    normed_two = rms(middle_turned, pre_feedforward_gain).astype(LOW)

    gate_up = product(normed_two, gate_up_full)
    gate_value = gate_up[:, :units]
    up_value = gate_up[:, units:]
    hidden_low = geglu(gate_value, up_value).astype(LOW)
    branch_two = scattered(
        turned_blocks(transposed_product(hidden_low, down_full).astype(LOW))
    )
    branch_two_low = jnp.concatenate(gathered(branch_two.astype(LOW)), axis=0).astype(F32)
    unused_four, pull_four = jax.vjp(rms, branch_two_low, post_feedforward_gain)
    grad_two_low = pull_four(upstream_turned.astype(F32))[0].astype(LOW)
    unused_four, pull_four = jax.vjp(rms, branch_two, post_feedforward_gain)
    grad_gain_four = pull_four(upstream)[1]

    down_sent, grad_two_low = lax.optimization_barrier(
        (sent_to_core(grad_two_low, hidden_low), grad_two_low)
    )
    down_arrived = over_cores(down_sent)
    _, pull_glu = jax.vjp(geglu, gate_value, up_value)
    grad_gate, grad_up = pull_glu(product(grad_two_low, down_full))
    grad_gate_up = jnp.concatenate([grad_gate.astype(LOW), grad_up.astype(LOW)], axis=1)
    grad_normed_two = transposed_product(grad_gate_up, gate_up_full).astype(LOW)
    grad_normed_two = sent_scattered(turned_blocks(grad_normed_two))
    result = (middle_turned + rms(branch_two_low, post_feedforward_gain)).astype(LOW)
    outputs = in_order(turned_blocks(by_chip(result)))
    grad_down_low = chip_rows(grad_two_low, hidden_low, down_arrived)
    down_share = share_rows(grad_down_low)
    gate_up_sent = sent_to_core(normed_two, grad_gate_up)
    gate_up_arrived = over_cores(gate_up_sent)
    grad_gate_up_low = chip_rows(normed_two, grad_gate_up, gate_up_arrived)
    gate_up_share = share_rows(grad_gate_up_low)

    _, pull_three = jax.vjp(rms, middle, pre_feedforward_gain)
    grad_middle_norm, grad_gain_three = pull_three(grad_normed_two)
    grad_middle = upstream + grad_middle_norm
    _, pull_two = jax.vjp(rms, branch_one, post_attention_gain)
    grad_branch_one, grad_gain_two = pull_two(grad_middle)
    grad_one_own = grad_branch_one.astype(LOW)
    grad_attended = product(grad_one_own, output_all).astype(LOW)
    grad_attended, grad_one_own = lax.optimization_barrier(
        (exchanged(grad_attended), grad_one_own)
    )
    grad_attended = grad_attended.reshape(length, kv_heads, repeats, HD)
    grad_one_low = in_order(sent_gathered(grad_one_own))
    output_sent = sent_to_core(grad_one_low, attended_low)
    output_arrived = over_cores(output_sent)
    grad_output_low = chip_rows(grad_one_low, attended_low, output_arrived)
    probs = powers / totals
    grad_probs = jnp.einsum(
        "qgrd,kgd->grqk", grad_attended, values_all, preferred_element_type=F32
    )
    inner = jnp.sum(probs * grad_probs, axis=-1, keepdims=True)
    grad_capped = probs * (grad_probs - inner)
    squashed = jnp.tanh(scores / CAP)
    grad_scores = (grad_capped * (1.0 - squashed * squashed)).astype(LOW)
    grad_query_low = (
        (
            jnp.einsum("grqk,kgd->qgrd", grad_scores, keys_all, preferred_element_type=F32)
            * scaling
        )
        .reshape(length, -1)
        .astype(LOW)
    )
    grad_keys_all = (
        jnp.einsum("grqk,qgrd->kgd", grad_scores, queries, preferred_element_type=F32) * scaling
    ).reshape(before + length, -1)
    grad_values_all = jnp.einsum(
        "grqk,qgrd->kgd", probs_low, grad_attended, preferred_element_type=F32
    ).reshape(before + length, -1)
    grad_kv_all = jnp.concatenate([grad_keys_all, grad_values_all], axis=1)
    grad_kv_back = passed_along(grad_kv_all[:before].astype(LOW), "ctx", -1)
    grad_kv_back = jnp.pad(grad_kv_back, ((length - before, 0), (0, 0))).astype(F32)
    grad_kv_low = (grad_kv_all[before:] + grad_kv_back).astype(LOW)
    grad_qkv = jnp.concatenate([grad_query_low, grad_kv_low], axis=1)
    grad_normed_one = transposed_product(grad_qkv, qkv_full).astype(LOW)
    grad_normed_one = sent_scattered(ordered_blocks(grad_normed_one))
    qkv_sent = sent_to_core(normed_one, grad_qkv)
    qkv_arrived = over_cores(qkv_sent)
    grad_qkv_low = chip_rows(normed_one, grad_qkv, qkv_arrived)
    grad_attention = by_rows(jnp.concatenate([grad_qkv_low, grad_output_low], axis=1))
    attention_share = share_rows(grad_attention).astype(F32)

    _, pull_one = jax.vjp(rms, inputs, pre_attention_gain)
    grad_inputs_norm, grad_gain_one = pull_one(grad_normed_one)
    grad_inputs_low = by_chip((grad_middle + grad_inputs_norm).astype(LOW))
    grad_inputs = in_order(sent_gathered(grad_inputs_low))

    gains = by_chip(jnp.stack([grad_gain_one, grad_gain_two, grad_gain_three, grad_gain_four]))
    for axis in ("tp",) + ROWS:
        gains = summed(gains, axis)
    share = hidden_in.shape[1] // (lax.axis_size("fsdp") * lax.axis_size("ctx"))
    row_rank = lax.axis_index("fsdp") * lax.axis_size("ctx") + lax.axis_index("ctx")
    gain_shares = lax.dynamic_slice_in_dim(gains, row_rank * share, share, axis=1)
    edges = [0, heads_width, heads_width + kv_width, qkv_width, qkv_width + heads_width]
    attention_shares = [attention_share[:, a:b] for a, b in zip(edges[:-1], edges[1:])]
    gate_up_share = gate_up_share.astype(F32)
    return (
        (outputs, grad_inputs)
        + tuple(gain_shares[i] for i in range(4))
        + tuple(attention_shares)
        + (gate_up_share[:, :units], gate_up_share[:, units:], down_share.astype(F32))
    )


def solution(mesh):
    tokens = P(ROWS, None)
    weight = P(ROWS, "tp")
    return jax.shard_map(
        shards,
        mesh=mesh,
        in_specs=(tokens, tokens, P("fsdp")) + (P(),) * 4 + (weight,) * 7,
        out_specs=(tokens, tokens) + (P(ROWS),) * 4 + (weight,) * 7,
        check_vma=False,
    )
```

```python
import jax
import jax.numpy as jnp
from jax import lax
from jax.experimental.layout import Layout, with_layout_constraint
from jax.sharding import PartitionSpec as P


HD = 256
BLOCK_TOKENS = 128
MAX_DOC_BLOCKS = 4
CAP = 50.0
EPS = 1e-06
ROWS = ("fsdp", "ctx")
LOW = jnp.bfloat16
F32 = jnp.float32


def passed_along(block, axis, distance):
    devices = range(lax.axis_size(axis))
    route = [(i - distance, i) for i in devices if i - distance in devices]
    return lax.ppermute(block, axis, route)


def rms(value, gain):
    return value * lax.rsqrt(jnp.mean(value * value, axis=-1, keepdims=True) + EPS) * gain


def geglu(gate_value, up_value):
    return jax.nn.gelu(gate_value, approximate=True) * up_value


def product(left, right):
    return jnp.dot(left, right, preferred_element_type=F32)


def rows_product(left, right):
    return lax.dot_general(left, right, (((0,), (0,)), ((), ())), preferred_element_type=F32)


def transposed_product(left, right):
    return lax.dot_general(left, right, (((1,), (1,)), ((), ())), preferred_element_type=F32)


def onward(block, distance, senders):
    return lax.ppermute(block, "tp", [(i, i + distance) for i in senders])


def shift(block, distance):
    size = lax.axis_size("tp")
    return lax.ppermute(block, "tp", [(i, (i + distance) % size) for i in range(size)])


def distances(size):
    return sorted(range(1, size), key=lambda k: (abs(2 * k - size), k))


def sent_scattered(blocks):
    blocks = lax.optimization_barrier(tuple(blocks))
    arrived = [shift(blocks[k], -k) for k in distances(len(blocks))]
    total = blocks[0].astype(F32)
    for block in arrived:
        total = total + block.astype(F32)
    return total


def sent_gathered(block):
    size = lax.axis_size("tp")
    pieces = {k: shift(block, k) for k in distances(size)}
    return [block] + [pieces[k] for k in range(1, size)]


def scattered(blocks):
    size = lax.axis_size("tp")
    rising, falling = None, None
    for step in range(1, size):
        rise, fall = blocks[step], blocks[size - step]
        if rising is not None:
            rise = (rise.astype(F32) + rising.astype(F32)).astype(LOW)
            fall = (fall.astype(F32) + falling.astype(F32)).astype(LOW)
        rise, fall = lax.optimization_barrier((rise, fall))
        rising = onward(rise, 1, range(step))
        falling = onward(fall, -1, range(size - step, size))
    return blocks[0].astype(F32) + (rising.astype(F32) + falling.astype(F32))


def gathered(block):
    size = lax.axis_size("tp")
    rank = lax.axis_index("tp")
    rising, falling = [block], [block]
    for step in range(1, size):
        rise = onward(rising[-1], 1, range(step - 1, size - 1))
        fall = onward(falling[-1], -1, range(1, size - step + 1))
        rise, fall = lax.optimization_barrier((rise, fall))
        rising.append(rise)
        falling.append(fall)
    return [block] + [
        jnp.where(rank >= k, rising[k], falling[size - k]) for k in range(1, size)
    ]


def ordered_blocks(partial):
    size = lax.axis_size("tp")
    rank = lax.axis_index("tp")
    blocks = partial.reshape(size, -1, partial.shape[-1])
    return [
        lax.dynamic_index_in_dim(blocks, (rank - k) % size, 0, False) for k in range(size)
    ]


def in_order(pieces):
    size = lax.axis_size("tp")
    rank = lax.axis_index("tp")
    whole = jnp.zeros((size,) + pieces[0].shape, pieces[0].dtype)
    for k in range(size):
        whole = lax.dynamic_update_index_in_dim(whole, pieces[k], (rank - k) % size, 0)
    return whole.reshape(-1, pieces[0].shape[-1])


def exchanged(value):
    size = lax.axis_size("tp")
    rank = lax.axis_index("tp")
    width = value.shape[1] // size
    pieces = [value[:, k * width : (k + 1) * width] for k in range(size)]
    pieces = lax.optimization_barrier(tuple(pieces))
    whole = jnp.zeros((size,) + pieces[0].shape, value.dtype)
    whole = lax.dynamic_update_index_in_dim(whole, pieces[0], rank, 0)
    for k in distances(size):
        arrived = shift(pieces[k], -k)
        whole = lax.dynamic_update_index_in_dim(whole, arrived, (rank + k) % size, 0)
    return whole.reshape(-1, width)


def summed(value, axis):
    size = lax.axis_size(axis)
    bit = 1
    while bit < size:
        value = value + lax.ppermute(value, axis, [(i, i ^ bit) for i in range(size)])
        bit *= 2
    return value


def attention_scores(queries, keys_all, allowed, scaling):
    scores = (
        jnp.einsum("qgrd,kgd->grqk", queries, keys_all, preferred_element_type=F32) * scaling
    )
    capped = CAP * jnp.tanh(scores / CAP)
    powers = jnp.where(allowed[None, None], jnp.exp(capped), 0.0)
    return (scores, powers)


def by_rows(value):
    return with_layout_constraint(value, Layout(major_to_minor=(0, 1)))


def row_groups():
    width = lax.axis_size("ctx")
    ranks = range(lax.axis_size("fsdp") * width)
    return [[r for r in ranks if r // width % 2 == core] for core in range(2)]


def swapped(value, first, second):
    part = value.shape[-1] // (first * second)
    order = [i * second + j for j in range(second) for i in range(first)]
    return jnp.concatenate([value[..., k * part : (k + 1) * part] for k in order], axis=-1)


def by_core(value):
    return swapped(value, lax.axis_size("fsdp") // 2, 2)


def by_chip(value):
    return swapped(value, 2, lax.axis_size("fsdp") // 2)


def gather_rows(weight):
    first, second = row_groups()
    return lax.all_gather(
        weight, ROWS, axis=0, tiled=True, axis_index_groups=[first + second]
    )


def rows_of_core(left, core):
    half = left.shape[-1] // 2
    return lax.dynamic_slice_in_dim(left, core * half, half, axis=left.ndim - 1)


def sent_to_core(left, right):
    other = 1 - lax.axis_index("fsdp") % 2
    return rows_product(rows_of_core(left, other), right).astype(LOW)


def over_cores(block):
    return lax.ppermute(block, "fsdp", [(i, i ^ 1) for i in range(lax.axis_size("fsdp"))])


def chip_rows(left, right, arrived):
    own = rows_product(rows_of_core(left, lax.axis_index("fsdp") % 2), right)
    return (own + arrived.astype(F32)).astype(LOW)


def share_rows(grad):
    return lax.psum_scatter(
        grad, ROWS, scatter_dimension=0, tiled=True, axis_index_groups=row_groups()
    )


def shards(
    hidden_in,
    cotangent,
    segment_ids,
    pre_attention_gain,
    post_attention_gain,
    pre_feedforward_gain,
    post_feedforward_gain,
    query_weight,
    key_weight,
    value_weight,
    output_weight,
    gate_weight,
    up_weight,
    down_weight,
):
    length = hidden_in.shape[0]
    heads_width = query_weight.shape[1]
    kv_width = key_weight.shape[1]
    kv_heads = kv_width // HD
    repeats = heads_width // kv_width
    units = gate_weight.shape[1]
    qkv_width = heads_width + 2 * kv_width
    scaling = HD ** (-0.5)
    tp_size = lax.axis_size("tp")
    tp_rank = lax.axis_index("tp")
    piece = length // tp_size

    attention_full = gather_rows(
        jnp.concatenate([query_weight, key_weight, value_weight, output_weight], axis=1)
    )
    qkv_full = attention_full[:, :qkv_width]
    output_full = attention_full[:, qkv_width:]
    units_full = gather_rows(jnp.concatenate([gate_weight, up_weight, down_weight], axis=1))
    gate_up_full = units_full[:, : 2 * units]
    down_full = units_full[:, 2 * units :]
    output_pieces = jnp.concatenate(sent_gathered(output_weight), axis=1)
    output_all = gather_rows(output_pieces)

    position = lax.axis_index("ctx")
    own_ids = lax.dynamic_slice_in_dim(segment_ids, position * length, length)
    before = min(length, (MAX_DOC_BLOCKS - 1) * BLOCK_TOKENS)
    prev_start = jnp.maximum(position * length - before, 0)
    prev_ids = jnp.where(
        position > 0, lax.dynamic_slice_in_dim(segment_ids, prev_start, before), -2
    )
    key_ids = jnp.concatenate([prev_ids, own_ids])
    query_pos = jnp.arange(length, dtype=jnp.int32)
    key_pos = jnp.arange(before + length, dtype=jnp.int32) - before
    allowed = (query_pos[:, None] == key_pos[None, :]) | (own_ids[:, None] == key_ids[None, :]) & (
        own_ids[:, None] >= 0
    ) & (key_pos[None, :] < query_pos[:, None])

    pre_attention_gain, post_attention_gain, pre_feedforward_gain, post_feedforward_gain = (
        by_core(gain)
        for gain in (
            pre_attention_gain,
            post_attention_gain,
            pre_feedforward_gain,
            post_feedforward_gain,
        )
    )
    hidden_in = by_core(hidden_in)
    normed_one = rms(hidden_in.astype(F32), pre_attention_gain).astype(LOW)
    upstream_all = by_core(cotangent)
    inputs = lax.dynamic_slice_in_dim(hidden_in, tp_rank * piece, piece).astype(F32)
    upstream = lax.dynamic_slice_in_dim(upstream_all, tp_rank * piece, piece).astype(F32)

    qkv_low = product(normed_one, qkv_full).astype(LOW)
    queries = qkv_low[:, :heads_width].reshape(length, kv_heads, repeats, HD)
    kv_low = qkv_low[:, heads_width:]
    kv_all = jnp.concatenate([passed_along(kv_low[-before:], "ctx", 1), kv_low], axis=0)
    keys_all = kv_all[:, :kv_width].reshape(before + length, kv_heads, HD)
    values_all = kv_all[:, kv_width:].reshape(before + length, kv_heads, HD)
    scores, powers = attention_scores(queries, keys_all, allowed, scaling)
    totals = jnp.sum(powers, axis=-1, keepdims=True)
    probs_low = (powers / totals).astype(LOW)
    attended = jnp.einsum("grqk,kgd->qgrd", probs_low, values_all, preferred_element_type=F32)
    attended_low = attended.reshape(length, -1).astype(LOW)

    branch_one = scattered(
        ordered_blocks(transposed_product(attended_low, output_full).astype(LOW))
    )
    branch_one_all = in_order(gathered(branch_one.astype(LOW))).astype(F32)
    middle_all = hidden_in.astype(F32) + rms(branch_one_all, post_attention_gain)
    middle = lax.dynamic_slice_in_dim(middle_all, tp_rank * piece, piece)
    normed_two = rms(middle_all, pre_feedforward_gain).astype(LOW)

    gate_up = product(normed_two, gate_up_full)
    gate_value = gate_up[:, :units]
    up_value = gate_up[:, units:]
    hidden_low = geglu(gate_value, up_value).astype(LOW)
    branch_two = lax.psum(transposed_product(hidden_low, down_full).astype(LOW), "tp")
    branch_two = branch_two.astype(F32)
    _, pull_four = jax.vjp(rms, branch_two, post_feedforward_gain)
    grad_branch_two, grad_gain_four = pull_four(upstream_all.astype(F32))
    grad_gain_four = grad_gain_four / tp_size
    grad_two_low = grad_branch_two.astype(LOW)

    down_sent, grad_two_low = lax.optimization_barrier(
        (sent_to_core(grad_two_low, hidden_low), grad_two_low)
    )
    down_arrived = over_cores(down_sent)
    _, pull_glu = jax.vjp(geglu, gate_value, up_value)
    grad_gate, grad_up = pull_glu(product(grad_two_low, down_full))
    grad_gate_up = jnp.concatenate([grad_gate.astype(LOW), grad_up.astype(LOW)], axis=1)
    grad_normed_two = transposed_product(grad_gate_up, gate_up_full).astype(LOW)
    grad_normed_two = sent_scattered(ordered_blocks(grad_normed_two))
    outputs = by_chip((middle_all + rms(branch_two, post_feedforward_gain)).astype(LOW))
    grad_down_low = chip_rows(grad_two_low, hidden_low, down_arrived)
    down_share = share_rows(grad_down_low)
    gate_up_sent = sent_to_core(normed_two, grad_gate_up)
    gate_up_arrived = over_cores(gate_up_sent)
    grad_gate_up_low = chip_rows(normed_two, grad_gate_up, gate_up_arrived)
    gate_up_share = share_rows(grad_gate_up_low)

    _, pull_three = jax.vjp(rms, middle, pre_feedforward_gain)
    grad_middle_norm, grad_gain_three = pull_three(grad_normed_two)
    grad_middle = upstream + grad_middle_norm
    _, pull_two = jax.vjp(rms, branch_one, post_attention_gain)
    grad_branch_one, grad_gain_two = pull_two(grad_middle)
    grad_one_own = grad_branch_one.astype(LOW)
    grad_attended = product(grad_one_own, output_all).astype(LOW)
    grad_attended, grad_one_own = lax.optimization_barrier(
        (exchanged(grad_attended), grad_one_own)
    )
    grad_attended = grad_attended.reshape(length, kv_heads, repeats, HD)
    grad_one_low = in_order(sent_gathered(grad_one_own))
    output_sent = sent_to_core(grad_one_low, attended_low)
    output_arrived = over_cores(output_sent)
    grad_output_low = chip_rows(grad_one_low, attended_low, output_arrived)
    probs = powers / totals
    grad_probs = jnp.einsum(
        "qgrd,kgd->grqk", grad_attended, values_all, preferred_element_type=F32
    )
    inner = jnp.sum(probs * grad_probs, axis=-1, keepdims=True)
    grad_capped = probs * (grad_probs - inner)
    squashed = jnp.tanh(scores / CAP)
    grad_scores = (grad_capped * (1.0 - squashed * squashed)).astype(LOW)
    grad_query_low = (
        (
            jnp.einsum("grqk,kgd->qgrd", grad_scores, keys_all, preferred_element_type=F32)
            * scaling
        )
        .reshape(length, -1)
        .astype(LOW)
    )
    grad_keys_all = (
        jnp.einsum("grqk,qgrd->kgd", grad_scores, queries, preferred_element_type=F32) * scaling
    ).reshape(before + length, -1)
    grad_values_all = jnp.einsum(
        "grqk,qgrd->kgd", probs_low, grad_attended, preferred_element_type=F32
    ).reshape(before + length, -1)
    grad_kv_all = jnp.concatenate([grad_keys_all, grad_values_all], axis=1)
    grad_kv_back = passed_along(grad_kv_all[:before].astype(LOW), "ctx", -1)
    grad_kv_back = jnp.pad(grad_kv_back, ((length - before, 0), (0, 0))).astype(F32)
    grad_kv_low = (grad_kv_all[before:] + grad_kv_back).astype(LOW)
    grad_qkv = jnp.concatenate([grad_query_low, grad_kv_low], axis=1)
    grad_normed_one = transposed_product(grad_qkv, qkv_full).astype(LOW)
    unused_one, pull_one = jax.vjp(rms, hidden_in.astype(F32), pre_attention_gain)
    grad_gain_one = pull_one(grad_normed_one.astype(F32))[1]
    gains = by_chip(jnp.stack([grad_gain_one, grad_gain_two, grad_gain_three, grad_gain_four]))
    for axis in ROWS:
        gains = summed(gains, axis)
    gains = sum((shift(gains, k) for k in range(1, tp_size)), gains)
    grad_normed_one = sent_scattered(ordered_blocks(grad_normed_one))
    qkv_sent = sent_to_core(normed_one, grad_qkv)
    qkv_arrived = over_cores(qkv_sent)
    grad_qkv_low = chip_rows(normed_one, grad_qkv, qkv_arrived)
    grad_attention = by_rows(jnp.concatenate([grad_qkv_low, grad_output_low], axis=1))
    attention_share = share_rows(grad_attention).astype(F32)

    unused_one, pull_one = jax.vjp(rms, inputs, pre_attention_gain)
    grad_inputs_low = by_chip((grad_middle + pull_one(grad_normed_one)[0]).astype(LOW))
    grad_inputs = in_order(sent_gathered(grad_inputs_low))

    share = hidden_in.shape[1] // (lax.axis_size("fsdp") * lax.axis_size("ctx"))
    row_rank = lax.axis_index("fsdp") * lax.axis_size("ctx") + lax.axis_index("ctx")
    gain_shares = lax.dynamic_slice_in_dim(gains, row_rank * share, share, axis=1)
    edges = [0, heads_width, heads_width + kv_width, qkv_width, qkv_width + heads_width]
    attention_shares = [attention_share[:, a:b] for a, b in zip(edges[:-1], edges[1:])]
    gate_up_share = gate_up_share.astype(F32)
    return (
        (outputs, grad_inputs)
        + tuple(gain_shares[i] for i in range(4))
        + tuple(attention_shares)
        + (gate_up_share[:, :units], gate_up_share[:, units:], down_share.astype(F32))
    )


def solution(mesh):
    tokens = P(ROWS, None)
    weight = P(ROWS, "tp")
    return jax.shard_map(
        shards,
        mesh=mesh,
        in_specs=(tokens, tokens, P("fsdp")) + (P(),) * 4 + (weight,) * 7,
        out_specs=(tokens, tokens) + (P(ROWS),) * 4 + (weight,) * 7,
        check_vma=False,
    )
```

```python
import jax
import jax.numpy as jnp
from jax import lax
from jax.experimental.layout import Layout, with_layout_constraint
from jax.sharding import PartitionSpec as P


HD = 256
BLOCK_TOKENS = 128
MAX_DOC_BLOCKS = 4
CAP = 50.0
EPS = 1e-06
ROWS = ("fsdp", "ctx")
LOW = jnp.bfloat16
F32 = jnp.float32


def passed_along(block, axis, distance):
    devices = range(lax.axis_size(axis))
    route = [(i - distance, i) for i in devices if i - distance in devices]
    return lax.ppermute(block, axis, route)


def rms(value, gain):
    return value * lax.rsqrt(jnp.mean(value * value, axis=-1, keepdims=True) + EPS) * gain


def geglu(gate_value, up_value):
    return jax.nn.gelu(gate_value, approximate=True) * up_value


def product(left, right):
    return jnp.dot(left, right, preferred_element_type=F32)


def rows_product(left, right):
    return lax.dot_general(left, right, (((0,), (0,)), ((), ())), preferred_element_type=F32)


def transposed_product(left, right):
    return lax.dot_general(left, right, (((1,), (1,)), ((), ())), preferred_element_type=F32)


def onward(block, distance, senders):
    return lax.ppermute(block, "tp", [(i, i + distance) for i in senders])


def returned(grads, length):
    before = grads.shape[0] - length
    back = passed_along(grads[:before].astype(LOW), "ctx", -1)
    back = jnp.pad(back, ((length - before, 0), (0, 0))).astype(F32)
    return (grads[before:] + back).astype(LOW)


def shift(block, distance):
    size = lax.axis_size("tp")
    return lax.ppermute(block, "tp", [(i, (i + distance) % size) for i in range(size)])


def distances(size):
    return sorted(range(1, size), key=lambda k: (abs(2 * k - size), k))


def sent_scattered(blocks):
    blocks = lax.optimization_barrier(tuple(blocks))
    arrived = [shift(blocks[k], -k) for k in distances(len(blocks))]
    total = blocks[0].astype(F32)
    for block in arrived:
        total = total + block.astype(F32)
    return total


def sent_gathered(block):
    size = lax.axis_size("tp")
    pieces = {k: shift(block, k) for k in distances(size)}
    return [block] + [pieces[k] for k in range(1, size)]


def scattered(blocks):
    size = lax.axis_size("tp")
    rising, falling = None, None
    for step in range(1, size):
        rise, fall = blocks[step], blocks[size - step]
        if rising is not None:
            rise = (rise.astype(F32) + rising.astype(F32)).astype(LOW)
            fall = (fall.astype(F32) + falling.astype(F32)).astype(LOW)
        rise, fall = lax.optimization_barrier((rise, fall))
        rising = onward(rise, 1, range(step))
        falling = onward(fall, -1, range(size - step, size))
    return blocks[0].astype(F32) + (rising.astype(F32) + falling.astype(F32))


def gathered(block):
    size = lax.axis_size("tp")
    rank = lax.axis_index("tp")
    rising, falling = [block], [block]
    for step in range(1, size):
        rise = onward(rising[-1], 1, range(step - 1, size - 1))
        fall = onward(falling[-1], -1, range(1, size - step + 1))
        rise, fall = lax.optimization_barrier((rise, fall))
        rising.append(rise)
        falling.append(fall)
    return [block] + [
        jnp.where(rank >= k, rising[k], falling[size - k]) for k in range(1, size)
    ]


def ordered_blocks(partial):
    size = lax.axis_size("tp")
    rank = lax.axis_index("tp")
    blocks = partial.reshape(size, -1, partial.shape[-1])
    return [
        lax.dynamic_index_in_dim(blocks, (rank - k) % size, 0, False) for k in range(size)
    ]


def in_order(pieces):
    size = lax.axis_size("tp")
    rank = lax.axis_index("tp")
    whole = jnp.zeros((size,) + pieces[0].shape, pieces[0].dtype)
    for k in range(size):
        whole = lax.dynamic_update_index_in_dim(whole, pieces[k], (rank - k) % size, 0)
    return whole.reshape(-1, pieces[0].shape[-1])


def exchanged(value):
    size = lax.axis_size("tp")
    rank = lax.axis_index("tp")
    width = value.shape[1] // size
    pieces = [value[:, k * width : (k + 1) * width] for k in range(size)]
    pieces = lax.optimization_barrier(tuple(pieces))
    whole = jnp.zeros((size,) + pieces[0].shape, value.dtype)
    whole = lax.dynamic_update_index_in_dim(whole, pieces[0], rank, 0)
    for k in distances(size):
        arrived = shift(pieces[k], -k)
        whole = lax.dynamic_update_index_in_dim(whole, arrived, (rank + k) % size, 0)
    return whole.reshape(-1, width)


def summed(value, axis):
    size = lax.axis_size(axis)
    bit = 1
    while bit < size:
        value = value + lax.ppermute(value, axis, [(i, i ^ bit) for i in range(size)])
        bit *= 2
    return value


def attention_scores(queries, keys_all, allowed, scaling):
    scores = (
        jnp.einsum("qgrd,kgd->grqk", queries, keys_all, preferred_element_type=F32) * scaling
    )
    capped = CAP * jnp.tanh(scores / CAP)
    powers = jnp.where(allowed[None, None], jnp.exp(capped), 0.0)
    return (scores, powers)


def by_rows(value):
    return with_layout_constraint(value, Layout(major_to_minor=(0, 1)))


def row_groups():
    width = lax.axis_size("ctx")
    ranks = range(lax.axis_size("fsdp") * width)
    return [[r for r in ranks if r // width % 2 == core] for core in range(2)]


def swapped(value, first, second):
    part = value.shape[-1] // (first * second)
    order = [i * second + j for j in range(second) for i in range(first)]
    return jnp.concatenate([value[..., k * part : (k + 1) * part] for k in order], axis=-1)


def by_core(value):
    return swapped(value, lax.axis_size("fsdp") // 2, 2)


def by_chip(value):
    return swapped(value, 2, lax.axis_size("fsdp") // 2)


def gather_rows(weight):
    first, second = row_groups()
    return lax.all_gather(
        weight, ROWS, axis=0, tiled=True, axis_index_groups=[first + second]
    )


def sent_rows(weight):
    ranks = lax.axis_size("fsdp") * lax.axis_size("ctx")
    if (lax.axis_size("fsdp"), lax.axis_size("ctx")) != (4, 2):
        return gather_rows(weight)
    core, pair, width = 2, 4, 1

    def sent(block, bits):
        return lax.ppermute(block, ROWS, [(r, r ^ bits) for r in range(ranks)])

    held = {0: weight}
    for bits in (pair | width, width, pair):
        held[bits] = sent(weight, bits)
    for bits in (0, width, pair, pair | width):
        held[bits | core] = sent(held[bits], core)
    place = {0: 0, width: 1, pair: 2, core: 4}
    rank = lax.axis_index("fsdp") * 2 + lax.axis_index("ctx")
    own = (rank // core) % 2 * 4 + rank // pair * 2 + rank % 2
    whole = jnp.zeros((ranks,) + weight.shape, weight.dtype)
    for bits in held:
        at = own ^ (place[bits & width] | place[bits & pair] | place[bits & core])
        whole = lax.dynamic_update_index_in_dim(whole, held[bits], at, 0)
    return whole.reshape(-1, weight.shape[1])


def rows_of_core(left, core):
    half = left.shape[-1] // 2
    return lax.dynamic_slice_in_dim(left, core * half, half, axis=left.ndim - 1)


def sent_to_core(left, right):
    other = 1 - lax.axis_index("fsdp") % 2
    return rows_product(rows_of_core(left, other), right).astype(LOW)


def over_cores(block):
    return lax.ppermute(block, "fsdp", [(i, i ^ 1) for i in range(lax.axis_size("fsdp"))])


def chip_rows(left, right, arrived):
    own = rows_product(rows_of_core(left, lax.axis_index("fsdp") % 2), right)
    return (own + arrived.astype(F32)).astype(LOW)


def share_rows(grad):
    return lax.psum_scatter(
        grad, ROWS, scatter_dimension=0, tiled=True, axis_index_groups=row_groups()
    )


def shards(
    hidden_in,
    cotangent,
    segment_ids,
    pre_attention_gain,
    post_attention_gain,
    pre_feedforward_gain,
    post_feedforward_gain,
    query_weight,
    key_weight,
    value_weight,
    output_weight,
    gate_weight,
    up_weight,
    down_weight,
):
    length = hidden_in.shape[0]
    heads_width = query_weight.shape[1]
    kv_width = key_weight.shape[1]
    kv_heads = kv_width // HD
    repeats = heads_width // kv_width
    units = gate_weight.shape[1]
    qkv_width = heads_width + 2 * kv_width
    scaling = HD ** (-0.5)
    tp_size = lax.axis_size("tp")
    tp_rank = lax.axis_index("tp")
    piece = length // tp_size

    attention_full = gather_rows(
        jnp.concatenate([query_weight, key_weight, value_weight, output_weight], axis=1)
    )
    qkv_full = attention_full[:, :qkv_width]
    output_full = attention_full[:, qkv_width:]
    units_full = gather_rows(jnp.concatenate([gate_weight, up_weight, down_weight], axis=1))
    gate_up_full = units_full[:, : 2 * units]
    down_full = units_full[:, 2 * units :]
    output_pieces = jnp.concatenate(sent_gathered(output_weight), axis=1)

    position = lax.axis_index("ctx")
    own_ids = lax.dynamic_slice_in_dim(segment_ids, position * length, length)
    before = min(length, (MAX_DOC_BLOCKS - 1) * BLOCK_TOKENS)
    prev_start = jnp.maximum(position * length - before, 0)
    prev_ids = jnp.where(
        position > 0, lax.dynamic_slice_in_dim(segment_ids, prev_start, before), -2
    )
    key_ids = jnp.concatenate([prev_ids, own_ids])
    query_pos = jnp.arange(length, dtype=jnp.int32)
    key_pos = jnp.arange(before + length, dtype=jnp.int32) - before
    allowed = (query_pos[:, None] == key_pos[None, :]) | (own_ids[:, None] == key_ids[None, :]) & (
        own_ids[:, None] >= 0
    ) & (key_pos[None, :] < query_pos[:, None])

    pre_attention_gain, post_attention_gain, pre_feedforward_gain, post_feedforward_gain = (
        by_core(gain)
        for gain in (
            pre_attention_gain,
            post_attention_gain,
            pre_feedforward_gain,
            post_feedforward_gain,
        )
    )
    hidden_in = by_core(hidden_in)
    normed_one = rms(hidden_in.astype(F32), pre_attention_gain).astype(LOW)
    upstream_all = by_core(cotangent)
    inputs = lax.dynamic_slice_in_dim(hidden_in, tp_rank * piece, piece).astype(F32)
    upstream = lax.dynamic_slice_in_dim(upstream_all, tp_rank * piece, piece).astype(F32)

    qkv_low = product(normed_one, qkv_full).astype(LOW)
    queries = qkv_low[:, :heads_width].reshape(length, kv_heads, repeats, HD)
    kv_low = qkv_low[:, heads_width:]
    kv_all = jnp.concatenate([passed_along(kv_low[-before:], "ctx", 1), kv_low], axis=0)
    keys_all = kv_all[:, :kv_width].reshape(before + length, kv_heads, HD)
    values_all = kv_all[:, kv_width:].reshape(before + length, kv_heads, HD)
    scores, powers = attention_scores(queries, keys_all, allowed, scaling)
    totals = jnp.sum(powers, axis=-1, keepdims=True)
    probs_low = (powers / totals).astype(LOW)
    attended = jnp.einsum("grqk,kgd->qgrd", probs_low, values_all, preferred_element_type=F32)
    attended_low = attended.reshape(length, -1).astype(LOW)

    branch_one = scattered(
        ordered_blocks(transposed_product(attended_low, output_full).astype(LOW))
    )
    branch_one_all = in_order(gathered(branch_one.astype(LOW))).astype(F32)
    middle_all = hidden_in.astype(F32) + rms(branch_one_all, post_attention_gain)
    middle = lax.dynamic_slice_in_dim(middle_all, tp_rank * piece, piece)
    normed_two = rms(middle_all, pre_feedforward_gain).astype(LOW)

    gate_up = product(normed_two, gate_up_full)
    gate_value = gate_up[:, :units]
    up_value = gate_up[:, units:]
    hidden_low = geglu(gate_value, up_value).astype(LOW)
    branch_two = lax.psum(transposed_product(hidden_low, down_full).astype(LOW), "tp")
    output_all = sent_rows(output_pieces)
    branch_two = branch_two.astype(F32)
    _, pull_four = jax.vjp(rms, branch_two, post_feedforward_gain)
    grad_branch_two, grad_gain_four = pull_four(upstream_all.astype(F32))
    grad_gain_four = grad_gain_four / tp_size
    grad_two_low = grad_branch_two.astype(LOW)

    down_sent, grad_two_low = lax.optimization_barrier(
        (sent_to_core(grad_two_low, hidden_low), grad_two_low)
    )
    down_arrived = over_cores(down_sent)
    _, pull_glu = jax.vjp(geglu, gate_value, up_value)
    grad_gate, grad_up = pull_glu(product(grad_two_low, down_full))
    grad_gate_up = jnp.concatenate([grad_gate.astype(LOW), grad_up.astype(LOW)], axis=1)
    grad_down_low = chip_rows(grad_two_low, hidden_low, down_arrived)
    down_share = share_rows(grad_down_low)
    grad_normed_two = transposed_product(grad_gate_up, gate_up_full).astype(LOW)
    grad_normed_two = sent_scattered(ordered_blocks(grad_normed_two))
    outputs = by_chip((middle_all + rms(branch_two, post_feedforward_gain)).astype(LOW))
    gate_up_sent = sent_to_core(normed_two, grad_gate_up)
    gate_up_arrived = over_cores(gate_up_sent)
    grad_gate_up_low = chip_rows(normed_two, grad_gate_up, gate_up_arrived)
    gate_up_share = share_rows(grad_gate_up_low)

    _, pull_three = jax.vjp(rms, middle, pre_feedforward_gain)
    grad_middle = upstream + pull_three(grad_normed_two)[0]
    _, pull_two = jax.vjp(rms, branch_one, post_attention_gain)
    grad_branch_one = pull_two(grad_middle)[0]
    grad_one_own = grad_branch_one.astype(LOW)
    grad_attended = product(grad_one_own, output_all).astype(LOW)
    grad_attended, grad_one_own = lax.optimization_barrier(
        (exchanged(grad_attended), grad_one_own)
    )
    grad_attended = grad_attended.reshape(length, kv_heads, repeats, HD)
    later = (middle, grad_normed_two, branch_one, grad_middle, grad_one_own)
    middle_kept, normed_kept, branch_kept, grad_kept, grad_one_own = lax.optimization_barrier(later)
    grad_one_low = in_order(sent_gathered(grad_one_own))
    output_sent = sent_to_core(grad_one_low, attended_low)
    output_arrived = over_cores(output_sent)
    grad_output_low = chip_rows(grad_one_low, attended_low, output_arrived)
    probs = powers / totals
    grad_probs = jnp.einsum(
        "qgrd,kgd->grqk", grad_attended, values_all, preferred_element_type=F32
    )
    inner = jnp.sum(probs * grad_probs, axis=-1, keepdims=True)
    grad_capped = probs * (grad_probs - inner)
    squashed = jnp.tanh(scores / CAP)
    grad_scores = (grad_capped * (1.0 - squashed * squashed)).astype(LOW)
    grad_query_low = (
        (
            jnp.einsum("grqk,kgd->qgrd", grad_scores, keys_all, preferred_element_type=F32)
            * scaling
        )
        .reshape(length, -1)
        .astype(LOW)
    )
    grad_keys_all = (
        jnp.einsum("grqk,qgrd->kgd", grad_scores, queries, preferred_element_type=F32) * scaling
    ).reshape(before + length, -1)
    grad_values_all = jnp.einsum(
        "grqk,qgrd->kgd", probs_low, grad_attended, preferred_element_type=F32
    ).reshape(before + length, -1)
    grad_value_low = returned(grad_values_all, length)
    grad_key_low = returned(grad_keys_all, length)
    grad_kv_low = jnp.concatenate([grad_key_low, grad_value_low], axis=1)
    grad_qkv = jnp.concatenate([grad_query_low, grad_kv_low], axis=1)
    grad_normed_one = transposed_product(grad_qkv, qkv_full).astype(LOW)
    unused_one, pull_one = jax.vjp(rms, hidden_in.astype(F32), pre_attention_gain)
    grad_gain_one = pull_one(grad_normed_one.astype(F32))[1]
    grad_gain_three = jax.vjp(rms, middle_kept, pre_feedforward_gain)[1](normed_kept)[1]
    grad_gain_two = jax.vjp(rms, branch_kept, post_attention_gain)[1](grad_kept)[1]
    gains = by_chip(jnp.stack([grad_gain_one, grad_gain_two, grad_gain_three, grad_gain_four]))
    gains = sum((shift(gains, k) for k in range(1, tp_size)), gains)
    for axis in ROWS:
        gains = summed(gains, axis)
    grad_normed_one = sent_scattered(ordered_blocks(grad_normed_one))
    qkv_sent = sent_to_core(normed_one, grad_qkv)
    qkv_arrived = over_cores(qkv_sent)
    grad_qkv_low = chip_rows(normed_one, grad_qkv, qkv_arrived)
    grad_attention = by_rows(jnp.concatenate([grad_qkv_low, grad_output_low], axis=1))
    attention_share = share_rows(grad_attention).astype(F32)

    unused_one, pull_one = jax.vjp(rms, inputs, pre_attention_gain)
    grad_inputs_low = by_chip((grad_middle + pull_one(grad_normed_one)[0]).astype(LOW))
    grad_inputs = in_order(sent_gathered(grad_inputs_low))

    share = hidden_in.shape[1] // (lax.axis_size("fsdp") * lax.axis_size("ctx"))
    row_rank = lax.axis_index("fsdp") * lax.axis_size("ctx") + lax.axis_index("ctx")
    gain_shares = lax.dynamic_slice_in_dim(gains, row_rank * share, share, axis=1)
    edges = [0, heads_width, heads_width + kv_width, qkv_width, qkv_width + heads_width]
    attention_shares = [attention_share[:, a:b] for a, b in zip(edges[:-1], edges[1:])]
    gate_up_share = gate_up_share.astype(F32)
    return (
        (outputs, grad_inputs)
        + tuple(gain_shares[i] for i in range(4))
        + tuple(attention_shares)
        + (gate_up_share[:, :units], gate_up_share[:, units:], down_share.astype(F32))
    )


def solution(mesh):
    tokens = P(ROWS, None)
    weight = P(ROWS, "tp")
    return jax.shard_map(
        shards,
        mesh=mesh,
        in_specs=(tokens, tokens, P("fsdp")) + (P(),) * 4 + (weight,) * 7,
        out_specs=(tokens, tokens) + (P(ROWS),) * 4 + (weight,) * 7,
        check_vma=False,
    )
```

```python
import jax
import jax.numpy as jnp
from jax import lax
from jax.experimental.layout import Layout, with_layout_constraint
from jax.sharding import PartitionSpec as P


HD = 256
BLOCK_TOKENS = 128
MAX_DOC_BLOCKS = 4
CAP = 50.0
EPS = 1e-06
ROWS = ("fsdp", "ctx")
LOW = jnp.bfloat16
F32 = jnp.float32


def passed_along(block, axis, distance):
    devices = range(lax.axis_size(axis))
    route = [(i - distance, i) for i in devices if i - distance in devices]
    return lax.ppermute(block, axis, route)


def rms(value, gain):
    return value * lax.rsqrt(jnp.mean(value * value, axis=-1, keepdims=True) + EPS) * gain


def geglu(gate_value, up_value):
    return jax.nn.gelu(gate_value, approximate=True) * up_value


def product(left, right):
    return jnp.dot(left, right, preferred_element_type=F32)


def rows_product(left, right):
    return lax.dot_general(left, right, (((0,), (0,)), ((), ())), preferred_element_type=F32)


def transposed_product(left, right):
    return lax.dot_general(left, right, (((1,), (1,)), ((), ())), preferred_element_type=F32)


def onward(block, distance, senders):
    return lax.ppermute(block, "tp", [(i, i + distance) for i in senders])


def returned(grads, length):
    before = grads.shape[0] - length
    back = passed_along(grads[:before].astype(LOW), "ctx", -1)
    back = jnp.pad(back, ((length - before, 0), (0, 0))).astype(F32)
    return (grads[before:] + back).astype(LOW)


def shift(block, distance):
    size = lax.axis_size("tp")
    return lax.ppermute(block, "tp", [(i, (i + distance) % size) for i in range(size)])


def distances(size):
    return sorted(range(1, size), key=lambda k: (abs(2 * k - size), k))


def sent_scattered(blocks):
    blocks = lax.optimization_barrier(tuple(blocks))
    arrived = [shift(blocks[k], -k) for k in distances(len(blocks))]
    total = blocks[0].astype(F32)
    for block in arrived:
        total = total + block.astype(F32)
    return total


def sent_gathered(block):
    size = lax.axis_size("tp")
    pieces = {k: shift(block, k) for k in distances(size)}
    return [block] + [pieces[k] for k in range(1, size)]


def scattered(blocks):
    size = lax.axis_size("tp")
    rising, falling = None, None
    for step in range(1, size):
        rise, fall = blocks[step], blocks[size - step]
        if rising is not None:
            rise = (rise.astype(F32) + rising.astype(F32)).astype(LOW)
            fall = (fall.astype(F32) + falling.astype(F32)).astype(LOW)
        rise, fall = lax.optimization_barrier((rise, fall))
        rising = onward(rise, 1, range(step))
        falling = onward(fall, -1, range(size - step, size))
    return blocks[0].astype(F32) + (rising.astype(F32) + falling.astype(F32))


def gathered(block):
    size = lax.axis_size("tp")
    rank = lax.axis_index("tp")
    rising, falling = [block], [block]
    for step in range(1, size):
        rise = onward(rising[-1], 1, range(step - 1, size - 1))
        fall = onward(falling[-1], -1, range(1, size - step + 1))
        rise, fall = lax.optimization_barrier((rise, fall))
        rising.append(rise)
        falling.append(fall)
    return [block] + [
        jnp.where(rank >= k, rising[k], falling[size - k]) for k in range(1, size)
    ]


def ordered_blocks(partial):
    size = lax.axis_size("tp")
    rank = lax.axis_index("tp")
    blocks = partial.reshape(size, -1, partial.shape[-1])
    return [
        lax.dynamic_index_in_dim(blocks, (rank - k) % size, 0, False) for k in range(size)
    ]


def in_order(pieces):
    size = lax.axis_size("tp")
    rank = lax.axis_index("tp")
    whole = jnp.zeros((size,) + pieces[0].shape, pieces[0].dtype)
    for k in range(size):
        whole = lax.dynamic_update_index_in_dim(whole, pieces[k], (rank - k) % size, 0)
    return whole.reshape(-1, pieces[0].shape[-1])


def exchanged(value):
    size = lax.axis_size("tp")
    rank = lax.axis_index("tp")
    width = value.shape[1] // size
    pieces = [value[:, k * width : (k + 1) * width] for k in range(size)]
    pieces = lax.optimization_barrier(tuple(pieces))
    whole = jnp.zeros((size,) + pieces[0].shape, value.dtype)
    whole = lax.dynamic_update_index_in_dim(whole, pieces[0], rank, 0)
    for k in distances(size):
        arrived = shift(pieces[k], -k)
        whole = lax.dynamic_update_index_in_dim(whole, arrived, (rank + k) % size, 0)
    return whole.reshape(-1, width)


def summed(value, axis):
    size = lax.axis_size(axis)
    bit = 1
    while bit < size:
        value = value + lax.ppermute(value, axis, [(i, i ^ bit) for i in range(size)])
        bit *= 2
    return value


def attention_scores(queries, keys_all, allowed, scaling):
    scores = (
        jnp.einsum("qgrd,kgd->grqk", queries, keys_all, preferred_element_type=F32) * scaling
    )
    capped = CAP * jnp.tanh(scores / CAP)
    powers = jnp.where(allowed[None, None], jnp.exp(capped), 0.0)
    return (scores, powers)


def by_rows(value):
    return with_layout_constraint(value, Layout(major_to_minor=(0, 1)))


def row_groups():
    width = lax.axis_size("ctx")
    ranks = range(lax.axis_size("fsdp") * width)
    return [[r for r in ranks if r // width % 2 == core] for core in range(2)]


def swapped(value, first, second):
    part = value.shape[-1] // (first * second)
    order = [i * second + j for j in range(second) for i in range(first)]
    return jnp.concatenate([value[..., k * part : (k + 1) * part] for k in order], axis=-1)


def by_core(value):
    return swapped(value, lax.axis_size("fsdp") // 2, 2)


def by_chip(value):
    return swapped(value, 2, lax.axis_size("fsdp") // 2)


def gather_rows(weight):
    first, second = row_groups()
    return lax.all_gather(
        weight, ROWS, axis=0, tiled=True, axis_index_groups=[first + second]
    )


def sent_rows(weight):
    ranks = lax.axis_size("fsdp") * lax.axis_size("ctx")
    if (lax.axis_size("fsdp"), lax.axis_size("ctx")) != (4, 2):
        return gather_rows(weight)
    core, pair, width = 2, 4, 1

    def sent(block, bits):
        return lax.ppermute(block, ROWS, [(r, r ^ bits) for r in range(ranks)])

    held = {0: weight}
    for bits in (pair | width, width, pair):
        held[bits] = sent(weight, bits)
    for bits in (0, width, pair, pair | width):
        held[bits | core] = sent(held[bits], core)
    place = {0: 0, width: 1, pair: 2, core: 4}
    rank = lax.axis_index("fsdp") * 2 + lax.axis_index("ctx")
    own = (rank // core) % 2 * 4 + rank // pair * 2 + rank % 2
    whole = jnp.zeros((ranks,) + weight.shape, weight.dtype)
    for bits in held:
        at = own ^ (place[bits & width] | place[bits & pair] | place[bits & core])
        whole = lax.dynamic_update_index_in_dim(whole, held[bits], at, 0)
    return whole.reshape(-1, weight.shape[1])


def rows_of_core(left, core):
    half = left.shape[-1] // 2
    return lax.dynamic_slice_in_dim(left, core * half, half, axis=left.ndim - 1)


def sent_to_core(left, right):
    other = 1 - lax.axis_index("fsdp") % 2
    return rows_product(rows_of_core(left, other), right).astype(LOW)


def over_cores(block):
    return lax.ppermute(block, "fsdp", [(i, i ^ 1) for i in range(lax.axis_size("fsdp"))])


def chip_rows(left, right, arrived):
    own = rows_product(rows_of_core(left, lax.axis_index("fsdp") % 2), right)
    return (own + arrived.astype(F32)).astype(LOW)


def share_rows(grad):
    return lax.psum_scatter(
        grad, ROWS, scatter_dimension=0, tiled=True, axis_index_groups=row_groups()
    )


def shards(
    hidden_in,
    cotangent,
    segment_ids,
    pre_attention_gain,
    post_attention_gain,
    pre_feedforward_gain,
    post_feedforward_gain,
    query_weight,
    key_weight,
    value_weight,
    output_weight,
    gate_weight,
    up_weight,
    down_weight,
):
    length = hidden_in.shape[0]
    heads_width = query_weight.shape[1]
    kv_width = key_weight.shape[1]
    kv_heads = kv_width // HD
    repeats = heads_width // kv_width
    units = gate_weight.shape[1]
    qkv_width = heads_width + 2 * kv_width
    scaling = HD ** (-0.5)
    tp_size = lax.axis_size("tp")
    tp_rank = lax.axis_index("tp")
    piece = length // tp_size

    attention_full = gather_rows(
        jnp.concatenate([query_weight, key_weight, value_weight, output_weight], axis=1)
    )
    qkv_full = attention_full[:, :qkv_width]
    output_full = attention_full[:, qkv_width:]
    units_full = gather_rows(jnp.concatenate([gate_weight, up_weight, down_weight], axis=1))
    gate_up_full = units_full[:, : 2 * units]
    down_full = units_full[:, 2 * units :]
    output_pieces = jnp.concatenate(sent_gathered(output_weight), axis=1)

    position = lax.axis_index("ctx")
    own_ids = lax.dynamic_slice_in_dim(segment_ids, position * length, length)
    before = min(length, (MAX_DOC_BLOCKS - 1) * BLOCK_TOKENS)
    prev_start = jnp.maximum(position * length - before, 0)
    prev_ids = jnp.where(
        position > 0, lax.dynamic_slice_in_dim(segment_ids, prev_start, before), -2
    )
    key_ids = jnp.concatenate([prev_ids, own_ids])
    query_pos = jnp.arange(length, dtype=jnp.int32)
    key_pos = jnp.arange(before + length, dtype=jnp.int32) - before
    allowed = (query_pos[:, None] == key_pos[None, :]) | (own_ids[:, None] == key_ids[None, :]) & (
        own_ids[:, None] >= 0
    ) & (key_pos[None, :] < query_pos[:, None])

    pre_attention_gain, post_attention_gain, pre_feedforward_gain, post_feedforward_gain = (
        by_core(gain)
        for gain in (
            pre_attention_gain,
            post_attention_gain,
            pre_feedforward_gain,
            post_feedforward_gain,
        )
    )
    hidden_in = by_core(hidden_in)
    normed_one = rms(hidden_in.astype(F32), pre_attention_gain).astype(LOW)
    upstream_all = by_core(cotangent)
    inputs = lax.dynamic_slice_in_dim(hidden_in, tp_rank * piece, piece).astype(F32)
    upstream = lax.dynamic_slice_in_dim(upstream_all, tp_rank * piece, piece).astype(F32)

    qkv_low = product(normed_one, qkv_full).astype(LOW)
    queries = qkv_low[:, :heads_width].reshape(length, kv_heads, repeats, HD)
    kv_low = qkv_low[:, heads_width:]
    kv_all = jnp.concatenate([passed_along(kv_low[-before:], "ctx", 1), kv_low], axis=0)
    keys_all = kv_all[:, :kv_width].reshape(before + length, kv_heads, HD)
    values_all = kv_all[:, kv_width:].reshape(before + length, kv_heads, HD)
    scores, powers = attention_scores(queries, keys_all, allowed, scaling)
    totals = jnp.sum(powers, axis=-1, keepdims=True)
    probs_low = (powers / totals).astype(LOW)
    attended = jnp.einsum("grqk,kgd->qgrd", probs_low, values_all, preferred_element_type=F32)
    attended_low = attended.reshape(length, -1).astype(LOW)

    branch_one = scattered(
        ordered_blocks(transposed_product(attended_low, output_full).astype(LOW))
    )
    branch_one_all = in_order(gathered(branch_one.astype(LOW))).astype(F32)
    middle_all = hidden_in.astype(F32) + rms(branch_one_all, post_attention_gain)
    middle = lax.dynamic_slice_in_dim(middle_all, tp_rank * piece, piece)
    normed_two = rms(middle_all, pre_feedforward_gain).astype(LOW)

    gate_up = product(normed_two, gate_up_full)
    gate_value = gate_up[:, :units]
    up_value = gate_up[:, units:]
    hidden_low = geglu(gate_value, up_value).astype(LOW)
    branch_two = lax.psum(transposed_product(hidden_low, down_full).astype(LOW), "tp")
    output_all = sent_rows(output_pieces)
    branch_two = branch_two.astype(F32)
    _, pull_four = jax.vjp(rms, branch_two, post_feedforward_gain)
    grad_branch_two, grad_gain_four = pull_four(upstream_all.astype(F32))
    grad_gain_four = grad_gain_four / tp_size
    grad_two_low = grad_branch_two.astype(LOW)

    down_sent, grad_two_low = lax.optimization_barrier(
        (sent_to_core(grad_two_low, hidden_low), grad_two_low)
    )
    down_arrived = over_cores(down_sent)
    order = distances(tp_size) + [0]
    halves = (order[: tp_size // 2], order[tp_size // 2 :])
    rows = {k: (tp_rank - k) % tp_size * piece for k in order}

    def rows_of(value, offsets):
        blocks = [lax.dynamic_slice_in_dim(value, rows[k], piece) for k in offsets]
        return jnp.concatenate(blocks, axis=0)

    def hidden_back(offsets):
        _, pull_glu = jax.vjp(geglu, rows_of(gate_value, offsets), rows_of(up_value, offsets))
        grad_gate, grad_up = pull_glu(product(rows_of(grad_two_low, offsets), down_full))
        grads = jnp.concatenate([grad_gate.astype(LOW), grad_up.astype(LOW)], axis=1)
        normed = transposed_product(grads, gate_up_full).astype(LOW)
        return grads, [normed[i * piece : (i + 1) * piece] for i in range(len(offsets))]

    first_grads, blocks = hidden_back(halves[0])
    arrived = [shift(block, -k) for k, block in zip(halves[0], blocks)]
    grad_down_low = chip_rows(grad_two_low, hidden_low, down_arrived)
    down_share = share_rows(grad_down_low)
    second_grads, blocks = hidden_back(halves[1])
    arrived += [shift(block, -k) for k, block in zip(halves[1][:-1], blocks[:-1])]
    grad_normed_two = sum((block.astype(F32) for block in arrived), blocks[-1].astype(F32))
    grad_gate_up = jnp.concatenate([first_grads, second_grads], axis=0)
    normed_two = rows_of(normed_two, order)

    outputs = by_chip((middle_all + rms(branch_two, post_feedforward_gain)).astype(LOW))
    gate_up_sent = sent_to_core(normed_two, grad_gate_up)
    gate_up_arrived = over_cores(gate_up_sent)
    grad_gate_up_low = chip_rows(normed_two, grad_gate_up, gate_up_arrived)
    gate_up_share = share_rows(grad_gate_up_low)

    _, pull_three = jax.vjp(rms, middle, pre_feedforward_gain)
    grad_middle = upstream + pull_three(grad_normed_two)[0]
    _, pull_two = jax.vjp(rms, branch_one, post_attention_gain)
    grad_branch_one = pull_two(grad_middle)[0]
    grad_one_own = grad_branch_one.astype(LOW)
    grad_attended = product(grad_one_own, output_all).astype(LOW)
    grad_attended, grad_one_own = lax.optimization_barrier(
        (exchanged(grad_attended), grad_one_own)
    )
    grad_attended = grad_attended.reshape(length, kv_heads, repeats, HD)
    later = (middle, grad_normed_two, branch_one, grad_middle, grad_one_own)
    middle_kept, normed_kept, branch_kept, grad_kept, grad_one_own = lax.optimization_barrier(later)
    grad_one_low = in_order(sent_gathered(grad_one_own))
    output_sent = sent_to_core(grad_one_low, attended_low)
    output_arrived = over_cores(output_sent)
    grad_output_low = chip_rows(grad_one_low, attended_low, output_arrived)
    probs = powers / totals
    grad_probs = jnp.einsum(
        "qgrd,kgd->grqk", grad_attended, values_all, preferred_element_type=F32
    )
    inner = jnp.sum(probs * grad_probs, axis=-1, keepdims=True)
    grad_capped = probs * (grad_probs - inner)
    squashed = jnp.tanh(scores / CAP)
    grad_scores = (grad_capped * (1.0 - squashed * squashed)).astype(LOW)
    grad_query_low = (
        (
            jnp.einsum("grqk,kgd->qgrd", grad_scores, keys_all, preferred_element_type=F32)
            * scaling
        )
        .reshape(length, -1)
        .astype(LOW)
    )
    grad_keys_all = (
        jnp.einsum("grqk,qgrd->kgd", grad_scores, queries, preferred_element_type=F32) * scaling
    ).reshape(before + length, -1)
    grad_values_all = jnp.einsum(
        "grqk,qgrd->kgd", probs_low, grad_attended, preferred_element_type=F32
    ).reshape(before + length, -1)
    grad_value_low = returned(grad_values_all, length)
    grad_key_low = returned(grad_keys_all, length)
    grad_kv_low = jnp.concatenate([grad_key_low, grad_value_low], axis=1)
    grad_qkv = jnp.concatenate([grad_query_low, grad_kv_low], axis=1)
    grad_normed_one = transposed_product(grad_qkv, qkv_full).astype(LOW)
    unused_one, pull_one = jax.vjp(rms, hidden_in.astype(F32), pre_attention_gain)
    grad_gain_one = pull_one(grad_normed_one.astype(F32))[1]
    grad_gain_three = jax.vjp(rms, middle_kept, pre_feedforward_gain)[1](normed_kept)[1]
    grad_gain_two = jax.vjp(rms, branch_kept, post_attention_gain)[1](grad_kept)[1]
    gains = by_chip(jnp.stack([grad_gain_one, grad_gain_two, grad_gain_three, grad_gain_four]))
    gains = sum((shift(gains, k) for k in range(1, tp_size)), gains)
    for axis in ROWS:
        gains = summed(gains, axis)
    grad_normed_one = sent_scattered(ordered_blocks(grad_normed_one))
    qkv_sent = sent_to_core(normed_one, grad_qkv)
    qkv_arrived = over_cores(qkv_sent)
    grad_qkv_low = chip_rows(normed_one, grad_qkv, qkv_arrived)
    grad_attention = by_rows(jnp.concatenate([grad_qkv_low, grad_output_low], axis=1))
    attention_share = share_rows(grad_attention).astype(F32)

    unused_one, pull_one = jax.vjp(rms, inputs, pre_attention_gain)
    grad_inputs_low = by_chip((grad_middle + pull_one(grad_normed_one)[0]).astype(LOW))
    grad_inputs = in_order(sent_gathered(grad_inputs_low))

    share = hidden_in.shape[1] // (lax.axis_size("fsdp") * lax.axis_size("ctx"))
    row_rank = lax.axis_index("fsdp") * lax.axis_size("ctx") + lax.axis_index("ctx")
    gain_shares = lax.dynamic_slice_in_dim(gains, row_rank * share, share, axis=1)
    edges = [0, heads_width, heads_width + kv_width, qkv_width, qkv_width + heads_width]
    attention_shares = [attention_share[:, a:b] for a, b in zip(edges[:-1], edges[1:])]
    gate_up_share = gate_up_share.astype(F32)
    return (
        (outputs, grad_inputs)
        + tuple(gain_shares[i] for i in range(4))
        + tuple(attention_shares)
        + (gate_up_share[:, :units], gate_up_share[:, units:], down_share.astype(F32))
    )


def solution(mesh):
    tokens = P(ROWS, None)
    weight = P(ROWS, "tp")
    return jax.shard_map(
        shards,
        mesh=mesh,
        in_specs=(tokens, tokens, P("fsdp")) + (P(),) * 4 + (weight,) * 7,
        out_specs=(tokens, tokens) + (P(ROWS),) * 4 + (weight,) * 7,
        check_vma=False,
    )
```

```python
import jax
import jax.numpy as jnp
from jax import lax
from jax.experimental.layout import Layout, with_layout_constraint
from jax.sharding import PartitionSpec as P


HD = 256
BLOCK_TOKENS = 128
MAX_DOC_BLOCKS = 4
CAP = 50.0
EPS = 1e-06
ROWS = ("fsdp", "ctx")
LOW = jnp.bfloat16
F32 = jnp.float32


def passed_along(block, axis, distance):
    devices = range(lax.axis_size(axis))
    route = [(i - distance, i) for i in devices if i - distance in devices]
    return lax.ppermute(block, axis, route)


def rms(value, gain):
    return value * lax.rsqrt(jnp.mean(value * value, axis=-1, keepdims=True) + EPS) * gain


def geglu(gate_value, up_value):
    return jax.nn.gelu(gate_value, approximate=True) * up_value


def product(left, right):
    return jnp.dot(left, right, preferred_element_type=F32)


def rows_product(left, right):
    return lax.dot_general(left, right, (((0,), (0,)), ((), ())), preferred_element_type=F32)


def transposed_product(left, right):
    return lax.dot_general(left, right, (((1,), (1,)), ((), ())), preferred_element_type=F32)


def onward(block, distance, senders):
    return lax.ppermute(block, "tp", [(i, i + distance) for i in senders])


def returned(grads, length):
    before = grads.shape[0] - length
    back = passed_along(grads[:before].astype(LOW), "ctx", -1)
    back = jnp.pad(back, ((length - before, 0), (0, 0))).astype(F32)
    return (grads[before:] + back).astype(LOW)


def shift(block, distance):
    size = lax.axis_size("tp")
    return lax.ppermute(block, "tp", [(i, (i + distance) % size) for i in range(size)])


def distances(size):
    return sorted(range(1, size), key=lambda k: (abs(2 * k - size), k))


def sent_scattered(blocks):
    blocks = lax.optimization_barrier(tuple(blocks))
    arrived = [shift(blocks[k], -k) for k in distances(len(blocks))]
    total = blocks[0].astype(F32)
    for block in arrived:
        total = total + block.astype(F32)
    return total


def sent_gathered(block):
    size = lax.axis_size("tp")
    pieces = {k: shift(block, k) for k in distances(size)}
    return [block] + [pieces[k] for k in range(1, size)]


def scattered(blocks):
    size = lax.axis_size("tp")
    rising, falling = None, None
    for step in range(1, size):
        rise, fall = blocks[step], blocks[size - step]
        if rising is not None:
            rise = (rise.astype(F32) + rising.astype(F32)).astype(LOW)
            fall = (fall.astype(F32) + falling.astype(F32)).astype(LOW)
        rise, fall = lax.optimization_barrier((rise, fall))
        rising = onward(rise, 1, range(step))
        falling = onward(fall, -1, range(size - step, size))
    return blocks[0].astype(F32) + (rising.astype(F32) + falling.astype(F32))


def gathered(block):
    size = lax.axis_size("tp")
    rank = lax.axis_index("tp")
    rising, falling = [block], [block]
    for step in range(1, size):
        rise = onward(rising[-1], 1, range(step - 1, size - 1))
        fall = onward(falling[-1], -1, range(1, size - step + 1))
        rise, fall = lax.optimization_barrier((rise, fall))
        rising.append(rise)
        falling.append(fall)
    return [block] + [
        jnp.where(rank >= k, rising[k], falling[size - k]) for k in range(1, size)
    ]


def ordered_blocks(partial):
    size = lax.axis_size("tp")
    rank = lax.axis_index("tp")
    blocks = partial.reshape(size, -1, partial.shape[-1])
    return [
        lax.dynamic_index_in_dim(blocks, (rank - k) % size, 0, False) for k in range(size)
    ]


def in_order(pieces):
    size = lax.axis_size("tp")
    rank = lax.axis_index("tp")
    whole = jnp.zeros((size,) + pieces[0].shape, pieces[0].dtype)
    for k in range(size):
        whole = lax.dynamic_update_index_in_dim(whole, pieces[k], (rank - k) % size, 0)
    return whole.reshape(-1, pieces[0].shape[-1])


def exchanged(value):
    size = lax.axis_size("tp")
    rank = lax.axis_index("tp")
    width = value.shape[1] // size
    pieces = [value[:, k * width : (k + 1) * width] for k in range(size)]
    pieces = lax.optimization_barrier(tuple(pieces))
    whole = jnp.zeros((size,) + pieces[0].shape, value.dtype)
    whole = lax.dynamic_update_index_in_dim(whole, pieces[0], rank, 0)
    for k in distances(size):
        arrived = shift(pieces[k], -k)
        whole = lax.dynamic_update_index_in_dim(whole, arrived, (rank + k) % size, 0)
    return whole.reshape(-1, width)


def summed(value, axis):
    size = lax.axis_size(axis)
    bit = 1
    while bit < size:
        value = value + lax.ppermute(value, axis, [(i, i ^ bit) for i in range(size)])
        bit *= 2
    return value


def attention_scores(queries, keys_all, allowed, scaling):
    scores = (
        jnp.einsum("qgrd,kgd->grqk", queries, keys_all, preferred_element_type=F32) * scaling
    )
    capped = CAP * jnp.tanh(scores / CAP)
    powers = jnp.where(allowed[None, None], jnp.exp(capped), 0.0)
    return (scores, powers)


def by_rows(value):
    return with_layout_constraint(value, Layout(major_to_minor=(0, 1)))


def row_groups():
    width = lax.axis_size("ctx")
    ranks = range(lax.axis_size("fsdp") * width)
    return [[r for r in ranks if r // width % 2 == core] for core in range(2)]


def swapped(value, first, second):
    part = value.shape[-1] // (first * second)
    order = [i * second + j for j in range(second) for i in range(first)]
    return jnp.concatenate([value[..., k * part : (k + 1) * part] for k in order], axis=-1)


def by_core(value):
    return swapped(value, lax.axis_size("fsdp") // 2, 2)


def by_chip(value):
    return swapped(value, 2, lax.axis_size("fsdp") // 2)


def gather_rows(weight):
    first, second = row_groups()
    return lax.all_gather(
        weight, ROWS, axis=0, tiled=True, axis_index_groups=[first + second]
    )


def sent_rows(weight):
    ranks = lax.axis_size("fsdp") * lax.axis_size("ctx")
    if (lax.axis_size("fsdp"), lax.axis_size("ctx")) != (4, 2):
        return gather_rows(weight)
    core, pair, width = 2, 4, 1

    def sent(block, bits):
        return lax.ppermute(block, ROWS, [(r, r ^ bits) for r in range(ranks)])

    held = {0: weight}
    for bits in (pair | width, width, pair):
        held[bits] = sent(weight, bits)
    for bits in (0, width, pair, pair | width):
        held[bits | core] = sent(held[bits], core)
    place = {0: 0, width: 1, pair: 2, core: 4}
    rank = lax.axis_index("fsdp") * 2 + lax.axis_index("ctx")
    own = (rank // core) % 2 * 4 + rank // pair * 2 + rank % 2
    whole = jnp.zeros((ranks,) + weight.shape, weight.dtype)
    for bits in held:
        at = own ^ (place[bits & width] | place[bits & pair] | place[bits & core])
        whole = lax.dynamic_update_index_in_dim(whole, held[bits], at, 0)
    return whole.reshape(-1, weight.shape[1])


def rows_of_core(left, core):
    half = left.shape[-1] // 2
    return lax.dynamic_slice_in_dim(left, core * half, half, axis=left.ndim - 1)


def sent_to_core(left, right):
    other = 1 - lax.axis_index("fsdp") % 2
    return rows_product(rows_of_core(left, other), right).astype(LOW)


def over_cores(block):
    return lax.ppermute(block, "fsdp", [(i, i ^ 1) for i in range(lax.axis_size("fsdp"))])


def chip_rows(left, right, arrived):
    own = rows_product(rows_of_core(left, lax.axis_index("fsdp") % 2), right)
    return (own + arrived.astype(F32)).astype(LOW)


def share_rows(grad):
    return lax.psum_scatter(
        grad, ROWS, scatter_dimension=0, tiled=True, axis_index_groups=row_groups()
    )


def shards(
    hidden_in,
    cotangent,
    segment_ids,
    pre_attention_gain,
    post_attention_gain,
    pre_feedforward_gain,
    post_feedforward_gain,
    query_weight,
    key_weight,
    value_weight,
    output_weight,
    gate_weight,
    up_weight,
    down_weight,
):
    length = hidden_in.shape[0]
    heads_width = query_weight.shape[1]
    kv_width = key_weight.shape[1]
    kv_heads = kv_width // HD
    repeats = heads_width // kv_width
    units = gate_weight.shape[1]
    qkv_width = heads_width + 2 * kv_width
    scaling = HD ** (-0.5)
    tp_size = lax.axis_size("tp")
    tp_rank = lax.axis_index("tp")
    piece = length // tp_size

    attention_full = gather_rows(
        jnp.concatenate([query_weight, key_weight, value_weight, output_weight], axis=1)
    )
    qkv_full = attention_full[:, :qkv_width]
    output_full = attention_full[:, qkv_width:]
    units_full = gather_rows(jnp.concatenate([gate_weight, up_weight, down_weight], axis=1))
    gate_up_full = units_full[:, : 2 * units]
    down_full = units_full[:, 2 * units :]
    output_pieces = jnp.concatenate(sent_gathered(output_weight), axis=1)

    position = lax.axis_index("ctx")
    own_ids = lax.dynamic_slice_in_dim(segment_ids, position * length, length)
    before = min(length, (MAX_DOC_BLOCKS - 1) * BLOCK_TOKENS)
    prev_start = jnp.maximum(position * length - before, 0)
    prev_ids = jnp.where(
        position > 0, lax.dynamic_slice_in_dim(segment_ids, prev_start, before), -2
    )
    key_ids = jnp.concatenate([prev_ids, own_ids])
    query_pos = jnp.arange(length, dtype=jnp.int32)
    key_pos = jnp.arange(before + length, dtype=jnp.int32) - before
    allowed = (query_pos[:, None] == key_pos[None, :]) | (own_ids[:, None] == key_ids[None, :]) & (
        own_ids[:, None] >= 0
    ) & (key_pos[None, :] < query_pos[:, None])

    pre_attention_gain, post_attention_gain, pre_feedforward_gain, post_feedforward_gain = (
        by_core(gain)
        for gain in (
            pre_attention_gain,
            post_attention_gain,
            pre_feedforward_gain,
            post_feedforward_gain,
        )
    )
    hidden_in = by_core(hidden_in)
    normed_one = rms(hidden_in.astype(F32), pre_attention_gain).astype(LOW)
    upstream_all = by_core(cotangent)
    inputs = lax.dynamic_slice_in_dim(hidden_in, tp_rank * piece, piece).astype(F32)
    upstream = lax.dynamic_slice_in_dim(upstream_all, tp_rank * piece, piece).astype(F32)

    qkv_low = product(normed_one, qkv_full).astype(LOW)
    queries = qkv_low[:, :heads_width].reshape(length, kv_heads, repeats, HD)
    kv_low = qkv_low[:, heads_width:]
    kv_all = jnp.concatenate([passed_along(kv_low[-before:], "ctx", 1), kv_low], axis=0)
    keys_all = kv_all[:, :kv_width].reshape(before + length, kv_heads, HD)
    values_all = kv_all[:, kv_width:].reshape(before + length, kv_heads, HD)
    scores, powers = attention_scores(queries, keys_all, allowed, scaling)
    totals = jnp.sum(powers, axis=-1, keepdims=True)
    probs_low = (powers / totals).astype(LOW)
    attended = jnp.einsum("grqk,kgd->qgrd", probs_low, values_all, preferred_element_type=F32)
    attended_low = attended.reshape(length, -1).astype(LOW)

    branch_one = scattered(
        ordered_blocks(transposed_product(attended_low, output_full).astype(LOW))
    )
    branch_one_all = in_order(gathered(branch_one.astype(LOW))).astype(F32)
    middle_all = hidden_in.astype(F32) + rms(branch_one_all, post_attention_gain)
    middle = lax.dynamic_slice_in_dim(middle_all, tp_rank * piece, piece)
    normed_two = rms(middle_all, pre_feedforward_gain).astype(LOW)

    gate_up = product(normed_two, gate_up_full)
    gate_value = gate_up[:, :units]
    up_value = gate_up[:, units:]
    hidden_low = geglu(gate_value, up_value).astype(LOW)
    branch_two = lax.psum(transposed_product(hidden_low, down_full).astype(LOW), "tp")
    output_all = sent_rows(output_pieces)
    branch_two = branch_two.astype(F32)
    _, pull_four = jax.vjp(rms, branch_two, post_feedforward_gain)
    grad_branch_two, grad_gain_four = pull_four(upstream_all.astype(F32))
    grad_gain_four = grad_gain_four / tp_size
    grad_two_low = grad_branch_two.astype(LOW)

    down_sent, grad_two_low = lax.optimization_barrier(
        (sent_to_core(grad_two_low, hidden_low), grad_two_low)
    )
    down_arrived = over_cores(down_sent)
    _, pull_glu = jax.vjp(geglu, gate_value, up_value)
    grad_gate, grad_up = pull_glu(product(grad_two_low, down_full))
    grad_gate_up = jnp.concatenate([grad_gate.astype(LOW), grad_up.astype(LOW)], axis=1)
    grad_normed_two = transposed_product(grad_gate_up, gate_up_full).astype(LOW)
    grad_normed_two = sent_scattered(ordered_blocks(grad_normed_two))
    outputs = by_chip((middle_all + rms(branch_two, post_feedforward_gain)).astype(LOW))
    grad_down_low = chip_rows(grad_two_low, hidden_low, down_arrived)
    down_share = share_rows(grad_down_low)
    gate_up_sent = sent_to_core(normed_two, grad_gate_up)
    gate_up_arrived = over_cores(gate_up_sent)
    grad_gate_up_low = chip_rows(normed_two, grad_gate_up, gate_up_arrived)
    gate_up_share = share_rows(grad_gate_up_low)

    _, pull_three = jax.vjp(rms, middle, pre_feedforward_gain)
    grad_middle = upstream + pull_three(grad_normed_two)[0]
    _, pull_two = jax.vjp(rms, branch_one, post_attention_gain)
    grad_branch_one = pull_two(grad_middle)[0]
    grad_one_own = grad_branch_one.astype(LOW)
    grad_attended = product(grad_one_own, output_all).astype(LOW)
    grad_attended, grad_one_own = lax.optimization_barrier(
        (exchanged(grad_attended), grad_one_own)
    )
    grad_attended = grad_attended.reshape(length, kv_heads, repeats, HD)
    later = (middle, grad_normed_two, branch_one, grad_middle, grad_one_own)
    middle_kept, normed_kept, branch_kept, grad_kept, grad_one_own = lax.optimization_barrier(later)
    grad_one_low = in_order(sent_gathered(grad_one_own))
    output_sent = sent_to_core(grad_one_low, attended_low)
    output_arrived = over_cores(output_sent)
    grad_output_low = chip_rows(grad_one_low, attended_low, output_arrived)
    probs = powers / totals
    grad_probs = jnp.einsum(
        "qgrd,kgd->grqk", grad_attended, values_all, preferred_element_type=F32
    )
    inner = jnp.sum(probs * grad_probs, axis=-1, keepdims=True)
    grad_capped = probs * (grad_probs - inner)
    squashed = jnp.tanh(scores / CAP)
    grad_scores = (grad_capped * (1.0 - squashed * squashed)).astype(LOW)
    grad_query_low = (
        (
            jnp.einsum("grqk,kgd->qgrd", grad_scores, keys_all, preferred_element_type=F32)
            * scaling
        )
        .reshape(length, -1)
        .astype(LOW)
    )
    grad_keys_all = (
        jnp.einsum("grqk,qgrd->kgd", grad_scores, queries, preferred_element_type=F32) * scaling
    ).reshape(before + length, -1)
    grad_values_all = jnp.einsum(
        "grqk,qgrd->kgd", probs_low, grad_attended, preferred_element_type=F32
    ).reshape(before + length, -1)
    grad_value_low = returned(grad_values_all, length)
    grad_key_low = returned(grad_keys_all, length)
    grad_kv_low = jnp.concatenate([grad_key_low, grad_value_low], axis=1)
    grad_qkv = jnp.concatenate([grad_query_low, grad_kv_low], axis=1)
    grad_normed_one = transposed_product(grad_qkv, qkv_full).astype(LOW)
    unused_one, pull_one = jax.vjp(rms, hidden_in.astype(F32), pre_attention_gain)
    grad_gain_one = pull_one(grad_normed_one.astype(F32))[1]
    grad_gain_three = jax.vjp(rms, middle_kept, pre_feedforward_gain)[1](normed_kept)[1]
    grad_gain_two = jax.vjp(rms, branch_kept, post_attention_gain)[1](grad_kept)[1]
    gains = by_chip(jnp.stack([grad_gain_one, grad_gain_two, grad_gain_three, grad_gain_four]))
    gains = sum((shift(gains, k) for k in range(1, tp_size)), gains)
    for axis in ROWS:
        gains = summed(gains, axis)
    grad_normed_one = sent_scattered(ordered_blocks(grad_normed_one))
    qkv_sent = sent_to_core(normed_one, grad_qkv)
    qkv_arrived = over_cores(qkv_sent)
    grad_qkv_low = chip_rows(normed_one, grad_qkv, qkv_arrived)
    grad_attention = by_rows(jnp.concatenate([grad_qkv_low, grad_output_low], axis=1))
    attention_share = share_rows(grad_attention)

    unused_one, pull_one = jax.vjp(rms, inputs, pre_attention_gain)
    grad_inputs_low = by_chip((grad_middle + pull_one(grad_normed_one)[0]).astype(LOW))
    grad_inputs = in_order(sent_gathered(grad_inputs_low))

    share = hidden_in.shape[1] // (lax.axis_size("fsdp") * lax.axis_size("ctx"))
    row_rank = lax.axis_index("fsdp") * lax.axis_size("ctx") + lax.axis_index("ctx")
    gain_shares = lax.dynamic_slice_in_dim(gains, row_rank * share, share, axis=1)
    edges = [0, heads_width, heads_width + kv_width, qkv_width, qkv_width + heads_width]
    attention_shares = [attention_share[:, a:b].astype(F32) for a, b in zip(edges[:-1], edges[1:])]
    gate_share = gate_up_share[:, :units].astype(F32)
    up_share = gate_up_share[:, units:].astype(F32)
    down_share = down_share.astype(F32)
    return (
        (outputs, grad_inputs)
        + tuple(gain_shares[i] for i in range(4))
        + tuple(attention_shares)
        + (gate_share, up_share, down_share)
    )


def solution(mesh):
    tokens = P(ROWS, None)
    weight = P(ROWS, "tp")
    return jax.shard_map(
        shards,
        mesh=mesh,
        in_specs=(tokens, tokens, P("fsdp")) + (P(),) * 4 + (weight,) * 7,
        out_specs=(tokens, tokens) + (P(ROWS),) * 4 + (weight,) * 7,
        check_vma=False,
    )
```

```python
import jax
import jax.numpy as jnp
from jax import lax
from jax.experimental.layout import Layout, with_layout_constraint
from jax.sharding import PartitionSpec as P


HD = 256
BLOCK_TOKENS = 128
MAX_DOC_BLOCKS = 4
CAP = 50.0
EPS = 1e-06
ROWS = ("fsdp", "ctx")
LOW = jnp.bfloat16
F32 = jnp.float32


def passed_along(block, axis, distance):
    devices = range(lax.axis_size(axis))
    route = [(i - distance, i) for i in devices if i - distance in devices]
    return lax.ppermute(block, axis, route)


def rms(value, gain):
    return value * lax.rsqrt(jnp.mean(value * value, axis=-1, keepdims=True) + EPS) * gain


def geglu(gate_value, up_value):
    return jax.nn.gelu(gate_value, approximate=True) * up_value


def product(left, right):
    return jnp.dot(left, right, preferred_element_type=F32)


def rows_product(left, right):
    return lax.dot_general(left, right, (((0,), (0,)), ((), ())), preferred_element_type=F32)


def transposed_product(left, right):
    return lax.dot_general(left, right, (((1,), (1,)), ((), ())), preferred_element_type=F32)


def onward(block, distance, senders):
    return lax.ppermute(block, "tp", [(i, i + distance) for i in senders])


def returned(grads, length):
    before = grads.shape[0] - length
    back = passed_along(grads[:before].astype(LOW), "ctx", -1)
    back = jnp.pad(back, ((length - before, 0), (0, 0))).astype(F32)
    return (grads[before:] + back).astype(LOW)


def shift(block, distance):
    size = lax.axis_size("tp")
    return lax.ppermute(block, "tp", [(i, (i + distance) % size) for i in range(size)])


def distances(size):
    return sorted(range(1, size), key=lambda k: (abs(2 * k - size), k))


def sent_scattered(blocks):
    blocks = lax.optimization_barrier(tuple(blocks))
    arrived = [shift(blocks[k], -k) for k in distances(len(blocks))]
    total = blocks[0].astype(F32)
    for block in arrived:
        total = total + block.astype(F32)
    return total


def sent_gathered(block):
    size = lax.axis_size("tp")
    pieces = {k: shift(block, k) for k in distances(size)}
    return [block] + [pieces[k] for k in range(1, size)]


def scattered(blocks):
    size = lax.axis_size("tp")
    rising, falling = None, None
    for step in range(1, size):
        rise, fall = blocks[step], blocks[size - step]
        if rising is not None:
            rise = (rise.astype(F32) + rising.astype(F32)).astype(LOW)
            fall = (fall.astype(F32) + falling.astype(F32)).astype(LOW)
        rise, fall = lax.optimization_barrier((rise, fall))
        rising = onward(rise, 1, range(step))
        falling = onward(fall, -1, range(size - step, size))
    return blocks[0].astype(F32) + (rising.astype(F32) + falling.astype(F32))


def gathered(block):
    size = lax.axis_size("tp")
    rank = lax.axis_index("tp")
    rising, falling = [block], [block]
    for step in range(1, size):
        rise = onward(rising[-1], 1, range(step - 1, size - 1))
        fall = onward(falling[-1], -1, range(1, size - step + 1))
        rise, fall = lax.optimization_barrier((rise, fall))
        rising.append(rise)
        falling.append(fall)
    return [block] + [
        jnp.where(rank >= k, rising[k], falling[size - k]) for k in range(1, size)
    ]


def ordered_blocks(partial):
    size = lax.axis_size("tp")
    rank = lax.axis_index("tp")
    blocks = partial.reshape(size, -1, partial.shape[-1])
    return [
        lax.dynamic_index_in_dim(blocks, (rank - k) % size, 0, False) for k in range(size)
    ]


def in_order(pieces):
    size = lax.axis_size("tp")
    rank = lax.axis_index("tp")
    whole = jnp.zeros((size,) + pieces[0].shape, pieces[0].dtype)
    for k in range(size):
        whole = lax.dynamic_update_index_in_dim(whole, pieces[k], (rank - k) % size, 0)
    return whole.reshape(-1, pieces[0].shape[-1])


def exchanged(value):
    size = lax.axis_size("tp")
    rank = lax.axis_index("tp")
    width = value.shape[1] // size
    pieces = [value[:, k * width : (k + 1) * width] for k in range(size)]
    pieces = lax.optimization_barrier(tuple(pieces))
    whole = jnp.zeros((size,) + pieces[0].shape, value.dtype)
    whole = lax.dynamic_update_index_in_dim(whole, pieces[0], rank, 0)
    for k in distances(size):
        arrived = shift(pieces[k], -k)
        whole = lax.dynamic_update_index_in_dim(whole, arrived, (rank + k) % size, 0)
    return whole.reshape(-1, width)


def summed(value, axis):
    size = lax.axis_size(axis)
    bit = 1
    while bit < size:
        value = value + lax.ppermute(value, axis, [(i, i ^ bit) for i in range(size)])
        bit *= 2
    return value


def attention_scores(queries, keys_all, allowed, scaling):
    scores = (
        jnp.einsum("qgrd,kgd->grqk", queries, keys_all, preferred_element_type=F32) * scaling
    )
    capped = CAP * jnp.tanh(scores / CAP)
    powers = jnp.where(allowed[None, None], jnp.exp(capped), 0.0)
    return (scores, powers)


def by_rows(value):
    return with_layout_constraint(value, Layout(major_to_minor=(0, 1)))


def row_groups():
    width = lax.axis_size("ctx")
    ranks = range(lax.axis_size("fsdp") * width)
    return [[r for r in ranks if r // width % 2 == core] for core in range(2)]


def swapped(value, first, second):
    part = value.shape[-1] // (first * second)
    order = [i * second + j for j in range(second) for i in range(first)]
    return jnp.concatenate([value[..., k * part : (k + 1) * part] for k in order], axis=-1)


def by_core(value):
    return swapped(value, lax.axis_size("fsdp") // 2, 2)


def by_chip(value):
    return swapped(value, 2, lax.axis_size("fsdp") // 2)


def gather_rows(weight):
    first, second = row_groups()
    return lax.all_gather(
        weight, ROWS, axis=0, tiled=True, axis_index_groups=[first + second]
    )


def sent_rows(weight):
    ranks = lax.axis_size("fsdp") * lax.axis_size("ctx")
    if (lax.axis_size("fsdp"), lax.axis_size("ctx")) != (4, 2):
        return gather_rows(weight)
    core, pair, width = 2, 4, 1

    def sent(block, bits):
        return lax.ppermute(block, ROWS, [(r, r ^ bits) for r in range(ranks)])

    held = {0: weight}
    for bits in (pair | width, width, pair):
        held[bits] = sent(weight, bits)
    for bits in (0, width, pair, pair | width):
        held[bits | core] = sent(held[bits], core)
    place = {0: 0, width: 1, pair: 2, core: 4}
    rank = lax.axis_index("fsdp") * 2 + lax.axis_index("ctx")
    own = (rank // core) % 2 * 4 + rank // pair * 2 + rank % 2
    whole = jnp.zeros((ranks,) + weight.shape, weight.dtype)
    for bits in held:
        at = own ^ (place[bits & width] | place[bits & pair] | place[bits & core])
        whole = lax.dynamic_update_index_in_dim(whole, held[bits], at, 0)
    return whole.reshape(-1, weight.shape[1])


def rows_of_core(left, core):
    half = left.shape[-1] // 2
    return lax.dynamic_slice_in_dim(left, core * half, half, axis=left.ndim - 1)


def sent_to_core(left, right):
    other = 1 - lax.axis_index("fsdp") % 2
    return rows_product(rows_of_core(left, other), right).astype(LOW)


def over_cores(block):
    return lax.ppermute(block, "fsdp", [(i, i ^ 1) for i in range(lax.axis_size("fsdp"))])


def chip_rows(left, right, arrived):
    own = rows_product(rows_of_core(left, lax.axis_index("fsdp") % 2), right)
    return (own + arrived.astype(F32)).astype(LOW)


def share_rows(grad):
    return lax.psum_scatter(
        grad, ROWS, scatter_dimension=0, tiled=True, axis_index_groups=row_groups()
    )


def share_all_rows(grad):
    first, second = row_groups()
    return lax.psum_scatter(
        grad, ROWS, scatter_dimension=0, tiled=True, axis_index_groups=[first + second]
    )


def shards(
    hidden_in,
    cotangent,
    segment_ids,
    pre_attention_gain,
    post_attention_gain,
    pre_feedforward_gain,
    post_feedforward_gain,
    query_weight,
    key_weight,
    value_weight,
    output_weight,
    gate_weight,
    up_weight,
    down_weight,
):
    length = hidden_in.shape[0]
    heads_width = query_weight.shape[1]
    kv_width = key_weight.shape[1]
    kv_heads = kv_width // HD
    repeats = heads_width // kv_width
    units = gate_weight.shape[1]
    qkv_width = heads_width + 2 * kv_width
    scaling = HD ** (-0.5)
    tp_size = lax.axis_size("tp")
    tp_rank = lax.axis_index("tp")
    piece = length // tp_size

    attention_full = gather_rows(
        jnp.concatenate([query_weight, key_weight, value_weight, output_weight], axis=1)
    )
    qkv_full = attention_full[:, :qkv_width]
    output_full = attention_full[:, qkv_width:]
    units_full = gather_rows(jnp.concatenate([gate_weight, up_weight, down_weight], axis=1))
    gate_up_full = units_full[:, : 2 * units]
    down_full = units_full[:, 2 * units :]
    output_pieces = jnp.concatenate(sent_gathered(output_weight), axis=1)

    position = lax.axis_index("ctx")
    own_ids = lax.dynamic_slice_in_dim(segment_ids, position * length, length)
    before = min(length, (MAX_DOC_BLOCKS - 1) * BLOCK_TOKENS)
    prev_start = jnp.maximum(position * length - before, 0)
    prev_ids = jnp.where(
        position > 0, lax.dynamic_slice_in_dim(segment_ids, prev_start, before), -2
    )
    key_ids = jnp.concatenate([prev_ids, own_ids])
    query_pos = jnp.arange(length, dtype=jnp.int32)
    key_pos = jnp.arange(before + length, dtype=jnp.int32) - before
    allowed = (query_pos[:, None] == key_pos[None, :]) | (own_ids[:, None] == key_ids[None, :]) & (
        own_ids[:, None] >= 0
    ) & (key_pos[None, :] < query_pos[:, None])

    pre_attention_gain, post_attention_gain, pre_feedforward_gain, post_feedforward_gain = (
        by_core(gain)
        for gain in (
            pre_attention_gain,
            post_attention_gain,
            pre_feedforward_gain,
            post_feedforward_gain,
        )
    )
    hidden_in = by_core(hidden_in)
    normed_one = rms(hidden_in.astype(F32), pre_attention_gain).astype(LOW)
    upstream_all = by_core(cotangent)
    inputs = lax.dynamic_slice_in_dim(hidden_in, tp_rank * piece, piece).astype(F32)
    upstream = lax.dynamic_slice_in_dim(upstream_all, tp_rank * piece, piece).astype(F32)

    qkv_low = product(normed_one, qkv_full).astype(LOW)
    queries = qkv_low[:, :heads_width].reshape(length, kv_heads, repeats, HD)
    kv_low = qkv_low[:, heads_width:]
    kv_all = jnp.concatenate([passed_along(kv_low[-before:], "ctx", 1), kv_low], axis=0)
    keys_all = kv_all[:, :kv_width].reshape(before + length, kv_heads, HD)
    values_all = kv_all[:, kv_width:].reshape(before + length, kv_heads, HD)
    scores, powers = attention_scores(queries, keys_all, allowed, scaling)
    totals = jnp.sum(powers, axis=-1, keepdims=True)
    probs_low = (powers / totals).astype(LOW)
    attended = jnp.einsum("grqk,kgd->qgrd", probs_low, values_all, preferred_element_type=F32)
    attended_low = attended.reshape(length, -1).astype(LOW)

    branch_one = scattered(
        ordered_blocks(transposed_product(attended_low, output_full).astype(LOW))
    )
    branch_one_all = in_order(gathered(branch_one.astype(LOW))).astype(F32)
    middle_all = hidden_in.astype(F32) + rms(branch_one_all, post_attention_gain)
    middle = lax.dynamic_slice_in_dim(middle_all, tp_rank * piece, piece)
    normed_two = rms(middle_all, pre_feedforward_gain).astype(LOW)

    gate_up = product(normed_two, gate_up_full)
    gate_value = gate_up[:, :units]
    up_value = gate_up[:, units:]
    hidden_low = geglu(gate_value, up_value).astype(LOW)
    branch_two = lax.psum(transposed_product(hidden_low, down_full).astype(LOW), "tp")
    output_all = sent_rows(output_pieces)
    branch_two = branch_two.astype(F32)
    _, pull_four = jax.vjp(rms, branch_two, post_feedforward_gain)
    grad_branch_two, grad_gain_four = pull_four(upstream_all.astype(F32))
    grad_gain_four = grad_gain_four / tp_size
    grad_two_low = grad_branch_two.astype(LOW)

    grad_down_low, grad_two_low = lax.optimization_barrier(
        (rows_product(grad_two_low, hidden_low).astype(LOW), grad_two_low)
    )
    down_share = share_all_rows(grad_down_low)
    _, pull_glu = jax.vjp(geglu, gate_value, up_value)
    grad_gate, grad_up = pull_glu(product(grad_two_low, down_full))
    grad_gate_up = jnp.concatenate([grad_gate.astype(LOW), grad_up.astype(LOW)], axis=1)
    grad_normed_two = transposed_product(grad_gate_up, gate_up_full).astype(LOW)
    grad_normed_two = sent_scattered(ordered_blocks(grad_normed_two))
    outputs = by_chip((middle_all + rms(branch_two, post_feedforward_gain)).astype(LOW))
    gate_up_sent = sent_to_core(normed_two, grad_gate_up)
    gate_up_arrived = over_cores(gate_up_sent)
    grad_gate_up_low = chip_rows(normed_two, grad_gate_up, gate_up_arrived)
    gate_up_share = share_rows(grad_gate_up_low)

    _, pull_three = jax.vjp(rms, middle, pre_feedforward_gain)
    grad_middle = upstream + pull_three(grad_normed_two)[0]
    _, pull_two = jax.vjp(rms, branch_one, post_attention_gain)
    grad_branch_one = pull_two(grad_middle)[0]
    grad_one_own = grad_branch_one.astype(LOW)
    grad_attended = product(grad_one_own, output_all).astype(LOW)
    grad_attended, grad_one_own = lax.optimization_barrier(
        (exchanged(grad_attended), grad_one_own)
    )
    grad_attended = grad_attended.reshape(length, kv_heads, repeats, HD)
    later = (middle, grad_normed_two, branch_one, grad_middle, grad_one_own)
    middle_kept, normed_kept, branch_kept, grad_kept, grad_one_own = lax.optimization_barrier(later)
    grad_one_low = in_order(sent_gathered(grad_one_own))
    output_sent = sent_to_core(grad_one_low, attended_low)
    output_arrived = over_cores(output_sent)
    grad_output_low = chip_rows(grad_one_low, attended_low, output_arrived)
    probs = powers / totals
    grad_probs = jnp.einsum(
        "qgrd,kgd->grqk", grad_attended, values_all, preferred_element_type=F32
    )
    inner = jnp.sum(probs * grad_probs, axis=-1, keepdims=True)
    grad_capped = probs * (grad_probs - inner)
    squashed = jnp.tanh(scores / CAP)
    grad_scores = (grad_capped * (1.0 - squashed * squashed)).astype(LOW)
    grad_query_low = (
        (
            jnp.einsum("grqk,kgd->qgrd", grad_scores, keys_all, preferred_element_type=F32)
            * scaling
        )
        .reshape(length, -1)
        .astype(LOW)
    )
    grad_keys_all = (
        jnp.einsum("grqk,qgrd->kgd", grad_scores, queries, preferred_element_type=F32) * scaling
    ).reshape(before + length, -1)
    grad_values_all = jnp.einsum(
        "grqk,qgrd->kgd", probs_low, grad_attended, preferred_element_type=F32
    ).reshape(before + length, -1)
    grad_value_low = returned(grad_values_all, length)
    grad_key_low = returned(grad_keys_all, length)
    grad_kv_low = jnp.concatenate([grad_key_low, grad_value_low], axis=1)
    grad_qkv = jnp.concatenate([grad_query_low, grad_kv_low], axis=1)
    grad_normed_one = transposed_product(grad_qkv, qkv_full).astype(LOW)
    unused_one, pull_one = jax.vjp(rms, hidden_in.astype(F32), pre_attention_gain)
    grad_gain_one = pull_one(grad_normed_one.astype(F32))[1]
    grad_gain_three = jax.vjp(rms, middle_kept, pre_feedforward_gain)[1](normed_kept)[1]
    grad_gain_two = jax.vjp(rms, branch_kept, post_attention_gain)[1](grad_kept)[1]
    gains = by_chip(jnp.stack([grad_gain_one, grad_gain_two, grad_gain_three, grad_gain_four]))
    gains_arrived = [shift(gains, k) for k in range(1, tp_size)]
    grad_normed_one = sent_scattered(ordered_blocks(grad_normed_one))
    qkv_sent = sent_to_core(normed_one, grad_qkv)
    qkv_arrived = over_cores(qkv_sent)
    grad_qkv_low = chip_rows(normed_one, grad_qkv, qkv_arrived)
    grad_attention = by_rows(jnp.concatenate([grad_qkv_low, grad_output_low], axis=1))
    attention_share = share_rows(grad_attention)

    unused_one, pull_one = jax.vjp(rms, inputs, pre_attention_gain)
    grad_inputs_low = by_chip((grad_middle + pull_one(grad_normed_one)[0]).astype(LOW))
    grad_inputs = in_order(sent_gathered(grad_inputs_low))

    gains_arrived, _ = lax.optimization_barrier((gains_arrived, grad_inputs_low))
    gains = sum(gains_arrived, gains)
    for axis in ROWS:
        gains = summed(gains, axis)
    share = hidden_in.shape[1] // (lax.axis_size("fsdp") * lax.axis_size("ctx"))
    row_rank = lax.axis_index("fsdp") * lax.axis_size("ctx") + lax.axis_index("ctx")
    gain_shares = lax.dynamic_slice_in_dim(gains, row_rank * share, share, axis=1)
    edges = [0, heads_width, heads_width + kv_width, qkv_width, qkv_width + heads_width]
    attention_shares = [
        attention_share[:, a:b].astype(F32) for a, b in zip(edges[:-1], edges[1:])
    ]
    gate_share = gate_up_share[:, :units].astype(F32)
    up_share = gate_up_share[:, units:].astype(F32)
    down_share = down_share.astype(F32)
    return (
        (outputs, grad_inputs)
        + tuple(gain_shares[i] for i in range(4))
        + tuple(attention_shares)
        + (gate_share, up_share, down_share)
    )


def solution(mesh):
    tokens = P(ROWS, None)
    weight = P(ROWS, "tp")
    return jax.shard_map(
        shards,
        mesh=mesh,
        in_specs=(tokens, tokens, P("fsdp")) + (P(),) * 4 + (weight,) * 7,
        out_specs=(tokens, tokens) + (P(ROWS),) * 4 + (weight,) * 7,
        check_vma=False,
    )
```

```python
import jax
import jax.numpy as jnp
from jax import lax
from jax.experimental.layout import Layout, with_layout_constraint
from jax.sharding import PartitionSpec as P


HD = 256
BLOCK_TOKENS = 128
MAX_DOC_BLOCKS = 4
CAP = 50.0
EPS = 1e-06
ROWS = ("fsdp", "ctx")
LOW = jnp.bfloat16
F32 = jnp.float32


def passed_along(block, axis, distance):
    devices = range(lax.axis_size(axis))
    route = [(i - distance, i) for i in devices if i - distance in devices]
    return lax.ppermute(block, axis, route)


def rms(value, gain):
    return value * lax.rsqrt(jnp.mean(value * value, axis=-1, keepdims=True) + EPS) * gain


def geglu(gate_value, up_value):
    return jax.nn.gelu(gate_value, approximate=True) * up_value


def product(left, right):
    return jnp.dot(left, right, preferred_element_type=F32)


def rows_product(left, right):
    return lax.dot_general(left, right, (((0,), (0,)), ((), ())), preferred_element_type=F32)


def transposed_product(left, right):
    return lax.dot_general(left, right, (((1,), (1,)), ((), ())), preferred_element_type=F32)


def onward(block, distance, senders):
    return lax.ppermute(block, "tp", [(i, i + distance) for i in senders])


def returned(grads, length):
    before = grads.shape[0] - length
    back = passed_along(grads[:before].astype(LOW), "ctx", -1)
    back = jnp.pad(back, ((length - before, 0), (0, 0))).astype(F32)
    return (grads[before:] + back).astype(LOW)


def shift(block, distance):
    size = lax.axis_size("tp")
    return lax.ppermute(block, "tp", [(i, (i + distance) % size) for i in range(size)])


def distances(size):
    return sorted(range(1, size), key=lambda k: (abs(2 * k - size), k))


def sent_scattered(blocks):
    blocks = lax.optimization_barrier(tuple(blocks))
    arrived = [shift(blocks[k], -k) for k in distances(len(blocks))]
    total = blocks[0].astype(F32)
    for block in arrived:
        total = total + block.astype(F32)
    return total


def sent_gathered(block, pieces=None):
    size = lax.axis_size("tp")
    pieces = dict(pieces or {})
    pieces.update({k: shift(block, k) for k in distances(size) if k not in pieces})
    return [block] + [pieces[k] for k in range(1, size)]


def scattered(blocks):
    size = lax.axis_size("tp")
    rising, falling = None, None
    for step in range(1, size):
        rise, fall = blocks[step], blocks[size - step]
        if rising is not None:
            rise = (rise.astype(F32) + rising.astype(F32)).astype(LOW)
            fall = (fall.astype(F32) + falling.astype(F32)).astype(LOW)
        rise, fall = lax.optimization_barrier((rise, fall))
        rising = onward(rise, 1, range(step))
        falling = onward(fall, -1, range(size - step, size))
    return blocks[0].astype(F32) + (rising.astype(F32) + falling.astype(F32))


def gathered(block):
    size = lax.axis_size("tp")
    rank = lax.axis_index("tp")
    rising, falling = [block], [block]
    for step in range(1, size):
        rise = onward(rising[-1], 1, range(step - 1, size - 1))
        fall = onward(falling[-1], -1, range(1, size - step + 1))
        rise, fall = lax.optimization_barrier((rise, fall))
        rising.append(rise)
        falling.append(fall)
    return [block] + [
        jnp.where(rank >= k, rising[k], falling[size - k]) for k in range(1, size)
    ]


def ordered_blocks(partial):
    size = lax.axis_size("tp")
    rank = lax.axis_index("tp")
    blocks = partial.reshape(size, -1, partial.shape[-1])
    return [
        lax.dynamic_index_in_dim(blocks, (rank - k) % size, 0, False) for k in range(size)
    ]


def in_order(pieces):
    size = lax.axis_size("tp")
    rank = lax.axis_index("tp")
    whole = jnp.zeros((size,) + pieces[0].shape, pieces[0].dtype)
    for k in range(size):
        whole = lax.dynamic_update_index_in_dim(whole, pieces[k], (rank - k) % size, 0)
    return whole.reshape(-1, pieces[0].shape[-1])


def exchanged(value):
    size = lax.axis_size("tp")
    rank = lax.axis_index("tp")
    width = value.shape[1] // size
    pieces = [value[:, k * width : (k + 1) * width] for k in range(size)]
    pieces = lax.optimization_barrier(tuple(pieces))
    whole = jnp.zeros((size,) + pieces[0].shape, value.dtype)
    whole = lax.dynamic_update_index_in_dim(whole, pieces[0], rank, 0)
    for k in distances(size):
        arrived = shift(pieces[k], -k)
        whole = lax.dynamic_update_index_in_dim(whole, arrived, (rank + k) % size, 0)
    return whole.reshape(-1, width)


def summed(value, axis):
    size = lax.axis_size(axis)
    bit = 1
    while bit < size:
        value = value + lax.ppermute(value, axis, [(i, i ^ bit) for i in range(size)])
        bit *= 2
    return value


def attention_scores(queries, keys_all, allowed, scaling):
    scores = (
        jnp.einsum("qgrd,kgd->grqk", queries, keys_all, preferred_element_type=F32) * scaling
    )
    capped = CAP * jnp.tanh(scores / CAP)
    powers = jnp.where(allowed[None, None], jnp.exp(capped), 0.0)
    return (scores, powers)


def by_rows(value):
    return with_layout_constraint(value, Layout(major_to_minor=(0, 1)))


def row_groups():
    width = lax.axis_size("ctx")
    ranks = range(lax.axis_size("fsdp") * width)
    return [[r for r in ranks if r // width % 2 == core] for core in range(2)]


def swapped(value, first, second):
    part = value.shape[-1] // (first * second)
    order = [i * second + j for j in range(second) for i in range(first)]
    return jnp.concatenate([value[..., k * part : (k + 1) * part] for k in order], axis=-1)


def by_core(value):
    return swapped(value, lax.axis_size("fsdp") // 2, 2)


def by_chip(value):
    return swapped(value, 2, lax.axis_size("fsdp") // 2)


def gather_rows(weight):
    first, second = row_groups()
    return lax.all_gather(
        weight, ROWS, axis=0, tiled=True, axis_index_groups=[first + second]
    )


def sent_rows(weight):
    ranks = lax.axis_size("fsdp") * lax.axis_size("ctx")
    if (lax.axis_size("fsdp"), lax.axis_size("ctx")) != (4, 2):
        return gather_rows(weight)
    core, pair, width = 2, 4, 1

    def sent(block, bits):
        return lax.ppermute(block, ROWS, [(r, r ^ bits) for r in range(ranks)])

    held = {0: weight}
    for bits in (pair | width, width, pair):
        held[bits] = sent(weight, bits)
    for bits in (0, width, pair, pair | width):
        held[bits | core] = sent(held[bits], core)
    place = {0: 0, width: 1, pair: 2, core: 4}
    rank = lax.axis_index("fsdp") * 2 + lax.axis_index("ctx")
    own = (rank // core) % 2 * 4 + rank // pair * 2 + rank % 2
    whole = jnp.zeros((ranks,) + weight.shape, weight.dtype)
    for bits in held:
        at = own ^ (place[bits & width] | place[bits & pair] | place[bits & core])
        whole = lax.dynamic_update_index_in_dim(whole, held[bits], at, 0)
    return whole.reshape(-1, weight.shape[1])


def rows_of_core(left, core):
    half = left.shape[-1] // 2
    return lax.dynamic_slice_in_dim(left, core * half, half, axis=left.ndim - 1)


def sent_to_core(left, right):
    other = 1 - lax.axis_index("fsdp") % 2
    return rows_product(rows_of_core(left, other), right).astype(LOW)


def over_cores(block):
    return lax.ppermute(block, "fsdp", [(i, i ^ 1) for i in range(lax.axis_size("fsdp"))])


def chip_rows(left, right, arrived):
    own = rows_product(rows_of_core(left, lax.axis_index("fsdp") % 2), right)
    return (own + arrived.astype(F32)).astype(LOW)


def share_rows(grad):
    return lax.psum_scatter(
        grad, ROWS, scatter_dimension=0, tiled=True, axis_index_groups=row_groups()
    )


def share_all_rows(grad):
    first, second = row_groups()
    return lax.psum_scatter(
        grad, ROWS, scatter_dimension=0, tiled=True, axis_index_groups=[first + second]
    )


def shards(
    hidden_in,
    cotangent,
    segment_ids,
    pre_attention_gain,
    post_attention_gain,
    pre_feedforward_gain,
    post_feedforward_gain,
    query_weight,
    key_weight,
    value_weight,
    output_weight,
    gate_weight,
    up_weight,
    down_weight,
):
    length = hidden_in.shape[0]
    heads_width = query_weight.shape[1]
    kv_width = key_weight.shape[1]
    kv_heads = kv_width // HD
    repeats = heads_width // kv_width
    units = gate_weight.shape[1]
    qkv_width = heads_width + 2 * kv_width
    scaling = HD ** (-0.5)
    tp_size = lax.axis_size("tp")
    tp_rank = lax.axis_index("tp")
    piece = length // tp_size

    attention_full = gather_rows(
        jnp.concatenate([query_weight, key_weight, value_weight, output_weight], axis=1)
    )
    qkv_full = attention_full[:, :qkv_width]
    output_full = attention_full[:, qkv_width:]
    units_full = gather_rows(jnp.concatenate([gate_weight, up_weight, down_weight], axis=1))
    gate_up_full = units_full[:, : 2 * units]
    down_full = units_full[:, 2 * units :]
    output_pieces = jnp.concatenate(sent_gathered(output_weight), axis=1)

    position = lax.axis_index("ctx")
    own_ids = lax.dynamic_slice_in_dim(segment_ids, position * length, length)
    before = min(length, (MAX_DOC_BLOCKS - 1) * BLOCK_TOKENS)
    prev_start = jnp.maximum(position * length - before, 0)
    prev_ids = jnp.where(
        position > 0, lax.dynamic_slice_in_dim(segment_ids, prev_start, before), -2
    )
    key_ids = jnp.concatenate([prev_ids, own_ids])
    query_pos = jnp.arange(length, dtype=jnp.int32)
    key_pos = jnp.arange(before + length, dtype=jnp.int32) - before
    allowed = (query_pos[:, None] == key_pos[None, :]) | (own_ids[:, None] == key_ids[None, :]) & (
        own_ids[:, None] >= 0
    ) & (key_pos[None, :] < query_pos[:, None])

    pre_attention_gain, post_attention_gain, pre_feedforward_gain, post_feedforward_gain = (
        by_core(gain)
        for gain in (
            pre_attention_gain,
            post_attention_gain,
            pre_feedforward_gain,
            post_feedforward_gain,
        )
    )
    hidden_in = by_core(hidden_in)
    normed_one = rms(hidden_in.astype(F32), pre_attention_gain).astype(LOW)
    upstream_all = by_core(cotangent)
    inputs = lax.dynamic_slice_in_dim(hidden_in, tp_rank * piece, piece).astype(F32)
    upstream = lax.dynamic_slice_in_dim(upstream_all, tp_rank * piece, piece).astype(F32)

    qkv_low = product(normed_one, qkv_full).astype(LOW)
    queries = qkv_low[:, :heads_width].reshape(length, kv_heads, repeats, HD)
    kv_low = qkv_low[:, heads_width:]
    kv_all = jnp.concatenate([passed_along(kv_low[-before:], "ctx", 1), kv_low], axis=0)
    keys_all = kv_all[:, :kv_width].reshape(before + length, kv_heads, HD)
    values_all = kv_all[:, kv_width:].reshape(before + length, kv_heads, HD)
    scores, powers = attention_scores(queries, keys_all, allowed, scaling)
    totals = jnp.sum(powers, axis=-1, keepdims=True)
    probs_low = (powers / totals).astype(LOW)
    attended = jnp.einsum("grqk,kgd->qgrd", probs_low, values_all, preferred_element_type=F32)
    attended_low = attended.reshape(length, -1).astype(LOW)

    branch_one = scattered(
        ordered_blocks(transposed_product(attended_low, output_full).astype(LOW))
    )
    branch_one_all = in_order(gathered(branch_one.astype(LOW))).astype(F32)
    middle_all = hidden_in.astype(F32) + rms(branch_one_all, post_attention_gain)
    middle = lax.dynamic_slice_in_dim(middle_all, tp_rank * piece, piece)
    normed_two = rms(middle_all, pre_feedforward_gain).astype(LOW)

    gate_up = product(normed_two, gate_up_full)
    gate_value = gate_up[:, :units]
    up_value = gate_up[:, units:]
    hidden_low = geglu(gate_value, up_value).astype(LOW)
    branch_two = lax.psum(transposed_product(hidden_low, down_full).astype(LOW), "tp")
    output_all = sent_rows(output_pieces)
    branch_two = branch_two.astype(F32)
    _, pull_four = jax.vjp(rms, branch_two, post_feedforward_gain)
    grad_branch_two, grad_gain_four = pull_four(upstream_all.astype(F32))
    grad_gain_four = grad_gain_four / tp_size
    grad_two_low = grad_branch_two.astype(LOW)

    grad_down_low, grad_two_low = lax.optimization_barrier(
        (rows_product(grad_two_low, hidden_low).astype(LOW), grad_two_low)
    )
    down_share = share_all_rows(grad_down_low)
    _, pull_glu = jax.vjp(geglu, gate_value, up_value)
    grad_gate, grad_up = pull_glu(product(grad_two_low, down_full))
    grad_gate_up = jnp.concatenate([grad_gate.astype(LOW), grad_up.astype(LOW)], axis=1)
    grad_normed_two = transposed_product(grad_gate_up, gate_up_full).astype(LOW)
    grad_normed_two = sent_scattered(ordered_blocks(grad_normed_two))
    outputs = by_chip((middle_all + rms(branch_two, post_feedforward_gain)).astype(LOW))
    gate_up_sent = sent_to_core(normed_two, grad_gate_up)
    gate_up_arrived = over_cores(gate_up_sent)
    grad_gate_up_low = chip_rows(normed_two, grad_gate_up, gate_up_arrived)
    gate_up_share = share_rows(grad_gate_up_low)

    _, pull_three = jax.vjp(rms, middle, pre_feedforward_gain)
    grad_middle = upstream + pull_three(grad_normed_two)[0]
    _, pull_two = jax.vjp(rms, branch_one, post_attention_gain)
    grad_branch_one = pull_two(grad_middle)[0]
    grad_one_own = grad_branch_one.astype(LOW)
    early = {1: shift(grad_one_own, 1)}
    grad_attended = product(grad_one_own, output_all).astype(LOW)
    grad_attended, grad_one_own = lax.optimization_barrier(
        (exchanged(grad_attended), grad_one_own)
    )
    grad_attended = grad_attended.reshape(length, kv_heads, repeats, HD)
    later = (middle, grad_normed_two, branch_one, grad_middle, grad_one_own)
    middle_kept, normed_kept, branch_kept, grad_kept, grad_one_own = lax.optimization_barrier(later)
    grad_one_low = in_order(sent_gathered(grad_one_own, early))
    output_sent = sent_to_core(grad_one_low, attended_low)
    output_arrived = over_cores(output_sent)
    grad_output_low = chip_rows(grad_one_low, attended_low, output_arrived)
    probs = powers / totals
    grad_probs = jnp.einsum(
        "qgrd,kgd->grqk", grad_attended, values_all, preferred_element_type=F32
    )
    inner = jnp.sum(probs * grad_probs, axis=-1, keepdims=True)
    grad_capped = probs * (grad_probs - inner)
    squashed = jnp.tanh(scores / CAP)
    grad_scores = (grad_capped * (1.0 - squashed * squashed)).astype(LOW)
    grad_query_low = (
        (
            jnp.einsum("grqk,kgd->qgrd", grad_scores, keys_all, preferred_element_type=F32)
            * scaling
        )
        .reshape(length, -1)
        .astype(LOW)
    )
    grad_keys_all = (
        jnp.einsum("grqk,qgrd->kgd", grad_scores, queries, preferred_element_type=F32) * scaling
    ).reshape(before + length, -1)
    grad_values_all = jnp.einsum(
        "grqk,qgrd->kgd", probs_low, grad_attended, preferred_element_type=F32
    ).reshape(before + length, -1)
    grad_value_low = returned(grad_values_all, length)
    grad_key_low = returned(grad_keys_all, length)
    grad_kv_low = jnp.concatenate([grad_key_low, grad_value_low], axis=1)
    grad_qkv = jnp.concatenate([grad_query_low, grad_kv_low], axis=1)
    grad_normed_one = transposed_product(grad_qkv, qkv_full).astype(LOW)
    unused_one, pull_one = jax.vjp(rms, hidden_in.astype(F32), pre_attention_gain)
    grad_gain_one = pull_one(grad_normed_one.astype(F32))[1]
    grad_gain_three = jax.vjp(rms, middle_kept, pre_feedforward_gain)[1](normed_kept)[1]
    grad_gain_two = jax.vjp(rms, branch_kept, post_attention_gain)[1](grad_kept)[1]
    gains = by_chip(jnp.stack([grad_gain_one, grad_gain_two, grad_gain_three, grad_gain_four]))
    gains_arrived = [shift(gains, k) for k in range(1, tp_size)]
    grad_normed_one = sent_scattered(ordered_blocks(grad_normed_one))
    qkv_sent = sent_to_core(normed_one, grad_qkv)
    qkv_arrived = over_cores(qkv_sent)
    grad_qkv_low = chip_rows(normed_one, grad_qkv, qkv_arrived)
    grad_attention = by_rows(jnp.concatenate([grad_qkv_low, grad_output_low], axis=1))
    attention_share = share_rows(grad_attention)

    unused_one, pull_one = jax.vjp(rms, inputs, pre_attention_gain)
    grad_inputs_low = by_chip((grad_middle + pull_one(grad_normed_one)[0]).astype(LOW))
    grad_inputs = in_order(sent_gathered(grad_inputs_low))

    gains_arrived, _ = lax.optimization_barrier((gains_arrived, grad_inputs_low))
    gains = sum(gains_arrived, gains)
    for axis in ROWS:
        gains = summed(gains, axis)
    share = hidden_in.shape[1] // (lax.axis_size("fsdp") * lax.axis_size("ctx"))
    row_rank = lax.axis_index("fsdp") * lax.axis_size("ctx") + lax.axis_index("ctx")
    gain_shares = lax.dynamic_slice_in_dim(gains, row_rank * share, share, axis=1)
    edges = [0, heads_width, heads_width + kv_width, qkv_width, qkv_width + heads_width]
    attention_shares = [
        attention_share[:, a:b].astype(F32) for a, b in zip(edges[:-1], edges[1:])
    ]
    gate_share = gate_up_share[:, :units].astype(F32)
    up_share = gate_up_share[:, units:].astype(F32)
    down_share = down_share.astype(F32)
    return (
        (outputs, grad_inputs)
        + tuple(gain_shares[i] for i in range(4))
        + tuple(attention_shares)
        + (gate_share, up_share, down_share)
    )


def solution(mesh):
    tokens = P(ROWS, None)
    weight = P(ROWS, "tp")
    return jax.shard_map(
        shards,
        mesh=mesh,
        in_specs=(tokens, tokens, P("fsdp")) + (P(),) * 4 + (weight,) * 7,
        out_specs=(tokens, tokens) + (P(ROWS),) * 4 + (weight,) * 7,
        check_vma=False,
    )
```

```python
import jax
import jax.numpy as jnp
from jax import lax
from jax.experimental.layout import Layout, with_layout_constraint
from jax.sharding import PartitionSpec as P


HD = 256
BLOCK_TOKENS = 128
MAX_DOC_BLOCKS = 4
CAP = 50.0
EPS = 1e-06
ROWS = ("fsdp", "ctx")
LOW = jnp.bfloat16
F32 = jnp.float32


def passed_along(block, axis, distance):
    devices = range(lax.axis_size(axis))
    route = [(i - distance, i) for i in devices if i - distance in devices]
    return lax.ppermute(block, axis, route)


def rms(value, gain):
    return value * lax.rsqrt(jnp.mean(value * value, axis=-1, keepdims=True) + EPS) * gain


def geglu(gate_value, up_value):
    return jax.nn.gelu(gate_value, approximate=True) * up_value


def product(left, right):
    return jnp.dot(left, right, preferred_element_type=F32)


def rows_product(left, right):
    return lax.dot_general(left, right, (((0,), (0,)), ((), ())), preferred_element_type=F32)


def transposed_product(left, right):
    return lax.dot_general(left, right, (((1,), (1,)), ((), ())), preferred_element_type=F32)


def onward(block, distance, senders):
    return lax.ppermute(block, "tp", [(i, i + distance) for i in senders])


def returned(grads, length):
    before = grads.shape[0] - length
    back = passed_along(grads[:before].astype(LOW), "ctx", -1)
    back = jnp.pad(back, ((length - before, 0), (0, 0))).astype(F32)
    return (grads[before:] + back).astype(LOW)


def shift(block, distance):
    size = lax.axis_size("tp")
    return lax.ppermute(block, "tp", [(i, (i + distance) % size) for i in range(size)])


def distances(size):
    return sorted(range(1, size), key=lambda k: (abs(2 * k - size), k))


def sent_scattered(blocks):
    blocks = lax.optimization_barrier(tuple(blocks))
    arrived = [shift(blocks[k], -k) for k in distances(len(blocks))]
    total = blocks[0].astype(F32)
    for block in arrived:
        total = total + block.astype(F32)
    return total


def sent_gathered(block, pieces=None):
    size = lax.axis_size("tp")
    pieces = dict(pieces or {})
    pieces.update({k: shift(block, k) for k in distances(size) if k not in pieces})
    return [block] + [pieces[k] for k in range(1, size)]


def scattered(blocks):
    size = lax.axis_size("tp")
    rising, falling = None, None
    for step in range(1, size):
        rise, fall = blocks[step], blocks[size - step]
        if rising is not None:
            rise = (rise.astype(F32) + rising.astype(F32)).astype(LOW)
            fall = (fall.astype(F32) + falling.astype(F32)).astype(LOW)
        rise, fall = lax.optimization_barrier((rise, fall))
        rising = onward(rise, 1, range(step))
        falling = onward(fall, -1, range(size - step, size))
    return blocks[0].astype(F32) + (rising.astype(F32) + falling.astype(F32))


def gathered(block):
    size = lax.axis_size("tp")
    rank = lax.axis_index("tp")
    rising, falling = [block], [block]
    for step in range(1, size):
        rise = onward(rising[-1], 1, range(step - 1, size - 1))
        fall = onward(falling[-1], -1, range(1, size - step + 1))
        rise, fall = lax.optimization_barrier((rise, fall))
        rising.append(rise)
        falling.append(fall)
    return [block] + [
        jnp.where(rank >= k, rising[k], falling[size - k]) for k in range(1, size)
    ]


def ordered_blocks(partial):
    size = lax.axis_size("tp")
    rank = lax.axis_index("tp")
    blocks = partial.reshape(size, -1, partial.shape[-1])
    return [
        lax.dynamic_index_in_dim(blocks, (rank - k) % size, 0, False) for k in range(size)
    ]


def in_order(pieces):
    size = lax.axis_size("tp")
    rank = lax.axis_index("tp")
    whole = jnp.zeros((size,) + pieces[0].shape, pieces[0].dtype)
    for k in range(size):
        whole = lax.dynamic_update_index_in_dim(whole, pieces[k], (rank - k) % size, 0)
    return whole.reshape(-1, pieces[0].shape[-1])


def exchanged(value):
    size = lax.axis_size("tp")
    rank = lax.axis_index("tp")
    width = value.shape[1] // size
    pieces = [value[:, k * width : (k + 1) * width] for k in range(size)]
    pieces = lax.optimization_barrier(tuple(pieces))
    whole = jnp.zeros((size,) + pieces[0].shape, value.dtype)
    whole = lax.dynamic_update_index_in_dim(whole, pieces[0], rank, 0)
    for k in distances(size):
        arrived = shift(pieces[k], -k)
        whole = lax.dynamic_update_index_in_dim(whole, arrived, (rank + k) % size, 0)
    return whole.reshape(-1, width)


def summed(value, axis):
    size = lax.axis_size(axis)
    bit = 1
    while bit < size:
        value = value + lax.ppermute(value, axis, [(i, i ^ bit) for i in range(size)])
        bit *= 2
    return value


def attention_scores(queries, keys_all, allowed, scaling):
    scores = (
        jnp.einsum("qgrd,kgd->grqk", queries, keys_all, preferred_element_type=F32) * scaling
    )
    capped = CAP * jnp.tanh(scores / CAP)
    powers = jnp.where(allowed[None, None], jnp.exp(capped), 0.0)
    return (scores, powers)


def by_rows(value):
    return with_layout_constraint(value, Layout(major_to_minor=(0, 1)))


def row_groups():
    width = lax.axis_size("ctx")
    ranks = range(lax.axis_size("fsdp") * width)
    return [[r for r in ranks if r // width % 2 == core] for core in range(2)]


def swapped(value, first, second):
    part = value.shape[-1] // (first * second)
    order = [i * second + j for j in range(second) for i in range(first)]
    return jnp.concatenate([value[..., k * part : (k + 1) * part] for k in order], axis=-1)


def by_core(value):
    return swapped(value, lax.axis_size("fsdp") // 2, 2)


def by_chip(value):
    return swapped(value, 2, lax.axis_size("fsdp") // 2)


def gather_rows(weight):
    first, second = row_groups()
    return lax.all_gather(
        weight, ROWS, axis=0, tiled=True, axis_index_groups=[first + second]
    )


def sent_rows(weight):
    ranks = lax.axis_size("fsdp") * lax.axis_size("ctx")
    if (lax.axis_size("fsdp"), lax.axis_size("ctx")) != (4, 2):
        return gather_rows(weight)
    core, pair, width = 2, 4, 1

    def sent(block, bits):
        return lax.ppermute(block, ROWS, [(r, r ^ bits) for r in range(ranks)])

    held = {0: weight}
    for bits in (pair | width, width, pair):
        held[bits] = sent(weight, bits)
    for bits in (0, width, pair, pair | width):
        held[bits | core] = sent(held[bits], core)
    place = {0: 0, width: 1, pair: 2, core: 4}
    rank = lax.axis_index("fsdp") * 2 + lax.axis_index("ctx")
    own = (rank // core) % 2 * 4 + rank // pair * 2 + rank % 2
    whole = jnp.zeros((ranks,) + weight.shape, weight.dtype)
    for bits in held:
        at = own ^ (place[bits & width] | place[bits & pair] | place[bits & core])
        whole = lax.dynamic_update_index_in_dim(whole, held[bits], at, 0)
    return whole.reshape(-1, weight.shape[1])


def rows_of_core(left, core):
    half = left.shape[-1] // 2
    return lax.dynamic_slice_in_dim(left, core * half, half, axis=left.ndim - 1)


def sent_to_core(left, right):
    other = 1 - lax.axis_index("fsdp") % 2
    return rows_product(rows_of_core(left, other), right).astype(LOW)


def over_cores(block):
    return lax.ppermute(block, "fsdp", [(i, i ^ 1) for i in range(lax.axis_size("fsdp"))])


def chip_rows(left, right, arrived):
    own = rows_product(rows_of_core(left, lax.axis_index("fsdp") % 2), right)
    return (own + arrived.astype(F32)).astype(LOW)


def share_rows(grad):
    return lax.psum_scatter(
        grad, ROWS, scatter_dimension=0, tiled=True, axis_index_groups=row_groups()
    )


def share_all_rows(grad):
    first, second = row_groups()
    return lax.psum_scatter(
        grad, ROWS, scatter_dimension=0, tiled=True, axis_index_groups=[first + second]
    )


def shards(
    hidden_in,
    cotangent,
    segment_ids,
    pre_attention_gain,
    post_attention_gain,
    pre_feedforward_gain,
    post_feedforward_gain,
    query_weight,
    key_weight,
    value_weight,
    output_weight,
    gate_weight,
    up_weight,
    down_weight,
):
    length = hidden_in.shape[0]
    heads_width = query_weight.shape[1]
    kv_width = key_weight.shape[1]
    kv_heads = kv_width // HD
    repeats = heads_width // kv_width
    units = gate_weight.shape[1]
    qkv_width = heads_width + 2 * kv_width
    scaling = HD ** (-0.5)
    tp_size = lax.axis_size("tp")
    tp_rank = lax.axis_index("tp")
    piece = length // tp_size

    attention_full = gather_rows(
        jnp.concatenate([query_weight, key_weight, value_weight, output_weight], axis=1)
    )
    qkv_full = attention_full[:, :qkv_width]
    output_full = attention_full[:, qkv_width:]
    units_full = gather_rows(jnp.concatenate([gate_weight, up_weight, down_weight], axis=1))
    gate_up_full = units_full[:, : 2 * units]
    down_full = units_full[:, 2 * units :]
    output_pieces = jnp.concatenate(sent_gathered(output_weight), axis=1)

    position = lax.axis_index("ctx")
    own_ids = lax.dynamic_slice_in_dim(segment_ids, position * length, length)
    before = min(length, (MAX_DOC_BLOCKS - 1) * BLOCK_TOKENS)
    prev_start = jnp.maximum(position * length - before, 0)
    prev_ids = jnp.where(
        position > 0, lax.dynamic_slice_in_dim(segment_ids, prev_start, before), -2
    )
    key_ids = jnp.concatenate([prev_ids, own_ids])
    query_pos = jnp.arange(length, dtype=jnp.int32)
    key_pos = jnp.arange(before + length, dtype=jnp.int32) - before
    allowed = (query_pos[:, None] == key_pos[None, :]) | (own_ids[:, None] == key_ids[None, :]) & (
        own_ids[:, None] >= 0
    ) & (key_pos[None, :] < query_pos[:, None])

    pre_attention_gain, post_attention_gain, pre_feedforward_gain, post_feedforward_gain = (
        by_core(gain)
        for gain in (
            pre_attention_gain,
            post_attention_gain,
            pre_feedforward_gain,
            post_feedforward_gain,
        )
    )
    hidden_in = by_core(hidden_in)
    normed_one = rms(hidden_in.astype(F32), pre_attention_gain).astype(LOW)
    upstream_all = by_core(cotangent)
    inputs = lax.dynamic_slice_in_dim(hidden_in, tp_rank * piece, piece).astype(F32)
    upstream = lax.dynamic_slice_in_dim(upstream_all, tp_rank * piece, piece).astype(F32)

    qkv_low = product(normed_one, qkv_full).astype(LOW)
    queries = qkv_low[:, :heads_width].reshape(length, kv_heads, repeats, HD)
    kv_low = qkv_low[:, heads_width:]
    kv_all = jnp.concatenate([passed_along(kv_low[-before:], "ctx", 1), kv_low], axis=0)
    keys_all = kv_all[:, :kv_width].reshape(before + length, kv_heads, HD)
    values_all = kv_all[:, kv_width:].reshape(before + length, kv_heads, HD)
    scores, powers = attention_scores(queries, keys_all, allowed, scaling)
    totals = jnp.sum(powers, axis=-1, keepdims=True)
    probs_low = (powers / totals).astype(LOW)
    attended = jnp.einsum("grqk,kgd->qgrd", probs_low, values_all, preferred_element_type=F32)
    attended_low = attended.reshape(length, -1).astype(LOW)

    branch_one = scattered(
        ordered_blocks(transposed_product(attended_low, output_full).astype(LOW))
    )
    branch_one_all = in_order(gathered(branch_one.astype(LOW))).astype(F32)
    middle_all = hidden_in.astype(F32) + rms(branch_one_all, post_attention_gain)
    middle = lax.dynamic_slice_in_dim(middle_all, tp_rank * piece, piece)
    normed_two = rms(middle_all, pre_feedforward_gain).astype(LOW)

    gate_up = product(normed_two, gate_up_full)
    gate_value = gate_up[:, :units]
    up_value = gate_up[:, units:]
    hidden_low = geglu(gate_value, up_value).astype(LOW)
    branch_two = lax.psum(transposed_product(hidden_low, down_full).astype(LOW), "tp")
    output_all = sent_rows(output_pieces)
    branch_two = branch_two.astype(F32)
    _, pull_four = jax.vjp(rms, branch_two, post_feedforward_gain)
    grad_branch_two, grad_gain_four = pull_four(upstream_all.astype(F32))
    grad_gain_four = grad_gain_four / tp_size
    grad_two_low = grad_branch_two.astype(LOW)

    grad_down_low, grad_two_low = lax.optimization_barrier(
        (rows_product(grad_two_low, hidden_low).astype(LOW), grad_two_low)
    )
    down_share = share_all_rows(grad_down_low)
    _, pull_glu = jax.vjp(geglu, gate_value, up_value)
    grad_gate, grad_up = pull_glu(product(grad_two_low, down_full))
    grad_gate_up = jnp.concatenate([grad_gate.astype(LOW), grad_up.astype(LOW)], axis=1)
    grad_normed_two = transposed_product(grad_gate_up, gate_up_full).astype(LOW)
    grad_normed_two = sent_scattered(ordered_blocks(grad_normed_two))
    outputs = by_chip((middle_all + rms(branch_two, post_feedforward_gain)).astype(LOW))
    gate_up_sent = sent_to_core(normed_two, grad_gate_up)
    gate_up_arrived = over_cores(gate_up_sent)
    grad_gate_up_low = chip_rows(normed_two, grad_gate_up, gate_up_arrived)
    gate_up_share = share_rows(grad_gate_up_low)

    _, pull_three = jax.vjp(rms, middle, pre_feedforward_gain)
    grad_middle = upstream + pull_three(grad_normed_two)[0]
    _, pull_two = jax.vjp(rms, branch_one, post_attention_gain)
    grad_branch_one = pull_two(grad_middle)[0]
    grad_one_own = grad_branch_one.astype(LOW)
    early = {1: shift(grad_one_own, 1)}
    grad_attended = product(grad_one_own, output_all).astype(LOW)
    grad_attended = exchanged(grad_attended)
    grad_attended, grad_one_own = lax.optimization_barrier((grad_attended, grad_one_own))
    grad_attended = grad_attended.reshape(length, kv_heads, repeats, HD)
    later = (middle, grad_normed_two, branch_one, grad_middle, grad_one_own)
    middle_kept, normed_kept, branch_kept, grad_kept, grad_one_own = lax.optimization_barrier(later)
    grad_one_low = in_order(sent_gathered(grad_one_own, early))
    output_sent = sent_to_core(grad_one_low, attended_low)
    output_arrived = over_cores(output_sent)
    grad_output_low = chip_rows(grad_one_low, attended_low, output_arrived)
    probs = powers / totals
    grad_probs = jnp.einsum(
        "qgrd,kgd->grqk", grad_attended, values_all, preferred_element_type=F32
    )
    inner = jnp.sum(probs * grad_probs, axis=-1, keepdims=True)
    grad_capped = probs * (grad_probs - inner)
    squashed = jnp.tanh(scores / CAP)
    grad_scores = (grad_capped * (1.0 - squashed * squashed)).astype(LOW)
    grad_query_low = (
        (
            jnp.einsum("grqk,kgd->qgrd", grad_scores, keys_all, preferred_element_type=F32)
            * scaling
        )
        .reshape(length, -1)
        .astype(LOW)
    )
    grad_keys_all = (
        jnp.einsum("grqk,qgrd->kgd", grad_scores, queries, preferred_element_type=F32) * scaling
    ).reshape(before + length, -1)
    grad_values_all = jnp.einsum(
        "grqk,qgrd->kgd", probs_low, grad_attended, preferred_element_type=F32
    ).reshape(before + length, -1)
    grad_value_low = returned(grad_values_all, length)
    grad_key_low = returned(grad_keys_all, length)
    grad_kv_low = jnp.concatenate([grad_key_low, grad_value_low], axis=1)
    grad_qkv = jnp.concatenate([grad_query_low, grad_kv_low], axis=1)
    grad_normed_one = transposed_product(grad_qkv, qkv_full).astype(LOW)
    unused_one, pull_one = jax.vjp(rms, hidden_in.astype(F32), pre_attention_gain)
    grad_gain_one = pull_one(grad_normed_one.astype(F32))[1]
    grad_gain_three = jax.vjp(rms, middle_kept, pre_feedforward_gain)[1](normed_kept)[1]
    grad_gain_two = jax.vjp(rms, branch_kept, post_attention_gain)[1](grad_kept)[1]
    gains = by_chip(jnp.stack([grad_gain_one, grad_gain_two, grad_gain_three, grad_gain_four]))
    gains_arrived = [shift(gains, k) for k in range(1, tp_size)]
    grad_normed_one = sent_scattered(ordered_blocks(grad_normed_one))
    qkv_sent = sent_to_core(normed_one, grad_qkv)
    qkv_arrived = over_cores(qkv_sent)
    grad_qkv_low = chip_rows(normed_one, grad_qkv, qkv_arrived)
    grad_attention = by_rows(jnp.concatenate([grad_qkv_low, grad_output_low], axis=1))
    attention_share = share_rows(grad_attention)

    unused_one, pull_one = jax.vjp(rms, inputs, pre_attention_gain)
    grad_inputs_low = by_chip((grad_middle + pull_one(grad_normed_one)[0]).astype(LOW))
    grad_inputs = in_order(sent_gathered(grad_inputs_low))

    gains_arrived, _ = lax.optimization_barrier((gains_arrived, grad_inputs_low))
    gains = sum(gains_arrived, gains)
    for axis in ROWS:
        gains = summed(gains, axis)
    share = hidden_in.shape[1] // (lax.axis_size("fsdp") * lax.axis_size("ctx"))
    row_rank = lax.axis_index("fsdp") * lax.axis_size("ctx") + lax.axis_index("ctx")
    gain_shares = lax.dynamic_slice_in_dim(gains, row_rank * share, share, axis=1)
    edges = [0, heads_width, heads_width + kv_width, qkv_width, qkv_width + heads_width]
    attention_shares = [
        attention_share[:, a:b].astype(F32) for a, b in zip(edges[:-1], edges[1:])
    ]
    gate_share = gate_up_share[:, :units].astype(F32)
    up_share = gate_up_share[:, units:].astype(F32)
    down_share = down_share.astype(F32)
    return (
        (outputs, grad_inputs)
        + tuple(gain_shares[i] for i in range(4))
        + tuple(attention_shares)
        + (gate_share, up_share, down_share)
    )


def solution(mesh):
    tokens = P(ROWS, None)
    weight = P(ROWS, "tp")
    return jax.shard_map(
        shards,
        mesh=mesh,
        in_specs=(tokens, tokens, P("fsdp")) + (P(),) * 4 + (weight,) * 7,
        out_specs=(tokens, tokens) + (P(ROWS),) * 4 + (weight,) * 7,
        check_vma=False,
    )
```

```python
import jax
import jax.numpy as jnp
from jax import lax
from jax.experimental.layout import Layout, with_layout_constraint
from jax.sharding import PartitionSpec as P


HD = 256
BLOCK_TOKENS = 128
MAX_DOC_BLOCKS = 4
CAP = 50.0
EPS = 1e-06
ROWS = ("fsdp", "ctx")
LOW = jnp.bfloat16
F32 = jnp.float32


def passed_along(block, axis, distance):
    devices = range(lax.axis_size(axis))
    route = [(i - distance, i) for i in devices if i - distance in devices]
    return lax.ppermute(block, axis, route)


def rms(value, gain):
    return value * lax.rsqrt(jnp.mean(value * value, axis=-1, keepdims=True) + EPS) * gain


def geglu(gate_value, up_value):
    return jax.nn.gelu(gate_value, approximate=True) * up_value


def product(left, right):
    return jnp.dot(left, right, preferred_element_type=F32)


def rows_product(left, right):
    return lax.dot_general(left, right, (((0,), (0,)), ((), ())), preferred_element_type=F32)


def transposed_product(left, right):
    return lax.dot_general(left, right, (((1,), (1,)), ((), ())), preferred_element_type=F32)


def onward(block, distance, senders):
    return lax.ppermute(block, "tp", [(i, i + distance) for i in senders])


def returned(grads, length):
    before = grads.shape[0] - length
    back = passed_along(grads[:before].astype(LOW), "ctx", -1)
    back = jnp.pad(back, ((length - before, 0), (0, 0))).astype(F32)
    return (grads[before:] + back).astype(LOW)


def shift(block, distance):
    size = lax.axis_size("tp")
    return lax.ppermute(block, "tp", [(i, (i + distance) % size) for i in range(size)])


def distances(size):
    return sorted(range(1, size), key=lambda k: (abs(2 * k - size), k))


def sent_scattered(blocks):
    blocks = lax.optimization_barrier(tuple(blocks))
    arrived = [shift(blocks[k], -k) for k in distances(len(blocks))]
    total = blocks[0].astype(F32)
    for block in arrived:
        total = total + block.astype(F32)
    return total


def sent_gathered(block, pieces=None):
    size = lax.axis_size("tp")
    pieces = dict(pieces or {})
    pieces.update({k: shift(block, k) for k in distances(size) if k not in pieces})
    return [block] + [pieces[k] for k in range(1, size)]


def scattered(blocks):
    size = lax.axis_size("tp")
    rising, falling = None, None
    for step in range(1, size):
        rise, fall = blocks[step], blocks[size - step]
        if rising is not None:
            rise = (rise.astype(F32) + rising.astype(F32)).astype(LOW)
            fall = (fall.astype(F32) + falling.astype(F32)).astype(LOW)
        rise, fall = lax.optimization_barrier((rise, fall))
        rising = onward(rise, 1, range(step))
        falling = onward(fall, -1, range(size - step, size))
    return blocks[0].astype(F32) + (rising.astype(F32) + falling.astype(F32))


def gathered(block):
    size = lax.axis_size("tp")
    rank = lax.axis_index("tp")
    rising, falling = [block], [block]
    for step in range(1, size):
        rise = onward(rising[-1], 1, range(step - 1, size - 1))
        fall = onward(falling[-1], -1, range(1, size - step + 1))
        rise, fall = lax.optimization_barrier((rise, fall))
        rising.append(rise)
        falling.append(fall)
    return [block] + [
        jnp.where(rank >= k, rising[k], falling[size - k]) for k in range(1, size)
    ]


def ordered_blocks(partial):
    size = lax.axis_size("tp")
    rank = lax.axis_index("tp")
    blocks = partial.reshape(size, -1, partial.shape[-1])
    return [
        lax.dynamic_index_in_dim(blocks, (rank - k) % size, 0, False) for k in range(size)
    ]


def in_order(pieces):
    size = lax.axis_size("tp")
    rank = lax.axis_index("tp")
    whole = jnp.zeros((size,) + pieces[0].shape, pieces[0].dtype)
    for k in range(size):
        whole = lax.dynamic_update_index_in_dim(whole, pieces[k], (rank - k) % size, 0)
    return whole.reshape(-1, pieces[0].shape[-1])


def exchanged(value):
    size = lax.axis_size("tp")
    rank = lax.axis_index("tp")
    width = value.shape[1] // size
    pieces = [value[:, k * width : (k + 1) * width] for k in range(size)]
    pieces = lax.optimization_barrier(tuple(pieces))
    whole = jnp.zeros((size,) + pieces[0].shape, value.dtype)
    whole = lax.dynamic_update_index_in_dim(whole, pieces[0], rank, 0)
    for k in distances(size):
        arrived = shift(pieces[k], -k)
        whole = lax.dynamic_update_index_in_dim(whole, arrived, (rank + k) % size, 0)
    return whole.reshape(-1, width)


def summed(value, axis):
    size = lax.axis_size(axis)
    bit = 1
    while bit < size:
        value = value + lax.ppermute(value, axis, [(i, i ^ bit) for i in range(size)])
        bit *= 2
    return value


def attention_scores(queries, keys_all, allowed, scaling):
    scores = (
        jnp.einsum("qgrd,kgd->grqk", queries, keys_all, preferred_element_type=F32) * scaling
    )
    capped = CAP * jnp.tanh(scores / CAP)
    powers = jnp.where(allowed[None, None], jnp.exp(capped), 0.0)
    return (scores, powers)


def by_rows(value):
    return with_layout_constraint(value, Layout(major_to_minor=(0, 1)))


def row_groups():
    width = lax.axis_size("ctx")
    ranks = range(lax.axis_size("fsdp") * width)
    return [[r for r in ranks if r // width % 2 == core] for core in range(2)]


def swapped(value, first, second):
    part = value.shape[-1] // (first * second)
    order = [i * second + j for j in range(second) for i in range(first)]
    return jnp.concatenate([value[..., k * part : (k + 1) * part] for k in order], axis=-1)


def by_core(value):
    return swapped(value, lax.axis_size("fsdp") // 2, 2)


def by_chip(value):
    return swapped(value, 2, lax.axis_size("fsdp") // 2)


def gather_rows(weight):
    first, second = row_groups()
    return lax.all_gather(
        weight, ROWS, axis=0, tiled=True, axis_index_groups=[first + second]
    )


def sent_rows(weight):
    ranks = lax.axis_size("fsdp") * lax.axis_size("ctx")
    if (lax.axis_size("fsdp"), lax.axis_size("ctx")) != (4, 2):
        return gather_rows(weight)
    core, pair, width = 2, 4, 1

    def sent(block, bits):
        return lax.ppermute(block, ROWS, [(r, r ^ bits) for r in range(ranks)])

    held = {0: weight}
    for bits in (pair | width, width, pair):
        held[bits] = sent(weight, bits)
    for bits in (0, width, pair, pair | width):
        held[bits | core] = sent(held[bits], core)
    place = {0: 0, width: 1, pair: 2, core: 4}
    rank = lax.axis_index("fsdp") * 2 + lax.axis_index("ctx")
    own = (rank // core) % 2 * 4 + rank // pair * 2 + rank % 2
    whole = jnp.zeros((ranks,) + weight.shape, weight.dtype)
    for bits in held:
        at = own ^ (place[bits & width] | place[bits & pair] | place[bits & core])
        whole = lax.dynamic_update_index_in_dim(whole, held[bits], at, 0)
    return whole.reshape(-1, weight.shape[1])


def rows_of_core(left, core):
    half = left.shape[-1] // 2
    return lax.dynamic_slice_in_dim(left, core * half, half, axis=left.ndim - 1)


def sent_to_core(left, right):
    other = 1 - lax.axis_index("fsdp") % 2
    return rows_product(rows_of_core(left, other), right).astype(LOW)


def over_cores(block):
    return lax.ppermute(block, "fsdp", [(i, i ^ 1) for i in range(lax.axis_size("fsdp"))])


def chip_rows(left, right, arrived):
    own = rows_product(rows_of_core(left, lax.axis_index("fsdp") % 2), right)
    return (own + arrived.astype(F32)).astype(LOW)


def share_rows(grad):
    return lax.psum_scatter(
        grad, ROWS, scatter_dimension=0, tiled=True, axis_index_groups=row_groups()
    )


def share_all_rows(grad):
    first, second = row_groups()
    return lax.psum_scatter(
        grad, ROWS, scatter_dimension=0, tiled=True, axis_index_groups=[first + second]
    )


def shards(
    hidden_in,
    cotangent,
    segment_ids,
    pre_attention_gain,
    post_attention_gain,
    pre_feedforward_gain,
    post_feedforward_gain,
    query_weight,
    key_weight,
    value_weight,
    output_weight,
    gate_weight,
    up_weight,
    down_weight,
):
    length = hidden_in.shape[0]
    heads_width = query_weight.shape[1]
    kv_width = key_weight.shape[1]
    kv_heads = kv_width // HD
    repeats = heads_width // kv_width
    units = gate_weight.shape[1]
    qkv_width = heads_width + 2 * kv_width
    scaling = HD ** (-0.5)
    tp_size = lax.axis_size("tp")
    tp_rank = lax.axis_index("tp")
    piece = length // tp_size

    attention_full = gather_rows(
        jnp.concatenate([query_weight, key_weight, value_weight, output_weight], axis=1)
    )
    qkv_full = attention_full[:, :qkv_width]
    output_full = attention_full[:, qkv_width:]
    units_full = gather_rows(jnp.concatenate([gate_weight, up_weight, down_weight], axis=1))
    gate_up_full = units_full[:, : 2 * units]
    down_full = units_full[:, 2 * units :]
    output_pieces = jnp.concatenate(sent_gathered(output_weight), axis=1)

    position = lax.axis_index("ctx")
    own_ids = lax.dynamic_slice_in_dim(segment_ids, position * length, length)
    before = min(length, (MAX_DOC_BLOCKS - 1) * BLOCK_TOKENS)
    prev_start = jnp.maximum(position * length - before, 0)
    prev_ids = jnp.where(
        position > 0, lax.dynamic_slice_in_dim(segment_ids, prev_start, before), -2
    )
    key_ids = jnp.concatenate([prev_ids, own_ids])
    query_pos = jnp.arange(length, dtype=jnp.int32)
    key_pos = jnp.arange(before + length, dtype=jnp.int32) - before
    allowed = (query_pos[:, None] == key_pos[None, :]) | (own_ids[:, None] == key_ids[None, :]) & (
        own_ids[:, None] >= 0
    ) & (key_pos[None, :] < query_pos[:, None])

    pre_attention_gain, post_attention_gain, pre_feedforward_gain, post_feedforward_gain = (
        by_core(gain)
        for gain in (
            pre_attention_gain,
            post_attention_gain,
            pre_feedforward_gain,
            post_feedforward_gain,
        )
    )
    hidden_in = by_core(hidden_in)
    normed_one = rms(hidden_in.astype(F32), pre_attention_gain).astype(LOW)
    upstream_all = by_core(cotangent)
    inputs = lax.dynamic_slice_in_dim(hidden_in, tp_rank * piece, piece).astype(F32)
    upstream = lax.dynamic_slice_in_dim(upstream_all, tp_rank * piece, piece).astype(F32)

    qkv_low = product(normed_one, qkv_full).astype(LOW)
    queries = qkv_low[:, :heads_width].reshape(length, kv_heads, repeats, HD)
    kv_low = qkv_low[:, heads_width:]
    kv_all = jnp.concatenate([passed_along(kv_low[-before:], "ctx", 1), kv_low], axis=0)
    keys_all = kv_all[:, :kv_width].reshape(before + length, kv_heads, HD)
    values_all = kv_all[:, kv_width:].reshape(before + length, kv_heads, HD)
    scores, powers = attention_scores(queries, keys_all, allowed, scaling)
    totals = jnp.sum(powers, axis=-1, keepdims=True)
    probs_low = (powers / totals).astype(LOW)
    attended = jnp.einsum("grqk,kgd->qgrd", probs_low, values_all, preferred_element_type=F32)
    attended_low = attended.reshape(length, -1).astype(LOW)

    branch_one = scattered(
        ordered_blocks(transposed_product(attended_low, output_full).astype(LOW))
    )
    branch_one_all = in_order(gathered(branch_one.astype(LOW))).astype(F32)
    middle_all = hidden_in.astype(F32) + rms(branch_one_all, post_attention_gain)
    middle = lax.dynamic_slice_in_dim(middle_all, tp_rank * piece, piece)
    normed_two = rms(middle_all, pre_feedforward_gain).astype(LOW)

    gate_up = product(normed_two, gate_up_full)
    gate_value = gate_up[:, :units]
    up_value = gate_up[:, units:]
    hidden_low = geglu(gate_value, up_value).astype(LOW)
    branch_two = lax.psum(transposed_product(hidden_low, down_full).astype(LOW), "tp")
    output_all = sent_rows(output_pieces)
    branch_two = branch_two.astype(F32)
    _, pull_four = jax.vjp(rms, branch_two, post_feedforward_gain)
    grad_branch_two, grad_gain_four = pull_four(upstream_all.astype(F32))
    grad_gain_four = grad_gain_four / tp_size
    grad_two_low = grad_branch_two.astype(LOW)

    grad_down_low, grad_two_low = lax.optimization_barrier(
        (rows_product(grad_two_low, hidden_low).astype(LOW), grad_two_low)
    )
    down_share = share_all_rows(grad_down_low)
    _, pull_glu = jax.vjp(geglu, gate_value, up_value)
    grad_gate, grad_up = pull_glu(product(grad_two_low, down_full))
    grad_gate_up = jnp.concatenate([grad_gate.astype(LOW), grad_up.astype(LOW)], axis=1)
    half = (gate_up_full.shape[0] // 256 + 1) // 2 * 256
    first_half = transposed_product(grad_gate_up, gate_up_full[:half]).astype(LOW)
    first_half = sent_scattered(ordered_blocks(first_half))
    second_half = transposed_product(grad_gate_up, gate_up_full[half:]).astype(LOW)
    second_half = sent_scattered(ordered_blocks(second_half))
    grad_normed_two = jnp.concatenate([first_half, second_half], axis=1)
    outputs = by_chip((middle_all + rms(branch_two, post_feedforward_gain)).astype(LOW))
    gate_up_sent = sent_to_core(normed_two, grad_gate_up)
    gate_up_arrived = over_cores(gate_up_sent)
    grad_gate_up_low = chip_rows(normed_two, grad_gate_up, gate_up_arrived)
    gate_up_share = share_rows(grad_gate_up_low)

    _, pull_three = jax.vjp(rms, middle, pre_feedforward_gain)
    grad_middle = upstream + pull_three(grad_normed_two)[0]
    _, pull_two = jax.vjp(rms, branch_one, post_attention_gain)
    grad_branch_one = pull_two(grad_middle)[0]
    grad_one_own = grad_branch_one.astype(LOW)
    early = {1: shift(grad_one_own, 1)}
    grad_attended = product(grad_one_own, output_all).astype(LOW)
    grad_attended, grad_one_own = lax.optimization_barrier(
        (exchanged(grad_attended), grad_one_own)
    )
    grad_attended = grad_attended.reshape(length, kv_heads, repeats, HD)
    later = (middle, grad_normed_two, branch_one, grad_middle, grad_one_own)
    middle_kept, normed_kept, branch_kept, grad_kept, grad_one_own = lax.optimization_barrier(later)
    grad_one_low = in_order(sent_gathered(grad_one_own, early))
    output_sent = sent_to_core(grad_one_low, attended_low)
    output_arrived = over_cores(output_sent)
    grad_output_low = chip_rows(grad_one_low, attended_low, output_arrived)
    probs = powers / totals
    grad_probs = jnp.einsum(
        "qgrd,kgd->grqk", grad_attended, values_all, preferred_element_type=F32
    )
    inner = jnp.sum(probs * grad_probs, axis=-1, keepdims=True)
    grad_capped = probs * (grad_probs - inner)
    squashed = jnp.tanh(scores / CAP)
    grad_scores = (grad_capped * (1.0 - squashed * squashed)).astype(LOW)
    grad_query_low = (
        (
            jnp.einsum("grqk,kgd->qgrd", grad_scores, keys_all, preferred_element_type=F32)
            * scaling
        )
        .reshape(length, -1)
        .astype(LOW)
    )
    grad_keys_all = (
        jnp.einsum("grqk,qgrd->kgd", grad_scores, queries, preferred_element_type=F32) * scaling
    ).reshape(before + length, -1)
    grad_values_all = jnp.einsum(
        "grqk,qgrd->kgd", probs_low, grad_attended, preferred_element_type=F32
    ).reshape(before + length, -1)
    grad_value_low = returned(grad_values_all, length)
    grad_key_low = returned(grad_keys_all, length)
    grad_kv_low = jnp.concatenate([grad_key_low, grad_value_low], axis=1)
    grad_qkv = jnp.concatenate([grad_query_low, grad_kv_low], axis=1)
    grad_normed_one = transposed_product(grad_qkv, qkv_full).astype(LOW)
    unused_one, pull_one = jax.vjp(rms, hidden_in.astype(F32), pre_attention_gain)
    grad_gain_one = pull_one(grad_normed_one.astype(F32))[1]
    grad_gain_three = jax.vjp(rms, middle_kept, pre_feedforward_gain)[1](normed_kept)[1]
    grad_gain_two = jax.vjp(rms, branch_kept, post_attention_gain)[1](grad_kept)[1]
    gains = by_chip(jnp.stack([grad_gain_one, grad_gain_two, grad_gain_three, grad_gain_four]))
    gains_arrived = [shift(gains, k) for k in range(1, tp_size)]
    grad_normed_one = sent_scattered(ordered_blocks(grad_normed_one))
    qkv_sent = sent_to_core(normed_one, grad_qkv)
    qkv_arrived = over_cores(qkv_sent)
    grad_qkv_low = chip_rows(normed_one, grad_qkv, qkv_arrived)
    grad_attention = by_rows(jnp.concatenate([grad_qkv_low, grad_output_low], axis=1))
    attention_share = share_rows(grad_attention)

    unused_one, pull_one = jax.vjp(rms, inputs, pre_attention_gain)
    grad_inputs_low = by_chip((grad_middle + pull_one(grad_normed_one)[0]).astype(LOW))
    grad_inputs = in_order(sent_gathered(grad_inputs_low))

    gains_arrived, _ = lax.optimization_barrier((gains_arrived, grad_inputs_low))
    gains = sum(gains_arrived, gains)
    for axis in ROWS:
        gains = summed(gains, axis)
    share = hidden_in.shape[1] // (lax.axis_size("fsdp") * lax.axis_size("ctx"))
    row_rank = lax.axis_index("fsdp") * lax.axis_size("ctx") + lax.axis_index("ctx")
    gain_shares = lax.dynamic_slice_in_dim(gains, row_rank * share, share, axis=1)
    edges = [0, heads_width, heads_width + kv_width, qkv_width, qkv_width + heads_width]
    attention_shares = [
        attention_share[:, a:b].astype(F32) for a, b in zip(edges[:-1], edges[1:])
    ]
    gate_share = gate_up_share[:, :units].astype(F32)
    up_share = gate_up_share[:, units:].astype(F32)
    down_share = down_share.astype(F32)
    return (
        (outputs, grad_inputs)
        + tuple(gain_shares[i] for i in range(4))
        + tuple(attention_shares)
        + (gate_share, up_share, down_share)
    )


def solution(mesh):
    tokens = P(ROWS, None)
    weight = P(ROWS, "tp")
    return jax.shard_map(
        shards,
        mesh=mesh,
        in_specs=(tokens, tokens, P("fsdp")) + (P(),) * 4 + (weight,) * 7,
        out_specs=(tokens, tokens) + (P(ROWS),) * 4 + (weight,) * 7,
        check_vma=False,
    )
```

```python
import jax
import jax.numpy as jnp
from jax import lax
from jax.experimental.layout import Layout, with_layout_constraint
from jax.sharding import PartitionSpec as P


HD = 256
BLOCK_TOKENS = 128
MAX_DOC_BLOCKS = 4
CAP = 50.0
EPS = 1e-06
ROWS = ("fsdp", "ctx")
LOW = jnp.bfloat16
F32 = jnp.float32


def passed_along(block, axis, distance):
    devices = range(lax.axis_size(axis))
    route = [(i - distance, i) for i in devices if i - distance in devices]
    return lax.ppermute(block, axis, route)


def rms(value, gain):
    return value * lax.rsqrt(jnp.mean(value * value, axis=-1, keepdims=True) + EPS) * gain


def geglu(gate_value, up_value):
    return jax.nn.gelu(gate_value, approximate=True) * up_value


def product(left, right):
    return jnp.dot(left, right, preferred_element_type=F32)


def rows_product(left, right):
    return lax.dot_general(left, right, (((0,), (0,)), ((), ())), preferred_element_type=F32)


def transposed_product(left, right):
    return lax.dot_general(left, right, (((1,), (1,)), ((), ())), preferred_element_type=F32)


def onward(block, distance, senders):
    return lax.ppermute(block, "tp", [(i, i + distance) for i in senders])


def returned(grads, length):
    before = grads.shape[0] - length
    back = passed_along(grads[:before].astype(LOW), "ctx", -1)
    back = jnp.pad(back, ((length - before, 0), (0, 0))).astype(F32)
    return (grads[before:] + back).astype(LOW)


def shift(block, distance):
    size = lax.axis_size("tp")
    return lax.ppermute(block, "tp", [(i, (i + distance) % size) for i in range(size)])


def distances(size):
    return sorted(range(1, size), key=lambda k: (abs(2 * k - size), k))


def sent_scattered(blocks):
    blocks = lax.optimization_barrier(tuple(blocks))
    arrived = [shift(blocks[k], -k) for k in distances(len(blocks))]
    total = blocks[0].astype(F32)
    for block in arrived:
        total = total + block.astype(F32)
    return total


def sent_gathered(block, pieces=None):
    size = lax.axis_size("tp")
    pieces = dict(pieces or {})
    pieces.update({k: shift(block, k) for k in distances(size) if k not in pieces})
    return [block] + [pieces[k] for k in range(1, size)]


def scattered(blocks):
    size = lax.axis_size("tp")
    rising, falling = None, None
    for step in range(1, size):
        rise, fall = blocks[step], blocks[size - step]
        if rising is not None:
            rise = (rise.astype(F32) + rising.astype(F32)).astype(LOW)
            fall = (fall.astype(F32) + falling.astype(F32)).astype(LOW)
        rise, fall = lax.optimization_barrier((rise, fall))
        rising = onward(rise, 1, range(step))
        falling = onward(fall, -1, range(size - step, size))
    return blocks[0].astype(F32) + (rising.astype(F32) + falling.astype(F32))


def gathered(block):
    size = lax.axis_size("tp")
    rank = lax.axis_index("tp")
    rising, falling = [block], [block]
    for step in range(1, size):
        rise = onward(rising[-1], 1, range(step - 1, size - 1))
        fall = onward(falling[-1], -1, range(1, size - step + 1))
        rise, fall = lax.optimization_barrier((rise, fall))
        rising.append(rise)
        falling.append(fall)
    return [block] + [
        jnp.where(rank >= k, rising[k], falling[size - k]) for k in range(1, size)
    ]


def ordered_blocks(partial):
    size = lax.axis_size("tp")
    rank = lax.axis_index("tp")
    blocks = partial.reshape(size, -1, partial.shape[-1])
    return [
        lax.dynamic_index_in_dim(blocks, (rank - k) % size, 0, False) for k in range(size)
    ]


def in_order(pieces):
    size = lax.axis_size("tp")
    rank = lax.axis_index("tp")
    whole = jnp.zeros((size,) + pieces[0].shape, pieces[0].dtype)
    for k in range(size):
        whole = lax.dynamic_update_index_in_dim(whole, pieces[k], (rank - k) % size, 0)
    return whole.reshape(-1, pieces[0].shape[-1])


def exchanged(value):
    size = lax.axis_size("tp")
    rank = lax.axis_index("tp")
    width = value.shape[1] // size
    pieces = [value[:, k * width : (k + 1) * width] for k in range(size)]
    pieces = lax.optimization_barrier(tuple(pieces))
    whole = jnp.zeros((size,) + pieces[0].shape, value.dtype)
    whole = lax.dynamic_update_index_in_dim(whole, pieces[0], rank, 0)
    for k in distances(size):
        arrived = shift(pieces[k], -k)
        whole = lax.dynamic_update_index_in_dim(whole, arrived, (rank + k) % size, 0)
    return whole.reshape(-1, width)


def summed(value, axis):
    size = lax.axis_size(axis)
    bit = 1
    while bit < size:
        value = value + lax.ppermute(value, axis, [(i, i ^ bit) for i in range(size)])
        bit *= 2
    return value


def attention_scores(queries, keys_all, allowed, scaling):
    scores = (
        jnp.einsum("qgrd,kgd->grqk", queries, keys_all, preferred_element_type=F32) * scaling
    )
    capped = CAP * jnp.tanh(scores / CAP)
    powers = jnp.where(allowed[None, None], jnp.exp(capped), 0.0)
    return (scores, powers)


def by_rows(value):
    return with_layout_constraint(value, Layout(major_to_minor=(0, 1)))


def row_groups():
    width = lax.axis_size("ctx")
    ranks = range(lax.axis_size("fsdp") * width)
    return [[r for r in ranks if r // width % 2 == core] for core in range(2)]


def swapped(value, first, second):
    part = value.shape[-1] // (first * second)
    order = [i * second + j for j in range(second) for i in range(first)]
    return jnp.concatenate([value[..., k * part : (k + 1) * part] for k in order], axis=-1)


def by_core(value):
    return swapped(value, lax.axis_size("fsdp") // 2, 2)


def by_chip(value):
    return swapped(value, 2, lax.axis_size("fsdp") // 2)


def gather_rows(weight):
    first, second = row_groups()
    return lax.all_gather(
        weight, ROWS, axis=0, tiled=True, axis_index_groups=[first + second]
    )


def sent_rows(weight):
    ranks = lax.axis_size("fsdp") * lax.axis_size("ctx")
    if (lax.axis_size("fsdp"), lax.axis_size("ctx")) != (4, 2):
        return gather_rows(weight)
    core, pair, width = 2, 4, 1

    def sent(block, bits):
        return lax.ppermute(block, ROWS, [(r, r ^ bits) for r in range(ranks)])

    held = {0: weight}
    for bits in (pair | width, width, pair):
        held[bits] = sent(weight, bits)
    for bits in (0, width, pair, pair | width):
        held[bits | core] = sent(held[bits], core)
    place = {0: 0, width: 1, pair: 2, core: 4}
    rank = lax.axis_index("fsdp") * 2 + lax.axis_index("ctx")
    own = (rank // core) % 2 * 4 + rank // pair * 2 + rank % 2
    whole = jnp.zeros((ranks,) + weight.shape, weight.dtype)
    for bits in held:
        at = own ^ (place[bits & width] | place[bits & pair] | place[bits & core])
        whole = lax.dynamic_update_index_in_dim(whole, held[bits], at, 0)
    return whole.reshape(-1, weight.shape[1])


def rows_of_core(left, core):
    half = left.shape[-1] // 2
    return lax.dynamic_slice_in_dim(left, core * half, half, axis=left.ndim - 1)


def sent_to_core(left, right):
    other = 1 - lax.axis_index("fsdp") % 2
    return rows_product(rows_of_core(left, other), right).astype(LOW)


def over_cores(block):
    return lax.ppermute(block, "fsdp", [(i, i ^ 1) for i in range(lax.axis_size("fsdp"))])


def chip_rows(left, right, arrived):
    own = rows_product(rows_of_core(left, lax.axis_index("fsdp") % 2), right)
    return (own + arrived.astype(F32)).astype(LOW)


def share_rows(grad):
    return lax.psum_scatter(
        grad, ROWS, scatter_dimension=0, tiled=True, axis_index_groups=row_groups()
    )


def share_all_rows(grad):
    first, second = row_groups()
    return lax.psum_scatter(
        grad, ROWS, scatter_dimension=0, tiled=True, axis_index_groups=[first + second]
    )


def shards(
    hidden_in,
    cotangent,
    segment_ids,
    pre_attention_gain,
    post_attention_gain,
    pre_feedforward_gain,
    post_feedforward_gain,
    query_weight,
    key_weight,
    value_weight,
    output_weight,
    gate_weight,
    up_weight,
    down_weight,
):
    length = hidden_in.shape[0]
    heads_width = query_weight.shape[1]
    kv_width = key_weight.shape[1]
    kv_heads = kv_width // HD
    repeats = heads_width // kv_width
    units = gate_weight.shape[1]
    qkv_width = heads_width + 2 * kv_width
    scaling = HD ** (-0.5)
    tp_size = lax.axis_size("tp")
    tp_rank = lax.axis_index("tp")
    piece = length // tp_size

    attention_full = gather_rows(
        jnp.concatenate([query_weight, key_weight, value_weight, output_weight], axis=1)
    )
    qkv_full = attention_full[:, :qkv_width]
    output_full = attention_full[:, qkv_width:]
    units_full = gather_rows(jnp.concatenate([gate_weight, up_weight, down_weight], axis=1))
    gate_up_full = units_full[:, : 2 * units]
    down_full = units_full[:, 2 * units :]
    output_pieces = jnp.concatenate(sent_gathered(output_weight), axis=1)

    position = lax.axis_index("ctx")
    own_ids = lax.dynamic_slice_in_dim(segment_ids, position * length, length)
    before = min(length, (MAX_DOC_BLOCKS - 1) * BLOCK_TOKENS)
    prev_start = jnp.maximum(position * length - before, 0)
    prev_ids = jnp.where(
        position > 0, lax.dynamic_slice_in_dim(segment_ids, prev_start, before), -2
    )
    key_ids = jnp.concatenate([prev_ids, own_ids])
    query_pos = jnp.arange(length, dtype=jnp.int32)
    key_pos = jnp.arange(before + length, dtype=jnp.int32) - before
    allowed = (query_pos[:, None] == key_pos[None, :]) | (own_ids[:, None] == key_ids[None, :]) & (
        own_ids[:, None] >= 0
    ) & (key_pos[None, :] < query_pos[:, None])

    pre_attention_gain, post_attention_gain, pre_feedforward_gain, post_feedforward_gain = (
        by_core(gain)
        for gain in (
            pre_attention_gain,
            post_attention_gain,
            pre_feedforward_gain,
            post_feedforward_gain,
        )
    )
    hidden_in = by_core(hidden_in)
    normed_one = rms(hidden_in.astype(F32), pre_attention_gain).astype(LOW)
    upstream_all = by_core(cotangent)
    inputs = lax.dynamic_slice_in_dim(hidden_in, tp_rank * piece, piece).astype(F32)
    upstream = lax.dynamic_slice_in_dim(upstream_all, tp_rank * piece, piece).astype(F32)

    qkv_low = product(normed_one, qkv_full).astype(LOW)
    queries = qkv_low[:, :heads_width].reshape(length, kv_heads, repeats, HD)
    kv_low = qkv_low[:, heads_width:]
    kv_all = jnp.concatenate([passed_along(kv_low[-before:], "ctx", 1), kv_low], axis=0)
    keys_all = kv_all[:, :kv_width].reshape(before + length, kv_heads, HD)
    values_all = kv_all[:, kv_width:].reshape(before + length, kv_heads, HD)
    scores, powers = attention_scores(queries, keys_all, allowed, scaling)
    totals = jnp.sum(powers, axis=-1, keepdims=True)
    probs_low = (powers / totals).astype(LOW)
    attended = jnp.einsum("grqk,kgd->qgrd", probs_low, values_all, preferred_element_type=F32)
    attended_low = attended.reshape(length, -1).astype(LOW)

    branch_one = scattered(
        ordered_blocks(transposed_product(attended_low, output_full).astype(LOW))
    )
    branch_one_all = in_order(gathered(branch_one.astype(LOW))).astype(F32)
    middle_all = hidden_in.astype(F32) + rms(branch_one_all, post_attention_gain)
    middle = lax.dynamic_slice_in_dim(middle_all, tp_rank * piece, piece)
    normed_two = rms(middle_all, pre_feedforward_gain).astype(LOW)

    gate_up = product(normed_two, gate_up_full)
    gate_value = gate_up[:, :units]
    up_value = gate_up[:, units:]
    hidden_low = geglu(gate_value, up_value).astype(LOW)
    branch_two = lax.psum(transposed_product(hidden_low, down_full).astype(LOW), "tp")
    output_all = sent_rows(output_pieces)
    branch_two = branch_two.astype(F32)
    _, pull_four = jax.vjp(rms, branch_two, post_feedforward_gain)
    grad_branch_two, grad_gain_four = pull_four(upstream_all.astype(F32))
    grad_gain_four = grad_gain_four / tp_size
    grad_two_low = grad_branch_two.astype(LOW)

    grad_down_low, grad_two_low = lax.optimization_barrier(
        (rows_product(grad_two_low, hidden_low).astype(LOW), grad_two_low)
    )
    down_share = share_all_rows(grad_down_low)
    _, pull_glu = jax.vjp(geglu, gate_value, up_value)
    grad_gate, grad_up = pull_glu(product(grad_two_low, down_full))
    grad_gate_up = jnp.concatenate([grad_gate.astype(LOW), grad_up.astype(LOW)], axis=1)
    half = (gate_up_full.shape[0] // 256 + 1) // 2 * 256
    first_half = transposed_product(grad_gate_up, gate_up_full[:half]).astype(LOW)
    first_half = sent_scattered(ordered_blocks(first_half))
    second_half = transposed_product(grad_gate_up, gate_up_full[half:]).astype(LOW)
    second_half = sent_scattered(ordered_blocks(second_half))
    grad_normed_two = jnp.concatenate([first_half, second_half], axis=1)
    outputs = by_chip((middle_all + rms(branch_two, post_feedforward_gain)).astype(LOW))
    gate_up_sent = sent_to_core(normed_two, grad_gate_up)
    gate_up_arrived = over_cores(gate_up_sent)
    own_rows = rows_of_core(normed_two, lax.axis_index("fsdp") % 2)
    gate_up_own = rows_product(own_rows, grad_gate_up).astype(LOW)
    gate_up_own = lax.optimization_barrier(gate_up_own)
    grad_gate_up_low = (gate_up_own.astype(F32) + gate_up_arrived.astype(F32)).astype(LOW)
    gate_up_share = share_rows(grad_gate_up_low)

    _, pull_three = jax.vjp(rms, middle, pre_feedforward_gain)
    grad_middle = upstream + pull_three(grad_normed_two)[0]
    _, pull_two = jax.vjp(rms, branch_one, post_attention_gain)
    grad_branch_one = pull_two(grad_middle)[0]
    grad_one_own = grad_branch_one.astype(LOW)
    early = {1: shift(grad_one_own, 1)}
    grad_attended = product(grad_one_own, output_all).astype(LOW)
    grad_attended, grad_one_own = lax.optimization_barrier(
        (exchanged(grad_attended), grad_one_own)
    )
    grad_attended = grad_attended.reshape(length, kv_heads, repeats, HD)
    later = (middle, grad_normed_two, branch_one, grad_middle, grad_one_own)
    middle_kept, normed_kept, branch_kept, grad_kept, grad_one_own = lax.optimization_barrier(later)
    grad_one_low = in_order(sent_gathered(grad_one_own, early))
    output_sent = sent_to_core(grad_one_low, attended_low)
    output_arrived = over_cores(output_sent)
    grad_output_low = chip_rows(grad_one_low, attended_low, output_arrived)
    probs = powers / totals
    grad_probs = jnp.einsum(
        "qgrd,kgd->grqk", grad_attended, values_all, preferred_element_type=F32
    )
    inner = jnp.sum(probs * grad_probs, axis=-1, keepdims=True)
    grad_capped = probs * (grad_probs - inner)
    squashed = jnp.tanh(scores / CAP)
    grad_scores = (grad_capped * (1.0 - squashed * squashed)).astype(LOW)
    grad_query_low = (
        (
            jnp.einsum("grqk,kgd->qgrd", grad_scores, keys_all, preferred_element_type=F32)
            * scaling
        )
        .reshape(length, -1)
        .astype(LOW)
    )
    grad_keys_all = (
        jnp.einsum("grqk,qgrd->kgd", grad_scores, queries, preferred_element_type=F32) * scaling
    ).reshape(before + length, -1)
    grad_values_all = jnp.einsum(
        "grqk,qgrd->kgd", probs_low, grad_attended, preferred_element_type=F32
    ).reshape(before + length, -1)
    grad_value_low = returned(grad_values_all, length)
    grad_key_low = returned(grad_keys_all, length)
    grad_kv_low = jnp.concatenate([grad_key_low, grad_value_low], axis=1)
    grad_qkv = jnp.concatenate([grad_query_low, grad_kv_low], axis=1)
    grad_normed_one = transposed_product(grad_qkv, qkv_full).astype(LOW)
    unused_one, pull_one = jax.vjp(rms, hidden_in.astype(F32), pre_attention_gain)
    grad_gain_one = pull_one(grad_normed_one.astype(F32))[1]
    grad_gain_three = jax.vjp(rms, middle_kept, pre_feedforward_gain)[1](normed_kept)[1]
    grad_gain_two = jax.vjp(rms, branch_kept, post_attention_gain)[1](grad_kept)[1]
    gains = by_chip(jnp.stack([grad_gain_one, grad_gain_two, grad_gain_three, grad_gain_four]))
    gains_arrived = [shift(gains, k) for k in range(1, tp_size)]
    grad_normed_one = sent_scattered(ordered_blocks(grad_normed_one))
    qkv_sent = sent_to_core(normed_one, grad_qkv)
    qkv_arrived = over_cores(qkv_sent)
    grad_qkv_low = chip_rows(normed_one, grad_qkv, qkv_arrived)
    grad_attention = by_rows(jnp.concatenate([grad_qkv_low, grad_output_low], axis=1))
    attention_share = share_rows(grad_attention)

    unused_one, pull_one = jax.vjp(rms, inputs, pre_attention_gain)
    grad_inputs_low = by_chip((grad_middle + pull_one(grad_normed_one)[0]).astype(LOW))
    grad_inputs = in_order(sent_gathered(grad_inputs_low))

    gains_arrived, _ = lax.optimization_barrier((gains_arrived, grad_inputs_low))
    gains = sum(gains_arrived, gains)
    for axis in ROWS:
        gains = summed(gains, axis)
    share = hidden_in.shape[1] // (lax.axis_size("fsdp") * lax.axis_size("ctx"))
    row_rank = lax.axis_index("fsdp") * lax.axis_size("ctx") + lax.axis_index("ctx")
    gain_shares = lax.dynamic_slice_in_dim(gains, row_rank * share, share, axis=1)
    edges = [0, heads_width, heads_width + kv_width, qkv_width, qkv_width + heads_width]
    attention_shares = [
        attention_share[:, a:b].astype(F32) for a, b in zip(edges[:-1], edges[1:])
    ]
    gate_share = gate_up_share[:, :units].astype(F32)
    up_share = gate_up_share[:, units:].astype(F32)
    down_share = down_share.astype(F32)
    return (
        (outputs, grad_inputs)
        + tuple(gain_shares[i] for i in range(4))
        + tuple(attention_shares)
        + (gate_share, up_share, down_share)
    )


def solution(mesh):
    tokens = P(ROWS, None)
    weight = P(ROWS, "tp")
    return jax.shard_map(
        shards,
        mesh=mesh,
        in_specs=(tokens, tokens, P("fsdp")) + (P(),) * 4 + (weight,) * 7,
        out_specs=(tokens, tokens) + (P(ROWS),) * 4 + (weight,) * 7,
        check_vma=False,
    )
```
